256 devices in a mesh: query: 8 (over x_hi, y), corpus: 32 (over z, x_lo, core).
Axes of the slice: x: 4 (x_hi: 2, x_lo: 2; x = x_hi * 2 + x_lo), y: 4, z: 8, core: 2. Of those that a mesh axis runs over, the one named last changes fastest.
Arguments:
- queries: float32 [3072, 768], P('query'), may hold values from -20 to 20
- codes: int32 [32768, 96], P('corpus'), may hold values from 0 to 255
- positive: int32 [3072], P('query'), may hold values from 0 to 32767
- codebook: float32 [256, 768], replicated, may hold values from -0.6 to 0.6
Outputs:
- grad_queries: float32 [3072, 768], P('query')
- grad_codebook: float32 [256, 768], replicated
- loss: float32 [3072], P('query')
The draws below stay inside these ranges and needn't reach their ends.
All inputs are finite; a program needn't handle non-finite values.
Results may differ from the reference program's by a relative error of at most 0.0003.
Values sent between devices are 32-bit elements; how exact they have to be, the bound alone decides.
A program may use at most 64 MiB of HBM per device.

```python
import math
import jax
import jax.numpy as jnp
from jax import lax

D = 768
SUB = 96
CW = 256
DOC_DEV = 1024
NQ = 3072
ND = 32768
N_CORPUS = 32


def make_codes(key):
    base = jax.random.randint(jax.random.fold_in(key, 11), (ND, SUB), 0, CW, dtype=jnp.int32)
    offset = jax.random.randint(jax.random.fold_in(key, 12), (ND, SUB), 1, CW, dtype=jnp.int32)
    row_ids = jnp.arange(ND, dtype=jnp.int32)[:, None]
    sub_ids = jnp.arange(SUB, dtype=jnp.int32)[None, :]
    before = jnp.concatenate([base[:1], base[:-1]], axis=0)
    changed = sub_ids == row_ids // 64 % SUB
    twin_codes = jnp.where(changed, (before + offset) % CW, before)
    return jnp.where(row_ids % 64 == 1, twin_codes, base)


def make_positive(key):
    drawn = jax.random.randint(jax.random.fold_in(key, 31), (NQ,), 0, ND, dtype=jnp.int32)
    return drawn.at[NQ - 1].set(ND - 1)


def make_codebook(key):
    factor = 3.0 / math.sqrt(D)
    values = jnp.clip(jax.random.normal(jax.random.fold_in(key, 21), (CW, D), jnp.float32), -5.0, 5.0)
    return jnp.clip(values * factor, -0.6, 0.6)


def draw_codes(key, part):
    return make_codes(key)


def draw_positive(key, part):
    return make_positive(key)


def draw_codebook(key, part):
    return make_codebook(key)


def draw_queries(key, part):
    noise = jnp.clip(jax.random.normal(jax.random.fold_in(key, 41), (NQ, D), jnp.float32), -5.0, 5.0)
    return noise


def setup_inputs(seed: int = 0) -> dict:
    arg_keys = jax.random.split(jax.random.key(seed), 5)
    queries = draw_queries(jax.random.fold_in(arg_keys[4], 71), 0)
    codes = draw_codes(jax.random.fold_in(arg_keys[4], 71), 0)
    positive = draw_positive(jax.random.fold_in(arg_keys[4], 71), 0)
    codebook = draw_codebook(jax.random.fold_in(arg_keys[4], 71), 0)
    return dict(queries=queries, codes=codes, positive=positive, codebook=codebook)


precise = lax.Precision.HIGHEST


def rebuild(codebook, codes_block):
    columns = jnp.repeat(codes_block, D // SUB, axis=1)
    return jnp.take_along_axis(codebook, columns, axis=0), columns


def reference(queries, codes, positive, codebook):
    codes_blocks = codes.reshape(N_CORPUS, DOC_DEV, SUB)

    def stats_step(carry, codes_block):
        row_top, row_total = carry
        rebuilt, unused = rebuild(codebook, codes_block)
        scores = lax.dot_general(queries, rebuilt, (((1,), (1,)), ((), ())), precision=precise, preferred_element_type=jnp.float32)
        new_top = jnp.maximum(row_top, jnp.max(scores, axis=1))
        new_total = row_total * jnp.exp(row_top - new_top) + jnp.sum(jnp.exp(scores - new_top[:, None]), axis=1)
        return (new_top, new_total), None

    start_top = jnp.full((NQ,), -jnp.inf, dtype=jnp.float32)
    start_total = jnp.zeros((NQ,), dtype=jnp.float32)
    (row_top, row_total), unused = lax.scan(stats_step, (start_top, start_total), codes_blocks)
    pos_docs, unused = rebuild(codebook, codes[positive])
    pos_score = jnp.sum(queries * pos_docs, axis=1)
    log_total = row_top + jnp.log(row_total)
    loss = log_total - pos_score
    column_ids = jnp.arange(D, dtype=jnp.int32)[None, :]

    def grad_step(carry, inputs):
        query_grad, codebook_grad = carry
        block_index, codes_block = inputs
        rebuilt, columns = rebuild(codebook, codes_block)
        scores = lax.dot_general(queries, rebuilt, (((1,), (1,)), ((), ())), precision=precise, preferred_element_type=jnp.float32)
        doc_ids = block_index * DOC_DEV + jnp.arange(DOC_DEV, dtype=jnp.int32)
        positive_hits = (positive[:, None] == doc_ids[None, :]).astype(jnp.float32)
        weights = jnp.exp(scores - log_total[:, None]) - positive_hits
        query_grad = query_grad + jnp.dot(weights, rebuilt, precision=precise, preferred_element_type=jnp.float32)
        doc_grad = lax.dot_general(weights, queries, (((0,), (0,)), ((), ())), precision=precise, preferred_element_type=jnp.float32)
        codebook_grad = codebook_grad.at[columns, column_ids].add(doc_grad)
        return (query_grad, codebook_grad), None

    start = (jnp.zeros((NQ, D), dtype=jnp.float32), jnp.zeros((CW, D), dtype=jnp.float32))
    block_ids = jnp.arange(N_CORPUS, dtype=jnp.int32)
    (grad_queries, grad_codebook), unused = lax.scan(grad_step, start, (block_ids, codes_blocks))
    return (grad_queries, grad_codebook, loss)
```

```python
import jax
import jax.numpy as jnp
from jax import lax
from jax.experimental import pallas as pl
from jax.experimental.pallas import tpu as pltpu
from jax.sharding import PartitionSpec as P

F32, BF16, I32 = jnp.float32, jnp.bfloat16, jnp.int32
NN = (((1,), (0,)), ((), ()))
NT = (((1,), (1,)), ((), ()))
HIGH_CODES = 64
LOW_CODES = 4


def dot(a, b, dims=NN):
    return lax.dot_general(a, b, dims, preferred_element_type=F32)


def split(x):
    high = x.astype(BF16)
    return high, (x - high.astype(F32)).astype(BF16)


def split3(x):
    high = x.astype(BF16)
    rest = x - high.astype(F32)
    mid = rest.astype(BF16)
    return high, mid, (rest - mid.astype(F32)).astype(BF16)


def transpose_inputs(codes_ref, book_ref, codes_t, book_t):
    codes_t[...] = codes_ref[...].T
    book_t[...] = book_ref[...].T


def split_queries(q_ref, q3, q_t):
    width = q_ref.shape[1]
    high, mid, low = split3(q_ref[...])
    q3[:, :width] = high
    q3[:, width : 2 * width] = mid
    q3[:, 2 * width :] = low
    rows = q_ref.shape[0]
    high, mid = split(q_ref[...].T)
    q_t[:, :rows] = high
    q_t[:, rows:] = mid


def rebuild(codes_t, book_t, r3):
    subs, docs = codes_t.shape
    width = book_t.shape[0]
    sub_width = width // subs

    def pair(p, _):
        parts = []
        for side in range(2):
            m = 2 * p + side
            base = pl.multiple_of(m * sub_width, sub_width)
            low = book_t[pl.ds(base, sub_width), :128]
            high = book_t[pl.ds(base, sub_width), 128:]
            code = codes_t[pl.ds(m, 1), :]
            tiles = []
            for t in range(docs // 128):
                picked = jnp.broadcast_to(code[:, 128 * t : 128 * t + 128], (sub_width, 128))
                lane = picked & 127
                a = jnp.take_along_axis(low, lane, axis=1)
                b = jnp.take_along_axis(high, lane, axis=1)
                tiles.append(jnp.where(picked < 128, a, b))
            parts.append(jnp.concatenate(tiles, axis=1))
        both = jnp.concatenate(parts, axis=0)
        high, mid, low = split3(both)
        at = pl.multiple_of(2 * p * sub_width, 2 * sub_width)
        r3[pl.ds(at, 2 * sub_width), :] = low
        r3[pl.ds(width + at, 2 * sub_width), :] = mid
        r3[pl.ds(2 * width + at, 2 * sub_width), :] = high
        return 0

    lax.fori_loop(0, subs // 2, pair, 0)


def score(q3, r3, s_ref, tile=256):
    width = q3.shape[1] // 3

    def block(t, _):
        at = pl.ds(pl.multiple_of(t * tile, tile), tile)
        acc = dot(q3[...], r3[:, at])
        acc = acc + dot(q3[:, : 2 * width], r3[width:, at])
        acc = acc + dot(q3[:, :width], r3[2 * width :, at])
        s_ref[:, at] = acc
        return 0

    lax.fori_loop(0, s_ref.shape[1] // tile, block, 0)


def statistics(s_ref, pos_col, cols, step=32):
    rows, docs = s_ref.shape
    lane = lax.broadcasted_iota(I32, (step, 128), 1)
    ids = lax.broadcasted_iota(I32, (step, docs), 1)

    def block(b, _):
        at = pl.ds(pl.multiple_of(b * step, step), step)
        s = s_ref[at, :]
        top = jnp.max(s, axis=1, keepdims=True)
        own = jnp.sum(jnp.where(pos_col[at, :1] == ids, s, 0.0), axis=1, keepdims=True)
        e = jnp.exp(s - top)
        total = jnp.sum(e, axis=1, keepdims=True)
        s_ref[at, :] = e
        cols[at, :] = jnp.where(
            lane == 0, top, jnp.where(lane == 1, total, jnp.where(lane == 2, own, 0.0))
        )
        return 0

    lax.fori_loop(0, rows // step, block, 0)


def as_column(row, column):
    column[...] = jnp.broadcast_to(row, (128, row.shape[1])).T


def weigh(e_ref, scale_col, pos_col, w2, step=32):
    rows, docs = e_ref.shape
    ids = lax.broadcasted_iota(I32, (step, docs), 1)

    def block(b, _):
        at = pl.ds(pl.multiple_of(b * step, step), step)
        w = e_ref[at, :] * scale_col[at, :1]
        w = w - jnp.where(pos_col[at, :1] == ids, 1.0, 0.0)
        high, low = split(w)
        w2[at, :] = low
        w2[pl.ds(pl.multiple_of(rows + b * step, step), step), :] = high
        return 0

    lax.fori_loop(0, rows // step, block, 0)


def query_gradient(w2, r3, out, tile=256):
    rows = w2.shape[0] // 2
    width = r3.shape[0] // 3

    def block(t, _):
        base = pl.multiple_of(t * tile, tile)
        mid = r3[pl.ds(width + base, tile), :]
        high = r3[pl.ds(2 * width + base, tile), :]
        acc = dot(w2[rows:, :], mid, NT)
        acc = acc + dot(w2[:rows, :], high, NT)
        acc = acc + dot(w2[rows:, :], high, NT)
        out[:, pl.ds(base, tile)] = acc
        return 0

    lax.fori_loop(0, width // tile, block, 0)


def document_gradient(w2, q_t, out, tile=256):
    rows = w2.shape[0] // 2

    def block(t, _):
        at = pl.ds(pl.multiple_of(t * tile, tile), tile)
        acc = dot(q_t[...], w2[:, at])
        out[:, at] = acc + dot(q_t[:, :rows], w2[rows:, at])
        return 0

    lax.fori_loop(0, out.shape[1] // tile, block, 0)


def collect(codes_t, d_ref, out, group=4):
    subs, docs = codes_t.shape
    sub_width = d_ref.shape[0] // subs
    word = lax.broadcasted_iota(I32, (HIGH_CODES, docs), 0)
    lane = lax.broadcasted_iota(I32, (sub_width, 128), 1)

    def block(g, _):
        tables, values = [], []
        for s in range(group):
            m = group * g + s
            code = codes_t[pl.ds(m, 1), :]
            inner = code & (HIGH_CODES - 1)
            outer = jnp.broadcast_to(code >> 6, (sub_width, docs))
            tables.append(jnp.where(word == inner, 1.0, 0.0).astype(BF16))
            d = d_ref[pl.ds(pl.multiple_of(m * sub_width, sub_width), sub_width), :]
            high = d.astype(BF16).astype(F32)
            low = d - high
            masks = [outer == k for k in range(LOW_CODES)]
            rows = [jnp.where(mask, part, 0.0) for part in (high, low) for mask in masks]
            values.append(jnp.concatenate(rows, axis=0).astype(BF16))
        found = dot(jnp.concatenate(values, axis=0), jnp.concatenate(tables, axis=0), NT)
        rows = 2 * LOW_CODES * sub_width
        for s in range(group):
            at = 128 * (s // 2)
            piece = found[rows * s : rows * (s + 1), at : at + 128]
            piece = piece[: rows // 2] + piece[rows // 2 :]
            parts = [piece[sub_width * k : sub_width * (k + 1)] for k in range(LOW_CODES)]
            base = pl.multiple_of((group * g + s) * sub_width, sub_width)
            for k in range(2):
                first, second = parts[2 * k], parts[2 * k + 1]
                if s % 2:
                    first = pltpu.roll(first, 64, 1)
                else:
                    second = pltpu.roll(second, 64, 1)
                out[pl.ds(base, sub_width), 128 * k : 128 * k + 128] = jnp.where(
                    lane < 64, first, second
                )
        return 0

    lax.fori_loop(0, subs // group, block, 0)


def front(q_ref, codes_ref, pos_ref, book_ref, r3, q_t, codes_t, e_ref, stats, book_t, q3, pos_col, cols):
    transpose_inputs(codes_ref, book_ref, codes_t, book_t)
    split_queries(q_ref, q3, q_t)
    rebuild(codes_t, book_t, r3)
    score(q3, r3, e_ref)
    as_column(pos_ref[...], pos_col)
    statistics(e_ref, pos_col, cols)
    stats[...] = cols[...].T[:8]


def back(r3, q_t, codes_t, e_ref, pos_ref, scale_ref, grad_q, grad_b, pos_col, scale_col, w2, d_ref):
    as_column(pos_ref[...], pos_col)
    as_column(scale_ref[...], scale_col)
    weigh(e_ref, scale_col, pos_col, w2)
    query_gradient(w2, r3, grad_q)
    document_gradient(w2, q_t, d_ref)
    collect(codes_t, d_ref, grad_b)


def local(queries, codes, positive, codebook):
    rows, width = queries.shape
    docs, subs = codes.shape
    words = codebook.shape[0]
    here = (positive - lax.axis_index("corpus") * docs).reshape(1, rows)
    r3, q_t, codes_t, e, stats = pl.pallas_call(
        front,
        out_shape=(
            jax.ShapeDtypeStruct((3 * width, docs), BF16),
            jax.ShapeDtypeStruct((width, 2 * rows), BF16),
            jax.ShapeDtypeStruct((subs, docs), I32),
            jax.ShapeDtypeStruct((rows, docs), F32),
            jax.ShapeDtypeStruct((8, rows), F32),
        ),
        scratch_shapes=[
            pltpu.VMEM((width, words), F32),
            pltpu.VMEM((rows, 3 * width), BF16),
            pltpu.VMEM((rows, 128), I32),
            pltpu.VMEM((rows, 128), F32),
        ],
        name="front",
    )(queries, codes, here, codebook)
    every = lax.all_gather(stats, "corpus")
    row_top = jnp.max(every[:, 0], axis=0)
    row_total = jnp.sum(every[:, 1] * jnp.exp(every[:, 0] - row_top), axis=0)
    log_total = row_top + jnp.log(row_total)
    loss = log_total - jnp.sum(every[:, 2], axis=0)
    scale = jnp.exp(stats[0] - log_total).reshape(1, rows)
    grad_q, grad_b = pl.pallas_call(
        back,
        out_shape=(
            jax.ShapeDtypeStruct((rows, width), F32),
            jax.ShapeDtypeStruct((width, words), F32),
        ),
        scratch_shapes=[
            pltpu.VMEM((rows, 128), I32),
            pltpu.VMEM((rows, 128), F32),
            pltpu.VMEM((2 * rows, docs), BF16),
            pltpu.VMEM((width, docs), F32),
        ],
        name="back",
    )(r3, q_t, codes_t, e, here, scale)
    grad_q = lax.psum(grad_q, "corpus")
    grad_b = lax.psum(grad_b, ("query", "corpus"))
    return grad_q, grad_b.T, loss


def solution(mesh):
    return jax.shard_map(
        local,
        mesh=mesh,
        in_specs=(P("query", None), P("corpus", None), P("query"), P()),
        out_specs=(P("query", None), P(), P("query")),
        check_vma=False,
    )
```

```python
import jax
import jax.numpy as jnp
from jax import lax
from jax.experimental import pallas as pl
from jax.experimental.pallas import tpu as pltpu
from jax.sharding import PartitionSpec as P

F32, BF16, I32 = jnp.float32, jnp.bfloat16, jnp.int32
NN = (((1,), (0,)), ((), ()))
NT = (((1,), (1,)), ((), ()))
HIGH_CODES = 64
LOW_CODES = 4


def dot(a, b, dims=NN):
    return lax.dot_general(a, b, dims, preferred_element_type=F32)


def split(x):
    high = x.astype(BF16)
    return high, (x - high.astype(F32)).astype(BF16)


def split3(x):
    high = x.astype(BF16)
    rest = x - high.astype(F32)
    mid = rest.astype(BF16)
    return high, mid, (rest - mid.astype(F32)).astype(BF16)


def split_queries(q_ref, q3, q_t):
    width = q_ref.shape[1]
    high, mid, low = split3(q_ref[...])
    q3[:, :width] = high
    q3[:, width : 2 * width] = mid
    q3[:, 2 * width :] = low
    rows = q_ref.shape[0]
    high, mid = split(q_ref[...].T)
    q_t[:, :rows] = high
    q_t[:, rows:] = mid


def rebuild(codes_t, book_t, r3):
    subs, docs = codes_t.shape
    width = book_t.shape[0]
    sub_width = width // subs

    def pair(p, _):
        parts = []
        for side in range(2):
            m = 2 * p + side
            base = pl.multiple_of(m * sub_width, sub_width)
            low = book_t[pl.ds(base, sub_width), :128]
            high = book_t[pl.ds(base, sub_width), 128:]
            code = codes_t[pl.ds(m, 1), :]
            tiles = []
            for t in range(docs // 128):
                picked = jnp.broadcast_to(code[:, 128 * t : 128 * t + 128], (sub_width, 128))
                lane = picked & 127
                a = jnp.take_along_axis(low, lane, axis=1)
                b = jnp.take_along_axis(high, lane, axis=1)
                tiles.append(jnp.where(picked < 128, a, b))
            parts.append(jnp.concatenate(tiles, axis=1))
        both = jnp.concatenate(parts, axis=0)
        high, mid, low = split3(both)
        at = pl.multiple_of(2 * p * sub_width, 2 * sub_width)
        r3[pl.ds(at, 2 * sub_width), :] = low
        r3[pl.ds(width + at, 2 * sub_width), :] = mid
        r3[pl.ds(2 * width + at, 2 * sub_width), :] = high
        return 0

    lax.fori_loop(0, subs // 2, pair, 0)


def score(q3, r3, s_ref, tile=256):
    width = q3.shape[1] // 3

    def block(t, _):
        at = pl.ds(pl.multiple_of(t * tile, tile), tile)
        acc = dot(q3[...], r3[:, at])
        acc = acc + dot(q3[:, : 2 * width], r3[width:, at])
        acc = acc + dot(q3[:, :width], r3[2 * width :, at])
        s_ref[:, at] = acc
        return 0

    lax.fori_loop(0, s_ref.shape[1] // tile, block, 0)


def statistics(s_ref, pos_col, cols, step=32):
    rows, docs = s_ref.shape
    lane = lax.broadcasted_iota(I32, (step, 128), 1)
    ids = lax.broadcasted_iota(I32, (step, docs), 1)

    def block(b, _):
        at = pl.ds(pl.multiple_of(b * step, step), step)
        s = s_ref[at, :]
        top = jnp.max(s, axis=1, keepdims=True)
        own = jnp.sum(jnp.where(pos_col[at, :1] == ids, s, 0.0), axis=1, keepdims=True)
        e = jnp.exp(s - top)
        total = jnp.sum(e, axis=1, keepdims=True)
        s_ref[at, :] = e
        cols[at, :] = jnp.where(
            lane == 0, top, jnp.where(lane == 1, total, jnp.where(lane == 2, own, 0.0))
        )
        return 0

    lax.fori_loop(0, rows // step, block, 0)


def as_column(row, column):
    column[...] = jnp.broadcast_to(row, (128, row.shape[1])).T


def weigh(e_ref, scale_col, pos_col, w2, step=32):
    rows, docs = e_ref.shape
    ids = lax.broadcasted_iota(I32, (step, docs), 1)

    def block(b, _):
        at = pl.ds(pl.multiple_of(b * step, step), step)
        w = e_ref[at, :] * scale_col[at, :1]
        w = w - jnp.where(pos_col[at, :1] == ids, 1.0, 0.0)
        high, low = split(w)
        w2[at, :] = low
        w2[pl.ds(pl.multiple_of(rows + b * step, step), step), :] = high
        return 0

    lax.fori_loop(0, rows // step, block, 0)


def query_gradient(w2, r3, out, tile=256):
    rows = w2.shape[0] // 2
    width = r3.shape[0] // 3

    def block(t, _):
        base = pl.multiple_of(t * tile, tile)
        mid = r3[pl.ds(width + base, tile), :]
        high = r3[pl.ds(2 * width + base, tile), :]
        acc = dot(w2[rows:, :], mid, NT)
        acc = acc + dot(w2[:rows, :], high, NT)
        acc = acc + dot(w2[rows:, :], high, NT)
        out[:, pl.ds(base, tile)] = acc
        return 0

    lax.fori_loop(0, width // tile, block, 0)


def document_gradient(w2, q_t, out, tile=256):
    rows = w2.shape[0] // 2

    def block(t, _):
        at = pl.ds(pl.multiple_of(t * tile, tile), tile)
        acc = dot(q_t[...], w2[:, at])
        out[:, at] = acc + dot(q_t[:, :rows], w2[rows:, at])
        return 0

    lax.fori_loop(0, out.shape[1] // tile, block, 0)


def collect(codes_t, d_ref, out, blocks, base, group=4):
    subs, docs = codes_t.shape
    sub_width = d_ref.shape[0] // subs
    word = lax.broadcasted_iota(I32, (HIGH_CODES, docs), 0)
    lane = lax.broadcasted_iota(I32, (sub_width, 128), 1)

    def block(b, _):
        g = lax.rem(b + base, subs // group)
        tables, values = [], []
        for s in range(group):
            m = group * g + s
            code = codes_t[pl.ds(m, 1), :]
            inner = code & (HIGH_CODES - 1)
            outer = jnp.broadcast_to(code >> 6, (sub_width, docs))
            tables.append(jnp.where(word == inner, 1.0, 0.0).astype(BF16))
            d = d_ref[pl.ds(pl.multiple_of(m * sub_width, sub_width), sub_width), :]
            high = d.astype(BF16).astype(F32)
            low = d - high
            masks = [outer == k for k in range(LOW_CODES)]
            rows = [jnp.where(mask, part, 0.0) for part in (high, low) for mask in masks]
            values.append(jnp.concatenate(rows, axis=0).astype(BF16))
        found = dot(jnp.concatenate(values, axis=0), jnp.concatenate(tables, axis=0), NT)
        rows = 2 * LOW_CODES * sub_width
        for s in range(group):
            at = 128 * (s // 2)
            piece = found[rows * s : rows * (s + 1), at : at + 128]
            piece = piece[: rows // 2] + piece[rows // 2 :]
            parts = [piece[sub_width * k : sub_width * (k + 1)] for k in range(LOW_CODES)]
            start = pl.multiple_of((group * g + s) * sub_width, sub_width)
            for k in range(2):
                first, second = parts[2 * k], parts[2 * k + 1]
                if s % 2:
                    first = pltpu.roll(first, 64, 1)
                else:
                    second = pltpu.roll(second, 64, 1)
                out[pl.ds(start, sub_width), 128 * k : 128 * k + 128] = jnp.where(
                    lane < 64, first, second
                )
        return 0

    lax.fori_loop(blocks[0], blocks[1], block, 0)


def front(q_ref, codes_t, pos_ref, book_ref, r3, q_t, e_ref, stats, book_t, q3, pos_col, cols):
    book_t[...] = book_ref[...].T
    split_queries(q_ref, q3, q_t)
    rebuild(codes_t, book_t, r3)
    score(q3, r3, e_ref)
    as_column(pos_ref[...], pos_col)
    statistics(e_ref, pos_col, cols)
    stats[...] = cols[...].T[:8]


class Place:
    def __init__(self):
        query, corpus = lax.axis_index("query"), lax.axis_index("corpus")
        self.y = lax.rem(query, 4)
        self.x = 2 * lax.div(query, 4) + lax.rem(lax.div(corpus, 2), 2)
        self.z = lax.div(corpus, 4)
        self.core = lax.rem(corpus, 2)

    def at(self, x=None, y=None, z=None, core=None):
        x = self.x if x is None else x
        y = self.y if y is None else y
        z = self.z if z is None else z
        core = self.core if core is None else core
        return (4 * lax.div(x, 2) + y, 4 * z + 2 * lax.rem(x, 2) + core)

    def next_y(self, d):
        return lax.rem(self.y + d, 4)

    def next_x(self, d):
        return lax.rem(self.x + d, 4)

    def next_z(self, d):
        return lax.rem(self.z + d, 8)


class Wire:
    def __init__(self, sent, arrived):
        self.sent, self.arrived, self.copies = sent, arrived, []

    def send(self, src, dst, device):
        i = len(self.copies)
        copy = pltpu.make_async_remote_copy(
            src_ref=src,
            dst_ref=dst,
            send_sem=self.sent.at[i],
            recv_sem=self.arrived.at[i],
            device_id=device,
            device_id_type=pl.DeviceIdType.MESH,
        )
        copy.start()
        self.copies.append(copy)
        return copy

    def finish(self):
        for copy in self.copies:
            copy.wait_send()


def rows_at(index, size):
    return pl.ds(pl.multiple_of(index * size, size), size)


def merge(stats):
    top = stats[0][0:1]
    for s in stats[1:]:
        top = jnp.maximum(top, s[0:1])
    total = sum(s[1:2] * jnp.exp(s[0:1] - top) for s in stats)
    own = sum(s[2:3] for s in stats)
    pad = jnp.zeros((8 - 3, top.shape[1]), F32)
    return jnp.concatenate([top, total, own, pad], axis=0)


def back(
    r3, q_t, codes_t, e_ref, pos_ref, stats_ref,
    grad_q, grad_b, loss_ref,
    pos_col, scale_col, w2, d_ref,
    near, far, part_q, half_q, sum_q, up, down, cross,
    part_b, half_b, sum_b, first_in, first_sum, second_in, second_sum, last_in,
    sent, arrived,
):
    me = Place()
    wire = Wire(sent, arrived)
    x_pair = me.x + 1 - 2 * lax.rem(me.x, 2)
    other = 1 - me.core
    partners = [me.at(core=other), me.at(x=x_pair), me.at(x=x_pair, core=other)]
    far_partners = [me.at(z=me.next_z(d)) for d in range(1, 8)]
    y_partners = [me.at(y=me.next_y(d)) for d in range(1, 4)]
    x_partners = [me.at(x=me.next_x(d)) for d in range(1, 4)]
    greeted = [partners[0], partners[2]] + far_partners + y_partners + x_partners
    barrier = pltpu.get_barrier_semaphore()
    for device in greeted:
        pl.semaphore_signal(barrier, inc=1, device_id=device, device_id_type=pl.DeviceIdType.MESH)
    as_column(pos_ref[...], pos_col)
    pl.semaphore_wait(barrier, len(greeted))

    mine = 2 * lax.rem(me.x, 2) + me.core
    near[mine] = stats_ref[...]
    copies = [wire.send(stats_ref, near.at[mine], device) for device in partners]
    for copy in copies:
        copy.wait_recv()
    far[me.z] = merge([near[k] for k in range(4)])
    copies = [wire.send(far.at[me.z], far.at[me.z], device) for device in far_partners]
    for copy in copies:
        copy.wait_recv()
    whole = merge([far[k] for k in range(8)])
    log_total = whole[0:1] + jnp.log(whole[1:2])
    loss_ref[...] = log_total - whole[2:3]
    as_column(jnp.exp(stats_ref[0:1] - log_total), scale_col)

    weigh(e_ref, scale_col, pos_col, w2)
    query_gradient(w2, r3, part_q)
    half = part_q.shape[0] // 2
    chunk = half // 8
    q_core = wire.send(part_q.at[rows_at(other, half)], half_q, partners[0])
    document_gradient(w2, q_t, d_ref)
    q_core.wait_recv()
    sum_q[...] = part_q[rows_at(me.core, half)] + half_q[...]

    z_up, z_down = far_partners[0], far_partners[6]

    def ring_send(step):
        copies = []
        for buffers, ahead, steps, device in ((up, 4 - step, 4, z_up), (down, 8 - 3 + step, 3, z_down)):
            if step >= steps:
                continue
            at = rows_at(me.next_z(ahead), chunk)
            if step == 0:
                src = sum_q.at[at]
            else:
                src = buffers.at[step - 1]
                src[...] = src[...] + sum_q[at]
            copies.append(wire.send(src, buffers.at[step], device))
        return copies

    def arrive(copies):
        for copy in copies:
            copy.wait_recv()

    subs = codes_t.shape[0]
    groups = subs // 4
    base = other * (groups // 2)
    b_half = part_b.shape[0] // 2

    copies = ring_send(0)
    collect(codes_t, d_ref, part_b, (0, groups // 4), base)
    arrive(copies)
    copies = ring_send(1)
    collect(codes_t, d_ref, part_b, (groups // 4, groups // 2), base)
    b_core = wire.send(part_b.at[rows_at(other, b_half)], half_b, partners[0])
    arrive(copies)
    copies = ring_send(2)
    collect(codes_t, d_ref, part_b, (groups // 2, 3 * groups // 4), base)
    arrive(copies)
    copies = ring_send(3)
    collect(codes_t, d_ref, part_b, (3 * groups // 4, groups), base)
    b_core.wait_recv()
    sum_b[...] = part_b[rows_at(me.core, b_half)] + half_b[...]

    lines = b_half // 4
    order = (
        ((me.y, me.next_y, y_partners), (me.x, me.next_x, x_partners)),
        ((me.x, me.next_x, x_partners), (me.y, me.next_y, y_partners)),
    )
    firsts = []
    for k in range(2):
        columns = pl.ds(128 * k, 128)
        _, following, devices = order[k][0]
        for d in range(1, 4):
            firsts.append(
                wire.send(
                    sum_b.at[rows_at(following(d), lines), columns],
                    first_in.at[k, d - 1],
                    devices[d - 1],
                )
            )

    arrive(copies)
    own = sum_q[rows_at(me.z, chunk)] + (up[3] + down[2])
    cross[0] = own
    across = wire.send(cross.at[0], cross.at[1], partners[1])

    seconds = []
    arrive(firsts)
    for k in range(2):
        index, _, _ = order[k][0]
        columns = pl.ds(128 * k, 128)
        acc = sum_b[rows_at(index, lines), columns]
        for d in range(3):
            acc = acc + first_in[k, d]
        first_sum[k] = acc
        _, following, devices = order[k][1]
        for d in range(1, 4):
            seconds.append(
                wire.send(
                    first_sum.at[k, rows_at(following(d), lines // 4)],
                    second_in.at[k, d - 1],
                    devices[d - 1],
                )
            )

    def q_rows(z):
        return pl.ds(pl.multiple_of(me.core * half + z * chunk, chunk), chunk)

    arrive([across])
    grad_q[q_rows(me.z)] = cross[0] + cross[1]
    passed = [wire.send(grad_q.at[q_rows(me.z)], grad_q.at[q_rows(me.z)], partners[0])]

    def pass_on(step):
        copies = []
        for back_by, steps, device in ((8 - step, 4, z_up), (step, 3, z_down)):
            if step < steps:
                at = q_rows(me.next_z(back_by))
                copies.append(wire.send(grad_q.at[at], grad_q.at[at], device))
        return copies

    def to_core(step):
        for ahead, steps in ((8 - step - 1, 4), (step + 1, 3)):
            if step < steps:
                at = q_rows(me.next_z(ahead))
                passed.append(wire.send(grad_q.at[at], grad_q.at[at], partners[0]))

    copies = pass_on(0)

    arrive(seconds)
    for k in range(2):
        index, _, _ = order[k][1]
        acc = first_sum[k, rows_at(index, lines // 4)]
        for d in range(3):
            acc = acc + second_in[k, d]
        last_in[me.z, k] = acc
    lasts = [wire.send(last_in.at[me.z], last_in.at[me.z], device) for device in far_partners]

    for step in range(3):
        arrive(copies)
        copies = pass_on(step + 1)
        to_core(step)
        if step == 1:
            arrive(lasts)
            acc = last_in[0]
            for z in range(1, 8):
                acc = acc + last_in[z]
            seconds = []
            for k in range(2):
                columns = pl.ds(128 * k, 128)
                at = me.core * b_half + order[k][0][0] * lines + order[k][1][0] * (lines // 4)
                at = pl.ds(pl.multiple_of(at, lines // 4), lines // 4)
                grad_b[at, columns] = acc[k]
                for device in order[k][1][2]:
                    seconds.append(wire.send(grad_b.at[at, columns], grad_b.at[at, columns], device))
        if step == 2:
            arrive(seconds)
            firsts = []
            for k in range(2):
                columns = pl.ds(128 * k, 128)
                at = me.core * b_half + order[k][0][0] * lines
                at = pl.ds(pl.multiple_of(at, lines), lines)
                for device in order[k][0][2]:
                    firsts.append(wire.send(grad_b.at[at, columns], grad_b.at[at, columns], device))
    arrive(copies)
    to_core(3)
    arrive(firsts)
    at = rows_at(me.core, b_half)
    passed.append(wire.send(grad_b.at[at], grad_b.at[at], partners[0]))
    arrive(passed)
    wire.finish()


def local(queries, codes, positive, codebook):
    rows, width = queries.shape
    docs, subs = codes.shape
    words = codebook.shape[0]
    here = (positive - lax.axis_index("corpus") * docs).reshape(1, rows)
    codes_t = codes.T
    r3, q_t, e, stats = pl.pallas_call(
        front,
        out_shape=(
            jax.ShapeDtypeStruct((3 * width, docs), BF16),
            jax.ShapeDtypeStruct((width, 2 * rows), BF16),
            jax.ShapeDtypeStruct((rows, docs), F32),
            jax.ShapeDtypeStruct((8, rows), F32),
        ),
        scratch_shapes=[
            pltpu.VMEM((width, words), F32),
            pltpu.VMEM((rows, 3 * width), BF16),
            pltpu.VMEM((rows, 128), I32),
            pltpu.VMEM((rows, 128), F32),
        ],
        name="front",
    )(queries, codes_t, here, codebook)
    chunk = rows // 16
    lines = width // 8
    vmem = pl.BlockSpec(memory_space=pltpu.VMEM)
    grad_q, grad_b, loss = pl.pallas_call(
        back,
        in_specs=[vmem] * 6,
        out_specs=(vmem, vmem, vmem),
        out_shape=(
            jax.ShapeDtypeStruct((rows, width), F32),
            jax.ShapeDtypeStruct((width, words), F32),
            jax.ShapeDtypeStruct((1, rows), F32),
        ),
        scratch_shapes=[
            pltpu.VMEM((rows, 128), I32),
            pltpu.VMEM((rows, 128), F32),
            pltpu.VMEM((2 * rows, docs), BF16),
            pltpu.VMEM((width, docs), F32),
            pltpu.VMEM((4, 8, rows), F32),
            pltpu.VMEM((8, 8, rows), F32),
            pltpu.VMEM((rows, width), F32),
            pltpu.VMEM((rows // 2, width), F32),
            pltpu.VMEM((rows // 2, width), F32),
            pltpu.VMEM((4, chunk, width), F32),
            pltpu.VMEM((3, chunk, width), F32),
            pltpu.VMEM((2, chunk, width), F32),
            pltpu.VMEM((width, words), F32),
            pltpu.VMEM((width // 2, words), F32),
            pltpu.VMEM((width // 2, words), F32),
            pltpu.VMEM((2, 3, lines, words // 2), F32),
            pltpu.VMEM((2, lines, words // 2), F32),
            pltpu.VMEM((2, 3, lines // 4, words // 2), F32),
            pltpu.VMEM((2, lines // 4, words // 2), F32),
            pltpu.VMEM((8, 2, lines // 4, words // 2), F32),
            pltpu.SemaphoreType.DMA((80,)),
            pltpu.SemaphoreType.DMA((80,)),
        ],
        compiler_params=pltpu.CompilerParams(collective_id=0, has_side_effects=True),
        name="back",
    )(r3, q_t, codes_t, e, here, stats)
    return grad_q, grad_b.T, loss.reshape(rows)


def solution(mesh):
    return jax.shard_map(
        local,
        mesh=mesh,
        in_specs=(P("query", None), P("corpus", None), P("query"), P()),
        out_specs=(P("query", None), P(), P("query")),
        check_vma=False,
    )
```

```python
import jax
import jax.numpy as jnp
from jax import lax
from jax.experimental import pallas as pl
from jax.experimental.pallas import tpu as pltpu
from jax.sharding import PartitionSpec as P

F32, BF16, I32 = jnp.float32, jnp.bfloat16, jnp.int32
NN = (((1,), (0,)), ((), ()))
NT = (((1,), (1,)), ((), ()))
HIGH_CODES = 64
LOW_CODES = 4


def dot(a, b, dims=NN):
    return lax.dot_general(a, b, dims, preferred_element_type=F32)


def split(x):
    high = x.astype(BF16)
    return high, (x - high.astype(F32)).astype(BF16)


def split3(x):
    high = x.astype(BF16)
    rest = x - high.astype(F32)
    mid = rest.astype(BF16)
    return high, mid, (rest - mid.astype(F32)).astype(BF16)


def split_queries(q_ref, q3, step=32):
    width = q_ref.shape[1]

    def block(b, _):
        at = pl.ds(pl.multiple_of(b * step, step), step)
        high, mid, low = split3(q_ref[at, :])
        q3[at, :width] = high
        q3[at, width : 2 * width] = mid
        q3[at, 2 * width :] = low
        return 0

    lax.fori_loop(0, q_ref.shape[0] // step, block, 0)


def transpose_queries(q_ref, q_t, step=128):
    rows = q_ref.shape[0]

    def block(b, _):
        at = pl.ds(pl.multiple_of(b * step, step), step)
        high, mid = split(q_ref[:, at].T)
        q_t[at, :rows] = high
        q_t[at, rows : 2 * rows] = mid
        q_t[at, 2 * rows :] = high
        return 0

    lax.fori_loop(0, q_ref.shape[1] // step, block, 0)


def transpose_book(book_ref, book_t, step=128):
    def block(b, _):
        at = pl.ds(pl.multiple_of(b * step, step), step)
        book_t[at, :] = book_ref[:, at].T
        return 0

    lax.fori_loop(0, book_ref.shape[1] // step, block, 0)


def rebuild(codes_t, book_t, r3, unroll=4):
    subs, docs = codes_t.shape
    width = book_t.shape[0]
    sub_width = width // subs

    def pair(p):
        parts = []
        for side in range(2):
            m = 2 * p + side
            base = pl.multiple_of(m * sub_width, sub_width)
            low = book_t[pl.ds(base, sub_width), :128]
            high = book_t[pl.ds(base, sub_width), 128:]
            code = codes_t[pl.ds(m, 1), :]
            tiles = []
            for t in range(docs // 128):
                picked = jnp.broadcast_to(code[:, 128 * t : 128 * t + 128], (sub_width, 128))
                lane = picked & 127
                a = jnp.take_along_axis(low, lane, axis=1, mode="promise_in_bounds")
                b = jnp.take_along_axis(high, lane, axis=1, mode="promise_in_bounds")
                tiles.append(jnp.where(picked < 128, a, b))
            parts.append(jnp.concatenate(tiles, axis=1))
        high, mid, low = split3(jnp.concatenate(parts, axis=0))
        at = pl.multiple_of(2 * p * sub_width, 2 * sub_width)
        r3[pl.ds(at, 2 * sub_width), :] = low
        r3[pl.ds(width + at, 2 * sub_width), :] = mid
        r3[pl.ds(2 * width + at, 2 * sub_width), :] = high

    def block(b, _):
        for u in range(unroll):
            pair(unroll * b + u)
        return 0

    lax.fori_loop(0, subs // 2 // unroll, block, 0)


def score(q3, r3, s_ref, tile=256):
    width = q3.shape[1] // 3

    def block(t, _):
        at = pl.ds(pl.multiple_of(t * tile, tile), tile)
        acc = dot(q3[...], r3[:, at])
        acc = acc + dot(q3[:, : 2 * width], r3[width:, at])
        acc = acc + dot(q3[:, :width], r3[2 * width :, at])
        s_ref[:, at] = acc
        return 0

    lax.fori_loop(0, s_ref.shape[1] // tile, block, 0)


def statistics(s_ref, pos_col, cols, step=64):
    rows, docs = s_ref.shape
    lane = lax.broadcasted_iota(I32, (step, 128), 1)
    ids = lax.broadcasted_iota(I32, (step, docs), 1)

    def block(b, _):
        at = pl.ds(pl.multiple_of(b * step, step), step)
        s = s_ref[at, :]
        top = jnp.max(s, axis=1, keepdims=True)
        own = jnp.sum(jnp.where(pos_col[at, :1] == ids, s, 0.0), axis=1, keepdims=True)
        e = jnp.exp(s - top)
        total = jnp.sum(e, axis=1, keepdims=True)
        s_ref[at, :] = e
        cols[at, :] = jnp.where(
            lane == 0, top, jnp.where(lane == 1, total, jnp.where(lane == 2, own, 0.0))
        )
        return 0

    lax.fori_loop(0, rows // step, block, 0)


def as_column(row, column):
    column[...] = jnp.broadcast_to(row, (128, row.shape[1])).T


def expose(e_ref, pos_col, e2, hits, step=32):
    rows, docs = e_ref.shape
    ids = lax.broadcasted_iota(I32, (step, docs), 1)

    def block(b, _):
        at = pl.ds(pl.multiple_of(b * step, step), step)
        high, low = split(e_ref[at, :])
        e2[at, :] = low
        e2[pl.ds(pl.multiple_of(rows + b * step, step), step), :] = high
        hits[at, :] = jnp.where(pos_col[at, :1] == ids, 1.0, 0.0).astype(BF16)
        return 0

    lax.fori_loop(0, rows // step, block, 0)


def query_products(e2, hits, r3, spread, pulled, tile=256):
    rows = hits.shape[0]
    width = r3.shape[0] // 3

    def block(t, _):
        base = pl.multiple_of(t * tile, tile)
        mid = r3[pl.ds(width + base, tile), :]
        high = r3[pl.ds(2 * width + base, tile), :]
        acc = dot(e2[rows:, :], mid, NT)
        acc = acc + dot(e2[:rows, :], high, NT)
        spread[:, pl.ds(base, tile)] = acc + dot(e2[rows:, :], high, NT)
        pull = dot(hits[...], r3[pl.ds(base, tile), :], NT)
        pull = pull + dot(hits[...], mid, NT)
        pulled[:, pl.ds(base, tile)] = pull + dot(hits[...], high, NT)
        return 0

    lax.fori_loop(0, width // tile, block, 0)


def query_gradient(spread, pulled, scale_col, out, step=32):
    def block(b, _):
        at = pl.ds(pl.multiple_of(b * step, step), step)
        out[at, :] = spread[at, :] * scale_col[at, :1] - pulled[at, :]
        return 0

    lax.fori_loop(0, spread.shape[0] // step, block, 0)


def weigh(e_ref, scale_col, pos_col, w3, step=32):
    rows, docs = e_ref.shape
    ids = lax.broadcasted_iota(I32, (step, docs), 1)

    def block(b, _):
        at = pl.ds(pl.multiple_of(b * step, step), step)
        w = e_ref[at, :] * scale_col[at, :1]
        w = w - jnp.where(pos_col[at, :1] == ids, 1.0, 0.0)
        high, low = split(w)
        w3[at, :] = low
        w3[pl.ds(pl.multiple_of(rows + b * step, step), step), :] = high
        w3[pl.ds(pl.multiple_of(2 * rows + b * step, step), step), :] = high
        return 0

    lax.fori_loop(0, rows // step, block, 0)


def document_gradient(w3, q_t, out, tile=256):
    def block(t, _):
        at = pl.ds(pl.multiple_of(t * tile, tile), tile)
        out[:, at] = dot(q_t[...], w3[:, at])
        return 0

    lax.fori_loop(0, out.shape[1] // tile, block, 0)


def collect(codes_t, d_ref, out, blocks, base, group=4, unroll=2):
    subs, docs = codes_t.shape
    sub_width = d_ref.shape[0] // subs
    word = lax.broadcasted_iota(I32, (HIGH_CODES, docs), 0)
    lane = lax.broadcasted_iota(I32, (sub_width, 128), 1)

    def one(b):
        g = lax.rem(b + base, subs // group)
        tables, values = [], []
        for s in range(group):
            m = group * g + s
            code = codes_t[pl.ds(m, 1), :]
            inner = code & (HIGH_CODES - 1)
            outer = jnp.broadcast_to(code >> 6, (sub_width, docs))
            tables.append(jnp.where(word == inner, 1.0, 0.0).astype(BF16))
            d = d_ref[pl.ds(pl.multiple_of(m * sub_width, sub_width), sub_width), :]
            high = d.astype(BF16).astype(F32)
            low = d - high
            masks = [outer == k for k in range(LOW_CODES)]
            rows = [jnp.where(mask, part, 0.0) for part in (high, low) for mask in masks]
            values.append(jnp.concatenate(rows, axis=0).astype(BF16))
        found = dot(jnp.concatenate(values, axis=0), jnp.concatenate(tables, axis=0), NT)
        rows = 2 * LOW_CODES * sub_width
        for s in range(group):
            at = 128 * (s // 2)
            piece = found[rows * s : rows * (s + 1), at : at + 128]
            piece = piece[: rows // 2] + piece[rows // 2 :]
            parts = [piece[sub_width * k : sub_width * (k + 1)] for k in range(LOW_CODES)]
            start = pl.multiple_of((group * g + s) * sub_width, sub_width)
            for k in range(2):
                first, second = parts[2 * k], parts[2 * k + 1]
                if s % 2:
                    first = pltpu.roll(first, 64, 1)
                else:
                    second = pltpu.roll(second, 64, 1)
                out[pl.ds(start, sub_width), 128 * k : 128 * k + 128] = jnp.where(
                    lane < 64, first, second
                )

    def block(b, _):
        for u in range(unroll):
            one(unroll * b + u)
        return 0

    lax.fori_loop(blocks[0] // unroll, blocks[1] // unroll, block, 0)


def transpose_half(part, core, out, step=128):
    half = part.shape[0] // 2

    def block(b, _):
        at = pl.ds(pl.multiple_of(core * half + b * step, step), step)
        out[:, at] = part[at, :].T
        return 0

    lax.fori_loop(0, half // step, block, 0)


class Place:
    def __init__(self):
        query, corpus = lax.axis_index("query"), lax.axis_index("corpus")
        self.y = lax.rem(query, 4)
        self.x = 2 * lax.div(query, 4) + lax.rem(lax.div(corpus, 2), 2)
        self.z = lax.div(corpus, 4)
        self.core = lax.rem(corpus, 2)

    def at(self, x=None, y=None, z=None, core=None):
        x = self.x if x is None else x
        y = self.y if y is None else y
        z = self.z if z is None else z
        core = self.core if core is None else core
        return (4 * lax.div(x, 2) + y, 4 * z + 2 * lax.rem(x, 2) + core)

    def next_y(self, d):
        return lax.rem(self.y + d, 4)

    def next_x(self, d):
        return lax.rem(self.x + d, 4)

    def next_z(self, d):
        return lax.rem(self.z + d, 8)


class Wire:
    def __init__(self, sent, arrived):
        self.sent, self.arrived, self.copies = sent, arrived, []

    def send(self, src, dst, device):
        i = len(self.copies)
        copy = pltpu.make_async_remote_copy(
            src_ref=src,
            dst_ref=dst,
            send_sem=self.sent.at[i],
            recv_sem=self.arrived.at[i],
            device_id=device,
            device_id_type=pl.DeviceIdType.MESH,
        )
        copy.start()
        self.copies.append(copy)
        return copy

    def finish(self):
        for copy in self.copies:
            copy.wait_send()


def rows_at(index, size):
    return pl.ds(pl.multiple_of(index * size, size), size)


def merge(stats):
    top = stats[0][0:1]
    for s in stats[1:]:
        top = jnp.maximum(top, s[0:1])
    total = sum(s[1:2] * jnp.exp(s[0:1] - top) for s in stats)
    own = sum(s[2:3] for s in stats)
    pad = jnp.zeros((8 - 3, top.shape[1]), F32)
    return jnp.concatenate([top, total, own, pad], axis=0)


def step(
    q_ref, codes_t, pos_ref, book_ref,
    grad_q, grad_b, loss_ref,
    book_t, q3, r3, q_t, e_ref, stats_ref, cols,
    pos_col, scale_col, e2, hits, spread, pulled, w3, d_ref,
    near, far, part_q, half_q, sum_q, up, down, cross,
    words_b, part_b, half_b, sum_b, first_in, first_sum, second_in, second_sum, last_in,
    sent, arrived,
):
    me = Place()
    wire = Wire(sent, arrived)
    x_pair = me.x + 1 - 2 * lax.rem(me.x, 2)
    other = 1 - me.core
    partners = [me.at(core=other), me.at(x=x_pair), me.at(x=x_pair, core=other)]
    far_partners = [me.at(z=me.next_z(d)) for d in range(1, 8)]
    y_partners = [me.at(y=me.next_y(d)) for d in range(1, 4)]
    x_partners = [me.at(x=me.next_x(d)) for d in range(1, 4)]
    greeted = [partners[0], partners[2]] + far_partners + y_partners + x_partners
    barrier = pltpu.get_barrier_semaphore()
    for device in greeted:
        pl.semaphore_signal(barrier, inc=1, device_id=device, device_id_type=pl.DeviceIdType.MESH)

    transpose_book(book_ref, book_t)
    split_queries(q_ref, q3)
    rebuild(codes_t, book_t, r3)
    score(q3, r3, e_ref)
    docs = codes_t.shape[1]
    here = pos_ref[...] - lax.axis_index("corpus") * docs
    as_column(here, pos_col)
    statistics(e_ref, pos_col, cols)
    stats_ref[...] = cols[...].T[:8]
    pl.semaphore_wait(barrier, len(greeted))

    mine = 2 * lax.rem(me.x, 2) + me.core
    near[mine] = stats_ref[...]
    copies = [wire.send(stats_ref, near.at[mine], device) for device in partners]
    expose(e_ref, pos_col, e2, hits)
    for copy in copies:
        copy.wait_recv()
    far[me.z] = merge([near[k] for k in range(4)])
    copies = [wire.send(far.at[me.z], far.at[me.z], device) for device in far_partners]
    query_products(e2, hits, r3, spread, pulled)
    transpose_queries(q_ref, q_t)
    for copy in copies:
        copy.wait_recv()
    whole = merge([far[k] for k in range(8)])
    log_total = whole[0:1] + jnp.log(whole[1:2])
    loss_ref[...] = log_total - whole[2:3]
    as_column(jnp.exp(stats_ref[0:1] - log_total), scale_col)

    query_gradient(spread, pulled, scale_col, part_q)
    half = part_q.shape[0] // 2
    chunk = half // 8
    q_core = wire.send(part_q.at[rows_at(other, half)], half_q, partners[0])
    weigh(e_ref, scale_col, pos_col, w3)
    document_gradient(w3, q_t, d_ref)
    q_core.wait_recv()
    sum_q[...] = part_q[rows_at(me.core, half)] + half_q[...]

    z_up, z_down = far_partners[0], far_partners[6]

    def ring_send(step):
        copies = []
        for buffers, ahead, steps, device in ((up, 4 - step, 4, z_up), (down, 8 - 3 + step, 3, z_down)):
            if step >= steps:
                continue
            at = rows_at(me.next_z(ahead), chunk)
            if step == 0:
                src = sum_q.at[at]
            else:
                src = buffers.at[step - 1]
                src[...] = src[...] + sum_q[at]
            copies.append(wire.send(src, buffers.at[step], device))
        return copies

    def arrive(copies):
        for copy in copies:
            copy.wait_recv()

    subs = codes_t.shape[0]
    groups = subs // 4
    base = other * (groups // 2)
    words, b_half = part_b.shape[0], part_b.shape[1] // 2

    ring = ring_send(0)
    collect(codes_t, d_ref, words_b, (0, groups // 2), base)
    transpose_half(words_b, other, part_b)
    b_core = wire.send(part_b.at[:, rows_at(other, b_half)], half_b, partners[0])
    arrive(ring)
    ring = ring_send(1)
    collect(codes_t, d_ref, words_b, (groups // 2, groups), base)
    transpose_half(words_b, me.core, part_b)
    arrive(ring)
    ring = ring_send(2)
    b_core.wait_recv()
    sum_b[...] = part_b[:, rows_at(me.core, b_half)] + half_b[...]

    lines = words // 8

    def lines_at(k, first, size, second=None):
        start = k * (words // 2) + first * lines
        if second is not None:
            start = start + second * size
        return pl.ds(pl.multiple_of(start, size), size)

    order = (
        ((me.y, me.next_y, y_partners), (me.x, me.next_x, x_partners)),
        ((me.x, me.next_x, x_partners), (me.y, me.next_y, y_partners)),
    )
    firsts = []
    for k in range(2):
        _, following, devices = order[k][0]
        for d in range(1, 4):
            firsts.append(
                wire.send(
                    sum_b.at[lines_at(k, following(d), lines)],
                    first_in.at[k, d - 1],
                    devices[d - 1],
                )
            )
    arrive(ring)
    ring = ring_send(3)
    arrive(firsts)
    seconds = []
    for k in range(2):
        index, _, _ = order[k][0]
        acc = sum_b[lines_at(k, index, lines)]
        for d in range(3):
            acc = acc + first_in[k, d]
        first_sum[k] = acc
        _, following, devices = order[k][1]
        for d in range(1, 4):
            seconds.append(
                wire.send(
                    first_sum.at[k, rows_at(following(d), lines // 4)],
                    second_in.at[k, d - 1],
                    devices[d - 1],
                )
            )

    arrive(ring)
    cross[0] = sum_q[rows_at(me.z, chunk)] + (up[3] + down[2])
    across = wire.send(cross.at[0], cross.at[1], partners[1])

    arrive(seconds)
    for k in range(2):
        index, _, _ = order[k][1]
        acc = first_sum[k, rows_at(index, lines // 4)]
        for d in range(3):
            acc = acc + second_in[k, d]
        last_in[me.z, k] = acc
    lasts = [wire.send(last_in.at[me.z], last_in.at[me.z], device) for device in far_partners]

    def q_rows(z):
        return pl.ds(pl.multiple_of(me.core * half + z * chunk, chunk), chunk)

    passed = []

    def pass_on(hop):
        copies = []
        for back_by, hops, device in ((8 - hop, 4, z_up), (hop, 3, z_down)):
            if hop < hops:
                at = q_rows(me.next_z(back_by))
                copies.append(wire.send(grad_q.at[at], grad_q.at[at], device))
        return copies

    def to_core(hop):
        for ahead, hops in ((8 - hop - 1, 4), (hop + 1, 3)):
            if hop < hops:
                at = q_rows(me.next_z(ahead))
                passed.append(wire.send(grad_q.at[at], grad_q.at[at], partners[0]))

    arrive([across])
    grad_q[q_rows(me.z)] = cross[0] + cross[1]
    ring = pass_on(0)
    passed.append(wire.send(grad_q.at[q_rows(me.z)], grad_q.at[q_rows(me.z)], partners[0]))

    columns = rows_at(me.core, b_half)
    arrive(lasts)
    acc = last_in[0]
    for z in range(1, 8):
        acc = acc + last_in[z]
    seconds = []
    for k in range(2):
        at = lines_at(k, order[k][0][0], lines // 4, order[k][1][0])
        grad_b[at, columns] = acc[k]
        for device in order[k][1][2]:
            seconds.append(wire.send(grad_b.at[at, columns], grad_b.at[at, columns], device))
    arrive(ring)
    ring = pass_on(1)
    to_core(0)
    arrive(seconds)
    firsts = []
    for k in range(2):
        at = lines_at(k, order[k][0][0], lines)
        for device in order[k][0][2]:
            firsts.append(wire.send(grad_b.at[at, columns], grad_b.at[at, columns], device))
    arrive(ring)
    ring = pass_on(2)
    to_core(1)
    arrive(firsts)
    passed.append(wire.send(grad_b.at[:, columns], grad_b.at[:, columns], partners[0]))
    arrive(ring)
    ring = pass_on(3)
    to_core(2)
    arrive(ring)
    to_core(3)
    arrive(passed)
    wire.finish()


def local(queries, codes, positive, codebook):
    rows, width = queries.shape
    docs, subs = codes.shape
    words = codebook.shape[0]
    chunk = rows // 16
    lines = words // 8
    half = width // 2
    vmem = pl.BlockSpec(memory_space=pltpu.VMEM)
    grad_q, grad_b, loss = pl.pallas_call(
        step,
        in_specs=[vmem] * 4,
        out_specs=(vmem, vmem, vmem),
        out_shape=(
            jax.ShapeDtypeStruct((rows, width), F32),
            jax.ShapeDtypeStruct((words, width), F32),
            jax.ShapeDtypeStruct((1, rows), F32),
        ),
        scratch_shapes=[
            pltpu.VMEM((width, words), F32),
            pltpu.VMEM((rows, 3 * width), BF16),
            pltpu.VMEM((3 * width, docs), BF16),
            pltpu.VMEM((width, 3 * rows), BF16),
            pltpu.VMEM((rows, docs), F32),
            pltpu.VMEM((8, rows), F32),
            pltpu.VMEM((rows, 128), F32),
            pltpu.VMEM((rows, 128), I32),
            pltpu.VMEM((rows, 128), F32),
            pltpu.VMEM((2 * rows, docs), BF16),
            pltpu.VMEM((rows, docs), BF16),
            pltpu.VMEM((rows, width), F32),
            pltpu.VMEM((rows, width), F32),
            pltpu.VMEM((3 * rows, docs), BF16),
            pltpu.VMEM((width, docs), F32),
            pltpu.VMEM((4, 8, rows), F32),
            pltpu.VMEM((8, 8, rows), F32),
            pltpu.VMEM((rows, width), F32),
            pltpu.VMEM((rows // 2, width), F32),
            pltpu.VMEM((rows // 2, width), F32),
            pltpu.VMEM((4, chunk, width), F32),
            pltpu.VMEM((3, chunk, width), F32),
            pltpu.VMEM((2, chunk, width), F32),
            pltpu.VMEM((width, words), F32),
            pltpu.VMEM((words, width), F32),
            pltpu.VMEM((words, half), F32),
            pltpu.VMEM((words, half), F32),
            pltpu.VMEM((2, 3, lines, half), F32),
            pltpu.VMEM((2, lines, half), F32),
            pltpu.VMEM((2, 3, lines // 4, half), F32),
            pltpu.VMEM((2, lines // 4, half), F32),
            pltpu.VMEM((8, 2, lines // 4, half), F32),
            pltpu.SemaphoreType.DMA((80,)),
            pltpu.SemaphoreType.DMA((80,)),
        ],
        compiler_params=pltpu.CompilerParams(collective_id=0, has_side_effects=True),
        name="step",
    )(queries, codes.T, positive.reshape(1, rows), codebook)
    return grad_q, grad_b, loss.reshape(rows)


def solution(mesh):
    return jax.shard_map(
        local,
        mesh=mesh,
        in_specs=(P("query", None), P("corpus", None), P("query"), P()),
        out_specs=(P("query", None), P(), P("query")),
        check_vma=False,
    )
```

```python
import jax
import jax.numpy as jnp
from jax import lax
from jax.experimental import pallas as pl
from jax.experimental.pallas import tpu as pltpu
from jax.sharding import PartitionSpec as P

F32, BF16, I32 = jnp.float32, jnp.bfloat16, jnp.int32
NN = (((1,), (0,)), ((), ()))
NT = (((1,), (1,)), ((), ()))
HIGH_CODES = 64
LOW_CODES = 4
UNROLL = 6
COPIES = 102


def dot(a, b, dims=NN):
    return lax.dot_general(a, b, dims, preferred_element_type=F32)


def split(x):
    high = x.astype(BF16)
    return high, (x - high.astype(F32)).astype(BF16)


def split3(x):
    high = x.astype(BF16)
    rest = x - high.astype(F32)
    mid = rest.astype(BF16)
    return high, mid, (rest - mid.astype(F32)).astype(BF16)


def split_queries(q_ref, q3, step=32):
    width = q_ref.shape[1]

    def block(b, _):
        at = pl.ds(pl.multiple_of(b * step, step), step)
        high, mid, low = split3(q_ref[at, :])
        q3[at, :width] = high
        q3[at, width : 2 * width] = mid
        q3[at, 2 * width :] = low
        return 0

    lax.fori_loop(0, q_ref.shape[0] // step, block, 0)


def transpose_queries(q_ref, q_t, step=128):
    rows = q_ref.shape[0]

    def block(b, _):
        at = pl.ds(pl.multiple_of(b * step, step), step)
        high, mid = split(q_ref[:, at].T)
        q_t[at, :rows] = high
        q_t[at, rows : 2 * rows] = mid
        q_t[at, 2 * rows : 3 * rows] = high
        q_t[at, 3 * rows :] = jnp.zeros((step, q_t.shape[1] - 3 * rows), BF16)
        return 0

    lax.fori_loop(0, q_ref.shape[1] // step, block, 0)


def transpose_book(book_ref, book_t, step=128):
    def block(b, _):
        at = pl.ds(pl.multiple_of(b * step, step), step)
        book_t[at, :] = book_ref[:, at].T
        return 0

    lax.fori_loop(0, book_ref.shape[1] // step, block, 0)


def rebuild(codes_t, book_t, r3, unroll=4):
    subs, docs = codes_t.shape
    width = book_t.shape[0]
    sub_width = width // subs

    def pair(p):
        parts = []
        for side in range(2):
            m = 2 * p + side
            base = pl.multiple_of(m * sub_width, sub_width)
            low = book_t[pl.ds(base, sub_width), :128]
            high = book_t[pl.ds(base, sub_width), 128:]
            code = codes_t[pl.ds(m, 1), :]
            tiles = []
            for t in range(docs // 128):
                picked = jnp.broadcast_to(code[:, 128 * t : 128 * t + 128], (sub_width, 128))
                lane = picked & 127
                a = jnp.take_along_axis(low, lane, axis=1, mode="promise_in_bounds")
                b = jnp.take_along_axis(high, lane, axis=1, mode="promise_in_bounds")
                tiles.append(jnp.where(picked < 128, a, b))
            parts.append(jnp.concatenate(tiles, axis=1))
        high, mid, low = split3(jnp.concatenate(parts, axis=0))
        at = pl.multiple_of(2 * p * sub_width, 2 * sub_width)
        r3[pl.ds(at, 2 * sub_width), :] = low
        r3[pl.ds(width + at, 2 * sub_width), :] = mid
        r3[pl.ds(2 * width + at, 2 * sub_width), :] = high

    def block(b, _):
        for u in range(unroll):
            pair(unroll * b + u)
        return 0

    lax.fori_loop(0, subs // 2 // unroll, block, 0)


def score(q3, r3, s_ref, tile=512):
    width = q3.shape[1] // 3

    def block(t, _):
        at = pl.ds(pl.multiple_of(t * tile, tile), tile)
        acc = dot(q3[...], r3[:, at])
        acc = acc + dot(q3[:, : 2 * width], r3[width:, at])
        s_ref[:, at] = acc + dot(q3[:, :width], r3[2 * width :, at])
        return 0

    lax.fori_loop(0, s_ref.shape[1] // tile, block, 0)


def statistics(s_ref, pos_col, cols, step=64):
    rows, docs = s_ref.shape
    lane = lax.broadcasted_iota(I32, (step, 128), 1)
    ids = lax.broadcasted_iota(I32, (step, docs), 1)

    def block(b, _):
        at = pl.ds(pl.multiple_of(b * step, step), step)
        s = s_ref[at, :]
        top = jnp.max(s, axis=1, keepdims=True)
        own = jnp.sum(jnp.where(pos_col[at, :1] == ids, s, 0.0), axis=1, keepdims=True)
        e = jnp.exp(s - top)
        total = jnp.sum(e, axis=1, keepdims=True)
        s_ref[at, :] = e
        cols[at, :] = jnp.where(
            lane == 0, top, jnp.where(lane == 1, total, jnp.where(lane == 2, own, 0.0))
        )
        return 0

    lax.fori_loop(0, rows // step, block, 0)


def as_column(row, column):
    column[...] = jnp.broadcast_to(row, (128, row.shape[1])).T


def expose(e_ref, pos_col, e2, hits, step=32):
    rows, docs = e_ref.shape
    ids = lax.broadcasted_iota(I32, (step, docs), 1)

    def block(b, _):
        at = pl.ds(pl.multiple_of(b * step, step), step)
        high, low = split(e_ref[at, :])
        e2[at, :] = low
        e2[pl.ds(pl.multiple_of(rows + b * step, step), step), :] = high
        hits[at, :] = jnp.where(pos_col[at, :1] == ids, 1.0, 0.0).astype(BF16)
        return 0

    lax.fori_loop(0, rows // step, block, 0)


def pull(hits, r3, pulled, tile=256):
    width = r3.shape[0] // 3

    def block(t, _):
        base = pl.multiple_of(t * tile, tile)
        acc = dot(hits[...], r3[pl.ds(width + base, tile), :], NT)
        pulled[:, pl.ds(base, tile)] = acc + dot(hits[...], r3[pl.ds(2 * width + base, tile), :], NT)
        return 0

    lax.fori_loop(0, width // tile, block, 0)


def spread_out(e2, r3, spread, tile=256):
    rows = e2.shape[0] // 2
    width = r3.shape[0] // 3

    def block(t, _):
        base = pl.multiple_of(t * tile, tile)
        mid = r3[pl.ds(width + base, tile), :]
        high = r3[pl.ds(2 * width + base, tile), :]
        acc = dot(e2[rows:, :], mid, NT)
        acc = acc + dot(e2[:rows, :], high, NT)
        spread[:, pl.ds(base, tile)] = acc + dot(e2[rows:, :], high, NT)
        return 0

    lax.fori_loop(0, width // tile, block, 0)


def query_gradient(spread, pulled, scale_col, out, step=32):
    def block(b, _):
        at = pl.ds(pl.multiple_of(b * step, step), step)
        out[at, :] = spread[at, :] * scale_col[at, :1] - pulled[at, :]
        return 0

    lax.fori_loop(0, spread.shape[0] // step, block, 0)


def weigh(e_ref, scale_col, pos_col, w3, step=32):
    rows, docs = e_ref.shape
    w3[3 * rows :, :] = jnp.zeros((w3.shape[0] - 3 * rows, docs), BF16)
    ids = lax.broadcasted_iota(I32, (step, docs), 1)

    def block(b, _):
        at = pl.ds(pl.multiple_of(b * step, step), step)
        w = e_ref[at, :] * scale_col[at, :1]
        w = w - jnp.where(pos_col[at, :1] == ids, 1.0, 0.0)
        high, low = split(w)
        w3[at, :] = low
        w3[pl.ds(pl.multiple_of(rows + b * step, step), step), :] = high
        w3[pl.ds(pl.multiple_of(2 * rows + b * step, step), step), :] = high
        return 0

    lax.fori_loop(0, rows // step, block, 0)


def document_gradient(w3, q_t, out, tile=256):
    for t in range(out.shape[1] // tile):
        at = slice(t * tile, t * tile + tile)
        out[:, at] = dot(q_t[...], w3[:, at])


def collect(codes_t, d_ref, out, blocks, base, group=4, unroll=UNROLL):
    subs, docs = codes_t.shape
    sub_width = d_ref.shape[0] // subs
    word = lax.broadcasted_iota(I32, (HIGH_CODES, docs), 0)
    lane = lax.broadcasted_iota(I32, (sub_width, 128), 1)

    def one(b):
        g = lax.rem(b + base, subs // group)
        tables, values = [], []
        for s in range(group):
            m = group * g + s
            code = codes_t[pl.ds(m, 1), :]
            inner = code & (HIGH_CODES - 1)
            outer = jnp.broadcast_to(code >> 6, (sub_width, docs))
            tables.append(jnp.where(word == inner, 1.0, 0.0).astype(BF16))
            d = d_ref[pl.ds(pl.multiple_of(m * sub_width, sub_width), sub_width), :]
            high = d.astype(BF16).astype(F32)
            low = d - high
            masks = [outer == k for k in range(LOW_CODES)]
            rows = [jnp.where(mask, part, 0.0) for part in (high, low) for mask in masks]
            values.append(jnp.concatenate(rows, axis=0).astype(BF16))
        found = dot(jnp.concatenate(values, axis=0), jnp.concatenate(tables, axis=0), NT)
        rows = 2 * LOW_CODES * sub_width
        for s in range(group):
            at = 128 * (s // 2)
            piece = found[rows * s : rows * (s + 1), at : at + 128]
            piece = piece[: rows // 2] + piece[rows // 2 :]
            parts = [piece[sub_width * k : sub_width * (k + 1)] for k in range(LOW_CODES)]
            start = pl.multiple_of((group * g + s) * sub_width, sub_width)
            for k in range(2):
                first, second = parts[2 * k], parts[2 * k + 1]
                if s % 2:
                    first = pltpu.roll(first, 64, 1)
                else:
                    second = pltpu.roll(second, 64, 1)
                out[pl.ds(start, sub_width), 128 * k : 128 * k + 128] = jnp.where(
                    lane < 64, first, second
                )

    def block(b, _):
        for u in range(unroll):
            one(unroll * b + u)
        return 0

    lax.fori_loop(blocks[0] // unroll, blocks[1] // unroll, block, 0)


def transpose_half(part, core, out, step=128):
    half = part.shape[0] // 2

    def block(b, _):
        at = pl.ds(pl.multiple_of(core * half + b * step, step), step)
        out[:, at] = part[at, :].T
        return 0

    lax.fori_loop(0, half // step, block, 0)


class Place:
    def __init__(self):
        query, corpus = lax.axis_index("query"), lax.axis_index("corpus")
        self.y = lax.rem(query, 4)
        self.x = 2 * lax.div(query, 4) + lax.rem(lax.div(corpus, 2), 2)
        self.z = lax.div(corpus, 4)
        self.core = lax.rem(corpus, 2)

    def at(self, x=None, y=None, z=None, core=None):
        x = self.x if x is None else x
        y = self.y if y is None else y
        z = self.z if z is None else z
        core = self.core if core is None else core
        return (4 * lax.div(x, 2) + y, 4 * z + 2 * lax.rem(x, 2) + core)

    def next_y(self, d):
        return lax.rem(self.y + d, 4)

    def next_x(self, d):
        return lax.rem(self.x + d, 4)

    def next_z(self, d):
        return lax.rem(self.z + d, 8)


class Wire:
    def __init__(self, sent, arrived):
        self.sent, self.arrived, self.copies = sent, arrived, []

    def send(self, src, dst, device):
        i = len(self.copies)
        copy = pltpu.make_async_remote_copy(
            src_ref=src,
            dst_ref=dst,
            send_sem=self.sent.at[i],
            recv_sem=self.arrived.at[i],
            device_id=device,
            device_id_type=pl.DeviceIdType.MESH,
        )
        copy.start()
        self.copies.append(copy)
        return copy

    def finish(self):
        for copy in self.copies:
            copy.wait_send()


def rows_at(index, size):
    return pl.ds(pl.multiple_of(index * size, size), size)


def merge(stats):
    top = stats[0][0:1]
    for s in stats[1:]:
        top = jnp.maximum(top, s[0:1])
    total = sum(s[1:2] * jnp.exp(s[0:1] - top) for s in stats)
    own = sum(s[2:3] for s in stats)
    pad = jnp.zeros((8 - 3, top.shape[1]), F32)
    return jnp.concatenate([top, total, own, pad], axis=0)


def step(
    q_ref, codes_t, pos_ref, book_ref,
    grad_q, grad_b, loss_ref,
    book_t, q3, r3, q_t, e_ref, stats_ref, cols,
    pos_col, scale_col, e2, hits, spread, pulled, w3, d_ref,
    near, far, part_q, half_q, sum_q, up, down, cross,
    words_b, part_b, half_b, sum_b, first_in, first_sum, second_in, second_sum, last_in,
    sent, arrived,
):
    me = Place()
    wire = Wire(sent, arrived)
    x_pair = me.x + 1 - 2 * lax.rem(me.x, 2)
    other = 1 - me.core
    partners = [me.at(core=other), me.at(x=x_pair), me.at(x=x_pair, core=other)]
    far_partners = [me.at(z=me.next_z(d)) for d in range(1, 8)]
    y_partners = [me.at(y=me.next_y(d)) for d in range(1, 4)]
    x_partners = [me.at(x=me.next_x(d)) for d in range(1, 4)]
    greeted = [partners[0], partners[2]] + far_partners + y_partners + x_partners
    barrier = pltpu.get_barrier_semaphore()
    for device in greeted:
        pl.semaphore_signal(barrier, inc=1, device_id=device, device_id_type=pl.DeviceIdType.MESH)

    transpose_book(book_ref, book_t)
    split_queries(q_ref, q3)
    rebuild(codes_t, book_t, r3)
    score(q3, r3, e_ref)
    docs = codes_t.shape[1]
    here = pos_ref[...].reshape(1, -1) - lax.axis_index("corpus") * docs
    as_column(here, pos_col)
    statistics(e_ref, pos_col, cols)
    stats_ref[...] = cols[...].T[:8]
    pl.semaphore_wait(barrier, len(greeted))

    mine = 2 * lax.rem(me.x, 2) + me.core
    near[mine] = stats_ref[...]
    copies = [wire.send(stats_ref, near.at[mine], device) for device in partners]
    expose(e_ref, pos_col, e2, hits)
    pull(hits, r3, pulled)
    for copy in copies:
        copy.wait_recv()
    far[me.z] = merge([near[k] for k in range(4)])
    copies = [wire.send(far.at[me.z], far.at[me.z], device) for device in far_partners]
    spread_out(e2, r3, spread)
    transpose_queries(q_ref, q_t)
    for copy in copies:
        copy.wait_recv()
    whole = merge([far[k] for k in range(8)])
    log_total = whole[0:1] + jnp.log(whole[1:2])
    loss_ref[...] = (log_total - whole[2:3]).reshape(-1)
    as_column(jnp.exp(stats_ref[0:1] - log_total), scale_col)

    query_gradient(spread, pulled, scale_col, part_q)
    half = part_q.shape[0] // 2
    chunk = half // 8
    q_core = wire.send(part_q.at[rows_at(other, half)], half_q, partners[0])
    weigh(e_ref, scale_col, pos_col, w3)
    document_gradient(w3, q_t, d_ref)
    q_core.wait_recv()
    sum_q[...] = part_q[rows_at(me.core, half)] + half_q[...]

    z_up, z_down = far_partners[0], far_partners[6]

    def ring_send(step):
        copies = []
        for buffers, ahead, steps, device in ((up, 4 - step, 4, z_up), (down, 8 - 3 + step, 3, z_down)):
            if step >= steps:
                continue
            at = rows_at(me.next_z(ahead), chunk)
            if step == 0:
                src = sum_q.at[at]
            else:
                src = buffers.at[step - 1]
                src[...] = src[...] + sum_q[at]
            copies.append(wire.send(src, buffers.at[step], device))
        return copies

    def arrive(copies):
        for copy in copies:
            copy.wait_recv()

    subs = codes_t.shape[0]
    groups = subs // 4
    base = other * (groups // 2)
    words, b_half = part_b.shape[0], part_b.shape[1] // 2

    ring = ring_send(0)
    collect(codes_t, d_ref, words_b, (0, groups // 2), base)
    transpose_half(words_b, other, part_b)
    b_core = wire.send(part_b.at[:, rows_at(other, b_half)], half_b, partners[0])
    arrive(ring)
    ring = ring_send(1)
    collect(codes_t, d_ref, words_b, (groups // 2, groups), base)
    transpose_half(words_b, me.core, part_b)
    arrive(ring)
    ring = ring_send(2)
    b_core.wait_recv()
    sum_b[...] = part_b[:, rows_at(me.core, b_half)] + half_b[...]

    lines = words // 8

    def lines_at(k, first, size, second=None):
        start = k * (words // 2) + first * lines
        if second is not None:
            start = start + second * size
        return pl.ds(pl.multiple_of(start, size), size)

    order = (
        ((me.y, me.next_y, y_partners), (me.x, me.next_x, x_partners)),
        ((me.x, me.next_x, x_partners), (me.y, me.next_y, y_partners)),
    )
    firsts = []
    for k in range(2):
        _, following, devices = order[k][0]
        for d in range(1, 4):
            firsts.append(
                wire.send(
                    sum_b.at[lines_at(k, following(d), lines)],
                    first_in.at[k, d - 1],
                    devices[d - 1],
                )
            )
    arrive(ring)
    ring = ring_send(3)
    arrive(firsts)
    seconds = []
    for k in range(2):
        index, _, _ = order[k][0]
        acc = sum_b[lines_at(k, index, lines)]
        for d in range(3):
            acc = acc + first_in[k, d]
        first_sum[k] = acc
        _, following, devices = order[k][1]
        for d in range(1, 4):
            seconds.append(
                wire.send(
                    first_sum.at[k, rows_at(following(d), lines // 4)],
                    second_in.at[k, d - 1],
                    devices[d - 1],
                )
            )

    arrive(ring)
    cross[0] = sum_q[rows_at(me.z, chunk)] + (up[3] + down[2])
    across = wire.send(cross.at[0], cross.at[1], partners[1])

    arrive(seconds)
    for k in range(2):
        index, _, _ = order[k][1]
        acc = first_sum[k, rows_at(index, lines // 4)]
        for d in range(3):
            acc = acc + second_in[k, d]
        last_in[me.z, k] = acc
    lasts = [wire.send(last_in.at[me.z], last_in.at[me.z], device) for device in far_partners]

    def q_rows(z):
        return pl.ds(pl.multiple_of(me.core * half + z * chunk, chunk), chunk)

    passed = []
    slices = 3
    size = chunk // slices

    def q_slice(z, k):
        return pl.ds(pl.multiple_of(me.core * half + z * chunk + k * size, size), size)

    def share(at, device):
        return wire.send(grad_q.at[at], grad_q.at[at], device)

    def pass_on(hop, k):
        copies = []
        for back_by, hops, device in ((8 - hop, 4, z_up), (hop, 3, z_down)):
            if hop < hops:
                copies.append(share(q_slice(me.next_z(back_by), k), device))
        return copies

    def to_core(hop, k):
        for ahead, hops in ((8 - hop - 1, 4), (hop + 1, 3)):
            if hop < hops:
                passed.append(share(q_slice(me.next_z(ahead), k), partners[0]))

    def next_hop(ring, hop):
        following = []
        for k in range(slices):
            arrive(ring[k])
            following.append(pass_on(hop, k) if hop < 4 else [])
            to_core(hop - 1, k)
        return following

    arrive([across])
    grad_q[q_rows(me.z)] = cross[0] + cross[1]
    ring = [pass_on(0, k) for k in range(slices)]
    passed.append(share(q_rows(me.z), partners[0]))

    columns = rows_at(me.core, b_half)

    def share_b(at, device):
        return wire.send(grad_b.at[at, columns], grad_b.at[at, columns], device)

    arrive(lasts)
    acc = last_in[0]
    for z in range(1, 8):
        acc = acc + last_in[z]
    seconds = []
    for k in range(2):
        at = lines_at(k, order[k][0][0], lines // 4, order[k][1][0])
        grad_b[at, columns] = acc[k]
        for device in order[k][1][2]:
            seconds.append(share_b(at, device))
    ring = next_hop(ring, 1)
    arrive(seconds)
    firsts = []
    for k in range(2):
        at = lines_at(k, order[k][0][0], lines)
        for device in order[k][0][2]:
            firsts.append(share_b(at, device))
    for k in range(2):
        passed.append(share_b(lines_at(k, order[k][0][0], lines), partners[0]))
    ring = next_hop(ring, 2)
    ring = next_hop(ring, 3)
    for d in (1, 3, 2):
        for k in range(2):
            arrive([firsts[3 * k + d - 1]])
            back = order[k][0][1](4 - d)
            passed.append(share_b(lines_at(k, back, lines), partners[0]))
    next_hop(ring, 4)
    arrive(passed)
    wire.finish()
    assert len(wire.copies) == COPIES, len(wire.copies)


def local(queries, codes, positive, codebook):
    rows, width = queries.shape
    docs, subs = codes.shape
    words = codebook.shape[0]
    chunk = rows // 16
    lines = words // 8
    half = width // 2
    depth = 256 * pl.cdiv(3 * rows, 256)
    vmem = pl.BlockSpec(memory_space=pltpu.VMEM)
    grad_q, grad_b, loss = pl.pallas_call(
        step,
        in_specs=[vmem] * 4,
        out_specs=(vmem, vmem, vmem),
        out_shape=(
            jax.ShapeDtypeStruct((rows, width), F32),
            jax.ShapeDtypeStruct((words, width), F32),
            jax.ShapeDtypeStruct((rows,), F32),
        ),
        scratch_shapes=[
            pltpu.VMEM((width, words), F32),
            pltpu.VMEM((rows, 3 * width), BF16),
            pltpu.VMEM((3 * width, docs), BF16),
            pltpu.VMEM((width, depth), BF16),
            pltpu.VMEM((rows, docs), F32),
            pltpu.VMEM((8, rows), F32),
            pltpu.VMEM((rows, 128), F32),
            pltpu.VMEM((rows, 128), I32),
            pltpu.VMEM((rows, 128), F32),
            pltpu.VMEM((2 * rows, docs), BF16),
            pltpu.VMEM((rows, docs), BF16),
            pltpu.VMEM((rows, width), F32),
            pltpu.VMEM((rows, width), F32),
            pltpu.VMEM((depth, docs), BF16),
            pltpu.VMEM((width, docs), F32),
            pltpu.VMEM((4, 8, rows), F32),
            pltpu.VMEM((8, 8, rows), F32),
            pltpu.VMEM((rows, width), F32),
            pltpu.VMEM((rows // 2, width), F32),
            pltpu.VMEM((rows // 2, width), F32),
            pltpu.VMEM((4, chunk, width), F32),
            pltpu.VMEM((3, chunk, width), F32),
            pltpu.VMEM((2, chunk, width), F32),
            pltpu.VMEM((width, words), F32),
            pltpu.VMEM((words, width), F32),
            pltpu.VMEM((words, half), F32),
            pltpu.VMEM((words, half), F32),
            pltpu.VMEM((2, 3, lines, half), F32),
            pltpu.VMEM((2, lines, half), F32),
            pltpu.VMEM((2, 3, lines // 4, half), F32),
            pltpu.VMEM((2, lines // 4, half), F32),
            pltpu.VMEM((8, 2, lines // 4, half), F32),
            pltpu.SemaphoreType.DMA((COPIES,)),
            pltpu.SemaphoreType.DMA((COPIES,)),
        ],
        compiler_params=pltpu.CompilerParams(
            collective_id=0, has_side_effects=True, vmem_limit_bytes=42 << 20
        ),
        name="step",
    )(queries, codes.T, positive, codebook)
    return grad_q, grad_b, loss


def solution(mesh):
    return jax.shard_map(
        local,
        mesh=mesh,
        in_specs=(P("query", None), P("corpus", None), P("query"), P()),
        out_specs=(P("query", None), P(), P("query")),
        check_vma=False,
    )
```

```python
import jax
import jax.numpy as jnp
from jax import lax
from jax.experimental import pallas as pl
from jax.experimental.pallas import tpu as pltpu
from jax.sharding import PartitionSpec as P

F32, BF16, I32 = jnp.float32, jnp.bfloat16, jnp.int32
NN = (((1,), (0,)), ((), ()))
NT = (((1,), (1,)), ((), ()))
HIGH_CODES = 64
LOW_CODES = 4
UNROLL = 6
COPIES = 102


def dot(a, b, dims=NN):
    return lax.dot_general(a, b, dims, preferred_element_type=F32)


def split(x):
    high = x.astype(BF16)
    return high, (x - high.astype(F32)).astype(BF16)


def split3(x):
    high = x.astype(BF16)
    rest = x - high.astype(F32)
    mid = rest.astype(BF16)
    return high, mid, (rest - mid.astype(F32)).astype(BF16)


def split_queries(q_ref, q3, step=32):
    width = q_ref.shape[1]

    def block(b, _):
        at = pl.ds(pl.multiple_of(b * step, step), step)
        high, mid, low = split3(q_ref[at, :])
        q3[at, :width] = high
        q3[at, width : 2 * width] = mid
        q3[at, 2 * width :] = low
        return 0

    lax.fori_loop(0, q_ref.shape[0] // step, block, 0)


def transpose_queries(q_ref, q_t, step=128):
    rows = q_ref.shape[0]

    def block(b, _):
        at = pl.ds(pl.multiple_of(b * step, step), step)
        high, mid = split(q_ref[:, at].T)
        q_t[at, :rows] = high
        q_t[at, rows : 2 * rows] = mid
        q_t[at, 2 * rows : 3 * rows] = high
        q_t[at, 3 * rows :] = jnp.zeros((step, q_t.shape[1] - 3 * rows), BF16)
        return 0

    lax.fori_loop(0, q_ref.shape[1] // step, block, 0)


def transpose_book(book_ref, book_t, step=128):
    def block(b, _):
        at = pl.ds(pl.multiple_of(b * step, step), step)
        book_t[at, :] = book_ref[:, at].T
        return 0

    lax.fori_loop(0, book_ref.shape[1] // step, block, 0)


def rebuild(codes_t, book_t, r3, unroll=4):
    subs, docs = codes_t.shape
    width = book_t.shape[0]
    sub_width = width // subs

    def pair(p):
        parts = []
        for side in range(2):
            m = 2 * p + side
            base = pl.multiple_of(m * sub_width, sub_width)
            low = book_t[pl.ds(base, sub_width), :128]
            high = book_t[pl.ds(base, sub_width), 128:]
            code = codes_t[pl.ds(m, 1), :]
            tiles = []
            for t in range(docs // 128):
                picked = jnp.broadcast_to(code[:, 128 * t : 128 * t + 128], (sub_width, 128))
                lane = picked & 127
                a = jnp.take_along_axis(low, lane, axis=1, mode="promise_in_bounds")
                b = jnp.take_along_axis(high, lane, axis=1, mode="promise_in_bounds")
                tiles.append(jnp.where(picked < 128, a, b))
            parts.append(jnp.concatenate(tiles, axis=1))
        high, mid, low = split3(jnp.concatenate(parts, axis=0))
        at = pl.multiple_of(2 * p * sub_width, 2 * sub_width)
        r3[pl.ds(at, 2 * sub_width), :] = low
        r3[pl.ds(width + at, 2 * sub_width), :] = mid
        r3[pl.ds(2 * width + at, 2 * sub_width), :] = high

    def block(b, _):
        for u in range(unroll):
            pair(unroll * b + u)
        return 0

    lax.fori_loop(0, subs // 2 // unroll, block, 0)


def score(q3, r3, s_ref, tile=512):
    width = q3.shape[1] // 3

    def block(t, _):
        at = pl.ds(pl.multiple_of(t * tile, tile), tile)
        acc = dot(q3[...], r3[:, at])
        acc = acc + dot(q3[:, : 2 * width], r3[width:, at])
        s_ref[:, at] = acc + dot(q3[:, :width], r3[2 * width :, at])
        return 0

    lax.fori_loop(0, s_ref.shape[1] // tile, block, 0)


def statistics(s_ref, pos_col, cols, step=64):
    rows, docs = s_ref.shape
    lane = lax.broadcasted_iota(I32, (step, 128), 1)
    ids = lax.broadcasted_iota(I32, (step, docs), 1)

    def block(b, _):
        at = pl.ds(pl.multiple_of(b * step, step), step)
        s = s_ref[at, :]
        top = jnp.max(s, axis=1, keepdims=True)
        own = jnp.sum(jnp.where(pos_col[at, :1] == ids, s, 0.0), axis=1, keepdims=True)
        e = jnp.exp(s - top)
        total = jnp.sum(e, axis=1, keepdims=True)
        s_ref[at, :] = e
        cols[at, :] = jnp.where(
            lane == 0, top, jnp.where(lane == 1, total, jnp.where(lane == 2, own, 0.0))
        )
        return 0

    lax.fori_loop(0, rows // step, block, 0)


def as_column(row, column):
    column[...] = jnp.broadcast_to(row, (128, row.shape[1])).T


def expose(e_ref, pos_col, e2, hits, step=32):
    rows, docs = e_ref.shape
    ids = lax.broadcasted_iota(I32, (step, docs), 1)

    def block(b, _):
        at = pl.ds(pl.multiple_of(b * step, step), step)
        high, low = split(e_ref[at, :])
        e2[at, :] = low
        e2[pl.ds(pl.multiple_of(rows + b * step, step), step), :] = high
        hits[at, :] = jnp.where(pos_col[at, :1] == ids, 1.0, 0.0).astype(BF16)
        return 0

    lax.fori_loop(0, rows // step, block, 0)


def pull(hits, r3, pulled, tile=256):
    width = r3.shape[0] // 3

    def block(t, _):
        base = pl.multiple_of(t * tile, tile)
        acc = dot(hits[...], r3[pl.ds(width + base, tile), :], NT)
        pulled[:, pl.ds(base, tile)] = acc + dot(hits[...], r3[pl.ds(2 * width + base, tile), :], NT)
        return 0

    lax.fori_loop(0, width // tile, block, 0)


def spread_out(e2, r3, spread, tile=256):
    rows = e2.shape[0] // 2
    width = r3.shape[0] // 3

    def block(t, _):
        base = pl.multiple_of(t * tile, tile)
        mid = r3[pl.ds(width + base, tile), :]
        high = r3[pl.ds(2 * width + base, tile), :]
        acc = dot(e2[rows:, :], mid, NT)
        acc = acc + dot(e2[:rows, :], high, NT)
        spread[:, pl.ds(base, tile)] = acc + dot(e2[rows:, :], high, NT)
        return 0

    lax.fori_loop(0, width // tile, block, 0)


def query_gradient(spread, pulled, scale_col, out, step=32):
    def block(b, _):
        at = pl.ds(pl.multiple_of(b * step, step), step)
        out[at, :] = spread[at, :] * scale_col[at, :1] - pulled[at, :]
        return 0

    lax.fori_loop(0, spread.shape[0] // step, block, 0)


def weigh(e_ref, scale_col, pos_col, w3, step=32):
    rows, docs = e_ref.shape
    w3[3 * rows :, :] = jnp.zeros((w3.shape[0] - 3 * rows, docs), BF16)
    ids = lax.broadcasted_iota(I32, (step, docs), 1)

    def block(b, _):
        at = pl.ds(pl.multiple_of(b * step, step), step)
        w = e_ref[at, :] * scale_col[at, :1]
        w = w - jnp.where(pos_col[at, :1] == ids, 1.0, 0.0)
        high, low = split(w)
        w3[at, :] = low
        w3[pl.ds(pl.multiple_of(rows + b * step, step), step), :] = high
        w3[pl.ds(pl.multiple_of(2 * rows + b * step, step), step), :] = high
        return 0

    lax.fori_loop(0, rows // step, block, 0)


def document_gradient(w3, q_t, out, tile=256):
    for t in range(out.shape[1] // tile):
        at = slice(t * tile, t * tile + tile)
        out[:, at] = dot(q_t[...], w3[:, at])


def collect(codes_t, d_ref, out, blocks, base, group=4, unroll=UNROLL):
    subs, docs = codes_t.shape
    sub_width = d_ref.shape[0] // subs
    word = lax.broadcasted_iota(I32, (HIGH_CODES, docs), 0)
    lane = lax.broadcasted_iota(I32, (sub_width, 128), 1)

    def one(b):
        g = lax.rem(b + base, subs // group)
        tables, values = [], []
        for s in range(group):
            m = group * g + s
            code = codes_t[pl.ds(m, 1), :]
            inner = code & (HIGH_CODES - 1)
            outer = jnp.broadcast_to(code >> 6, (sub_width, docs))
            tables.append(jnp.where(word == inner, 1.0, 0.0).astype(BF16))
            d = d_ref[pl.ds(pl.multiple_of(m * sub_width, sub_width), sub_width), :]
            high = d.astype(BF16).astype(F32)
            low = d - high
            masks = [outer == k for k in range(LOW_CODES)]
            rows = [jnp.where(mask, part, 0.0) for part in (high, low) for mask in masks]
            values.append(jnp.concatenate(rows, axis=0).astype(BF16))
        found = dot(jnp.concatenate(values, axis=0), jnp.concatenate(tables, axis=0), NT)
        rows = 2 * LOW_CODES * sub_width
        for s in range(group):
            at = 128 * (s // 2)
            piece = found[rows * s : rows * (s + 1), at : at + 128]
            piece = piece[: rows // 2] + piece[rows // 2 :]
            parts = [piece[sub_width * k : sub_width * (k + 1)] for k in range(LOW_CODES)]
            start = pl.multiple_of((group * g + s) * sub_width, sub_width)
            for k in range(2):
                first, second = parts[2 * k], parts[2 * k + 1]
                if s % 2:
                    first = pltpu.roll(first, 64, 1)
                else:
                    second = pltpu.roll(second, 64, 1)
                out[pl.ds(start, sub_width), 128 * k : 128 * k + 128] = jnp.where(
                    lane < 64, first, second
                )

    def block(b, _):
        for u in range(unroll):
            one(unroll * b + u)
        return 0

    lax.fori_loop(blocks[0] // unroll, blocks[1] // unroll, block, 0)


def transpose_half(part, core, out, step=128):
    half = part.shape[0] // 2

    def block(b, _):
        at = pl.ds(pl.multiple_of(core * half + b * step, step), step)
        out[:, at] = part[at, :].T
        return 0

    lax.fori_loop(0, half // step, block, 0)


class Place:
    def __init__(self):
        query, corpus = lax.axis_index("query"), lax.axis_index("corpus")
        self.y = lax.rem(query, 4)
        self.x = 2 * lax.div(query, 4) + lax.rem(lax.div(corpus, 2), 2)
        self.z = lax.div(corpus, 4)
        self.core = lax.rem(corpus, 2)

    def at(self, x=None, y=None, z=None, core=None):
        x = self.x if x is None else x
        y = self.y if y is None else y
        z = self.z if z is None else z
        core = self.core if core is None else core
        return (4 * lax.div(x, 2) + y, 4 * z + 2 * lax.rem(x, 2) + core)

    def next_y(self, d):
        return lax.rem(self.y + d, 4)

    def next_x(self, d):
        return lax.rem(self.x + d, 4)

    def next_z(self, d):
        return lax.rem(self.z + d, 8)


class Wire:
    def __init__(self, sent, arrived):
        self.sent, self.arrived, self.copies = sent, arrived, []

    def send(self, src, dst, device):
        i = len(self.copies)
        copy = pltpu.make_async_remote_copy(
            src_ref=src,
            dst_ref=dst,
            send_sem=self.sent.at[i],
            recv_sem=self.arrived.at[i],
            device_id=device,
            device_id_type=pl.DeviceIdType.MESH,
        )
        copy.start()
        self.copies.append(copy)
        return copy

    def finish(self):
        for copy in self.copies:
            copy.wait_send()


def rows_at(index, size):
    return pl.ds(pl.multiple_of(index * size, size), size)


def merge(stats):
    top = stats[0][0:1]
    for s in stats[1:]:
        top = jnp.maximum(top, s[0:1])
    total = sum(s[1:2] * jnp.exp(s[0:1] - top) for s in stats)
    own = sum(s[2:3] for s in stats)
    pad = jnp.zeros((8 - 3, top.shape[1]), F32)
    return jnp.concatenate([top, total, own, pad], axis=0)


def step(
    q_hbm, codes_hbm, pos_ref, book_hbm,
    grad_q, grad_b, loss_ref,
    q_ref, codes_t, book_ref, book_t, q3, r3, q_t, e_ref, stats_ref, cols,
    pos_col, scale_col, e2, hits, spread, pulled, w3, d_ref,
    near, far, part_q, half_q, sum_q, up, down, cross,
    words_b, part_b, half_b, sum_b, first_in, first_sum, second_in, second_sum, last_in,
    sent, arrived, loaded,
):
    loads = [
        pltpu.make_async_copy(book_hbm, book_ref, loaded.at[0]),
        pltpu.make_async_copy(codes_hbm, codes_t, loaded.at[1]),
        pltpu.make_async_copy(q_hbm, q_ref, loaded.at[2]),
    ]
    for load in loads:
        load.start()
    me = Place()
    wire = Wire(sent, arrived)
    x_pair = me.x + 1 - 2 * lax.rem(me.x, 2)
    other = 1 - me.core
    partners = [me.at(core=other), me.at(x=x_pair), me.at(x=x_pair, core=other)]
    far_partners = [me.at(z=me.next_z(d)) for d in range(1, 8)]
    y_partners = [me.at(y=me.next_y(d)) for d in range(1, 4)]
    x_partners = [me.at(x=me.next_x(d)) for d in range(1, 4)]
    greeted = [partners[0], partners[2]] + far_partners + y_partners + x_partners
    barrier = pltpu.get_barrier_semaphore()
    for device in greeted:
        pl.semaphore_signal(barrier, inc=1, device_id=device, device_id_type=pl.DeviceIdType.MESH)

    loads[0].wait()
    transpose_book(book_ref, book_t)
    loads[1].wait()
    rebuild(codes_t, book_t, r3)
    loads[2].wait()
    split_queries(q_ref, q3)
    score(q3, r3, e_ref)
    docs = codes_t.shape[1]
    here = pos_ref[...].reshape(1, -1) - lax.axis_index("corpus") * docs
    as_column(here, pos_col)
    statistics(e_ref, pos_col, cols)
    stats_ref[...] = cols[...].T[:8]
    pl.semaphore_wait(barrier, len(greeted))

    mine = 2 * lax.rem(me.x, 2) + me.core
    near[mine] = stats_ref[...]
    copies = [wire.send(stats_ref, near.at[mine], device) for device in partners]
    expose(e_ref, pos_col, e2, hits)
    pull(hits, r3, pulled)
    for copy in copies:
        copy.wait_recv()
    far[me.z] = merge([near[k] for k in range(4)])
    copies = [wire.send(far.at[me.z], far.at[me.z], device) for device in far_partners]
    spread_out(e2, r3, spread)
    transpose_queries(q_ref, q_t)
    for copy in copies:
        copy.wait_recv()
    whole = merge([far[k] for k in range(8)])
    log_total = whole[0:1] + jnp.log(whole[1:2])
    loss_ref[...] = (log_total - whole[2:3]).reshape(-1)
    as_column(jnp.exp(stats_ref[0:1] - log_total), scale_col)

    query_gradient(spread, pulled, scale_col, part_q)
    half = part_q.shape[0] // 2
    chunk = half // 8
    q_core = wire.send(part_q.at[rows_at(other, half)], half_q, partners[0])
    weigh(e_ref, scale_col, pos_col, w3)
    document_gradient(w3, q_t, d_ref)
    q_core.wait_recv()
    sum_q[...] = part_q[rows_at(me.core, half)] + half_q[...]

    z_up, z_down = far_partners[0], far_partners[6]

    def ring_send(step):
        copies = []
        for buffers, ahead, steps, device in ((up, 4 - step, 4, z_up), (down, 8 - 3 + step, 3, z_down)):
            if step >= steps:
                continue
            at = rows_at(me.next_z(ahead), chunk)
            if step == 0:
                src = sum_q.at[at]
            else:
                src = buffers.at[step - 1]
                src[...] = src[...] + sum_q[at]
            copies.append(wire.send(src, buffers.at[step], device))
        return copies

    def arrive(copies):
        for copy in copies:
            copy.wait_recv()

    subs = codes_t.shape[0]
    groups = subs // 4
    base = other * (groups // 2)
    words, b_half = part_b.shape[0], part_b.shape[1] // 2

    ring = ring_send(0)
    collect(codes_t, d_ref, words_b, (0, groups // 2), base)
    transpose_half(words_b, other, part_b)
    b_core = wire.send(part_b.at[:, rows_at(other, b_half)], half_b, partners[0])
    arrive(ring)
    ring = ring_send(1)
    collect(codes_t, d_ref, words_b, (groups // 2, groups), base)
    transpose_half(words_b, me.core, part_b)
    arrive(ring)
    ring = ring_send(2)
    b_core.wait_recv()
    sum_b[...] = part_b[:, rows_at(me.core, b_half)] + half_b[...]

    lines = words // 8

    def lines_at(k, first, size, second=None):
        start = k * (words // 2) + first * lines
        if second is not None:
            start = start + second * size
        return pl.ds(pl.multiple_of(start, size), size)

    order = (
        ((me.y, me.next_y, y_partners), (me.x, me.next_x, x_partners)),
        ((me.x, me.next_x, x_partners), (me.y, me.next_y, y_partners)),
    )
    firsts = []
    for k in range(2):
        _, following, devices = order[k][0]
        for d in range(1, 4):
            firsts.append(
                wire.send(
                    sum_b.at[lines_at(k, following(d), lines)],
                    first_in.at[k, d - 1],
                    devices[d - 1],
                )
            )
    arrive(ring)
    ring = ring_send(3)
    arrive(firsts)
    seconds = []
    for k in range(2):
        index, _, _ = order[k][0]
        acc = sum_b[lines_at(k, index, lines)]
        for d in range(3):
            acc = acc + first_in[k, d]
        first_sum[k] = acc
        _, following, devices = order[k][1]
        for d in range(1, 4):
            seconds.append(
                wire.send(
                    first_sum.at[k, rows_at(following(d), lines // 4)],
                    second_in.at[k, d - 1],
                    devices[d - 1],
                )
            )

    arrive(ring)
    cross[0] = sum_q[rows_at(me.z, chunk)] + (up[3] + down[2])
    across = wire.send(cross.at[0], cross.at[1], partners[1])

    arrive(seconds)
    for k in range(2):
        index, _, _ = order[k][1]
        acc = first_sum[k, rows_at(index, lines // 4)]
        for d in range(3):
            acc = acc + second_in[k, d]
        last_in[me.z, k] = acc
    lasts = [wire.send(last_in.at[me.z], last_in.at[me.z], device) for device in far_partners]

    def q_rows(z):
        return pl.ds(pl.multiple_of(me.core * half + z * chunk, chunk), chunk)

    passed = []
    slices = 3
    size = chunk // slices

    def q_slice(z, k):
        return pl.ds(pl.multiple_of(me.core * half + z * chunk + k * size, size), size)

    def share(at, device):
        return wire.send(grad_q.at[at], grad_q.at[at], device)

    def pass_on(hop, k):
        copies = []
        for back_by, hops, device in ((8 - hop, 4, z_up), (hop, 3, z_down)):
            if hop < hops:
                copies.append(share(q_slice(me.next_z(back_by), k), device))
        return copies

    def to_core(hop, k):
        for ahead, hops in ((8 - hop - 1, 4), (hop + 1, 3)):
            if hop < hops:
                passed.append(share(q_slice(me.next_z(ahead), k), partners[0]))

    def next_hop(ring, hop):
        following = []
        for k in range(slices):
            arrive(ring[k])
            following.append(pass_on(hop, k) if hop < 4 else [])
            to_core(hop - 1, k)
        return following

    arrive([across])
    grad_q[q_rows(me.z)] = cross[0] + cross[1]
    ring = [pass_on(0, k) for k in range(slices)]
    passed.append(share(q_rows(me.z), partners[0]))

    columns = rows_at(me.core, b_half)

    def share_b(at, device):
        return wire.send(grad_b.at[at, columns], grad_b.at[at, columns], device)

    ring = next_hop(ring, 1)
    arrive(lasts)
    acc = last_in[0]
    for z in range(1, 8):
        acc = acc + last_in[z]
    seconds = []
    for k in range(2):
        at = lines_at(k, order[k][0][0], lines // 4, order[k][1][0])
        grad_b[at, columns] = acc[k]
        for device in order[k][1][2]:
            seconds.append(share_b(at, device))
    ring = next_hop(ring, 2)
    arrive(seconds)
    firsts = []
    for k in range(2):
        at = lines_at(k, order[k][0][0], lines)
        for device in order[k][0][2]:
            firsts.append(share_b(at, device))
    for k in range(2):
        passed.append(share_b(lines_at(k, order[k][0][0], lines), partners[0]))
    ring = next_hop(ring, 3)
    for d in (1, 3, 2):
        for k in range(2):
            arrive([firsts[3 * k + d - 1]])
            back = order[k][0][1](4 - d)
            passed.append(share_b(lines_at(k, back, lines), partners[0]))
    next_hop(ring, 4)
    arrive(passed)
    wire.finish()
    assert len(wire.copies) == COPIES, len(wire.copies)


def hand_over(*refs):
    copies = [pltpu.make_async_copy(refs[k], refs[3 + k], refs[6].at[k]) for k in range(3)]
    for copy in copies:
        copy.start()
    for copy in copies:
        copy.wait()


def local(queries, codes, positive, codebook):
    rows, width = queries.shape
    docs, subs = codes.shape
    words = codebook.shape[0]
    chunk = rows // 16
    lines = words // 8
    half = width // 2
    depth = 256 * pl.cdiv(3 * rows, 256)
    vmem = pl.BlockSpec(memory_space=pltpu.VMEM)
    hbm = pl.BlockSpec(memory_space=pltpu.HBM)
    grad_q, grad_b, loss = pl.pallas_call(
        step,
        in_specs=[hbm, hbm, vmem, hbm],
        out_specs=(vmem, vmem, vmem),
        out_shape=(
            jax.ShapeDtypeStruct((rows, width), F32),
            jax.ShapeDtypeStruct((words, width), F32),
            jax.ShapeDtypeStruct((rows,), F32),
        ),
        scratch_shapes=[
            pltpu.VMEM((rows, width), F32),
            pltpu.VMEM((subs, docs), I32),
            pltpu.VMEM((words, width), F32),
            pltpu.VMEM((width, words), F32),
            pltpu.VMEM((rows, 3 * width), BF16),
            pltpu.VMEM((3 * width, docs), BF16),
            pltpu.VMEM((width, depth), BF16),
            pltpu.VMEM((rows, docs), F32),
            pltpu.VMEM((8, rows), F32),
            pltpu.VMEM((rows, 128), F32),
            pltpu.VMEM((rows, 128), I32),
            pltpu.VMEM((rows, 128), F32),
            pltpu.VMEM((2 * rows, docs), BF16),
            pltpu.VMEM((rows, docs), BF16),
            pltpu.VMEM((rows, width), F32),
            pltpu.VMEM((rows, width), F32),
            pltpu.VMEM((depth, docs), BF16),
            pltpu.VMEM((width, docs), F32),
            pltpu.VMEM((4, 8, rows), F32),
            pltpu.VMEM((8, 8, rows), F32),
            pltpu.VMEM((rows, width), F32),
            pltpu.VMEM((rows // 2, width), F32),
            pltpu.VMEM((rows // 2, width), F32),
            pltpu.VMEM((4, chunk, width), F32),
            pltpu.VMEM((3, chunk, width), F32),
            pltpu.VMEM((2, chunk, width), F32),
            pltpu.VMEM((width, words), F32),
            pltpu.VMEM((words, width), F32),
            pltpu.VMEM((words, half), F32),
            pltpu.VMEM((words, half), F32),
            pltpu.VMEM((2, 3, lines, half), F32),
            pltpu.VMEM((2, lines, half), F32),
            pltpu.VMEM((2, 3, lines // 4, half), F32),
            pltpu.VMEM((2, lines // 4, half), F32),
            pltpu.VMEM((8, 2, lines // 4, half), F32),
            pltpu.SemaphoreType.DMA((COPIES,)),
            pltpu.SemaphoreType.DMA((COPIES,)),
            pltpu.SemaphoreType.DMA((3,)),
        ],
        compiler_params=pltpu.CompilerParams(
            collective_id=0, has_side_effects=True, vmem_limit_bytes=56 << 20
        ),
        name="step",
    )(queries, codes.T, positive, codebook)
    return pl.pallas_call(
        hand_over,
        in_specs=[vmem] * 3,
        out_specs=[hbm] * 3,
        out_shape=[jax.ShapeDtypeStruct(x.shape, F32) for x in (grad_q, grad_b, loss)],
        scratch_shapes=[pltpu.SemaphoreType.DMA((3,))],
        name="hand_over",
    )(grad_q, grad_b, loss)


def solution(mesh):
    return jax.shard_map(
        local,
        mesh=mesh,
        in_specs=(P("query", None), P("corpus", None), P("query"), P()),
        out_specs=(P("query", None), P(), P("query")),
        check_vma=False,
    )
```

```python
import jax
import jax.numpy as jnp
from jax import lax
from jax.experimental import pallas as pl
from jax.experimental.pallas import tpu as pltpu
from jax.sharding import PartitionSpec as P

F32, BF16, I32 = jnp.float32, jnp.bfloat16, jnp.int32
NN = (((1,), (0,)), ((), ()))
NT = (((1,), (1,)), ((), ()))
HIGH_CODES = 64
LOW_CODES = 4
COPIES = 142


def dot(a, b, dims=NN):
    return lax.dot_general(a, b, dims, preferred_element_type=F32)


def split(x):
    high = x.astype(BF16)
    return high, (x - high.astype(F32)).astype(BF16)


def split3(x):
    high = x.astype(BF16)
    rest = x - high.astype(F32)
    mid = rest.astype(BF16)
    return high, mid, (rest - mid.astype(F32)).astype(BF16)


def split_queries(q_ref, q3, step=32):
    width = q_ref.shape[1]

    def block(b, _):
        at = pl.ds(pl.multiple_of(b * step, step), step)
        high, mid, low = split3(q_ref[at, :])
        q3[at, :width] = high
        q3[at, width : 2 * width] = mid
        q3[at, 2 * width :] = low
        return 0

    lax.fori_loop(0, q_ref.shape[0] // step, block, 0)


def transpose_queries(q_ref, q_t, step=128):
    rows = q_ref.shape[0]

    def block(b, _):
        at = pl.ds(pl.multiple_of(b * step, step), step)
        high, mid = split(q_ref[:, at].T)
        q_t[at, :rows] = high
        q_t[at, rows : 2 * rows] = mid
        q_t[at, 2 * rows : 3 * rows] = high
        q_t[at, 3 * rows :] = jnp.zeros((step, q_t.shape[1] - 3 * rows), BF16)
        return 0

    lax.fori_loop(0, q_ref.shape[1] // step, block, 0)


def transpose_book(book_ref, book_t, step=128):
    def block(b, _):
        at = pl.ds(pl.multiple_of(b * step, step), step)
        book_t[at, :] = book_ref[:, at].T
        return 0

    lax.fori_loop(0, book_ref.shape[1] // step, block, 0)


def rebuild(codes_t, book_t, r3, unroll=4):
    subs, docs = codes_t.shape
    width = book_t.shape[0]
    sub_width = width // subs

    def pair(p):
        parts = []
        for side in range(2):
            m = 2 * p + side
            base = pl.multiple_of(m * sub_width, sub_width)
            low = book_t[pl.ds(base, sub_width), :128]
            high = book_t[pl.ds(base, sub_width), 128:]
            code = codes_t[pl.ds(m, 1), :]
            tiles = []
            for t in range(docs // 128):
                picked = jnp.broadcast_to(code[:, 128 * t : 128 * t + 128], (sub_width, 128))
                lane = picked & 127
                a = jnp.take_along_axis(low, lane, axis=1, mode="promise_in_bounds")
                b = jnp.take_along_axis(high, lane, axis=1, mode="promise_in_bounds")
                tiles.append(jnp.where(picked < 128, a, b))
            parts.append(jnp.concatenate(tiles, axis=1))
        high, mid, low = split3(jnp.concatenate(parts, axis=0))
        at = pl.multiple_of(2 * p * sub_width, 2 * sub_width)
        r3[pl.ds(at, 2 * sub_width), :] = low
        r3[pl.ds(width + at, 2 * sub_width), :] = mid
        r3[pl.ds(2 * width + at, 2 * sub_width), :] = high

    def block(b, _):
        for u in range(unroll):
            pair(unroll * b + u)
        return 0

    lax.fori_loop(0, subs // 2 // unroll, block, 0)


def score(q3, r3, s_ref, tile=512):
    width = q3.shape[1] // 3

    def block(t, _):
        at = pl.ds(pl.multiple_of(t * tile, tile), tile)
        acc = dot(q3[...], r3[:, at])
        acc = acc + dot(q3[:, : 2 * width], r3[width:, at])
        s_ref[:, at] = acc + dot(q3[:, :width], r3[2 * width :, at])
        return 0

    lax.fori_loop(0, s_ref.shape[1] // tile, block, 0)


def statistics(s_ref, pos_col, cols, e2, hits, step=64):
    rows, docs = s_ref.shape
    lane = lax.broadcasted_iota(I32, (step, 128), 1)
    ids = lax.broadcasted_iota(I32, (step, docs), 1)

    def block(b, _):
        at = pl.ds(pl.multiple_of(b * step, step), step)
        s = s_ref[at, :]
        top = jnp.max(s, axis=1, keepdims=True)
        hit = pos_col[at, :1] == ids
        own = jnp.sum(jnp.where(hit, s, 0.0), axis=1, keepdims=True)
        hits[at, :] = jnp.where(hit, 1.0, 0.0).astype(BF16)
        e = jnp.exp(s - top)
        total = jnp.sum(e, axis=1, keepdims=True)
        s_ref[at, :] = e
        high, low = split(e)
        e2[at, :] = low
        e2[pl.ds(pl.multiple_of(rows + b * step, step), step), :] = high
        cols[at, :] = jnp.where(
            lane == 0, top, jnp.where(lane == 1, total, jnp.where(lane == 2, own, 0.0))
        )
        return 0

    lax.fori_loop(0, rows // step, block, 0)


def as_column(row, column):
    column[...] = jnp.broadcast_to(row, (128, row.shape[1])).T


def pull(hits, r3, pulled, tile=256):
    width = r3.shape[0] // 3

    def block(t, _):
        base = pl.multiple_of(t * tile, tile)
        acc = dot(hits[...], r3[pl.ds(width + base, tile), :], NT)
        pulled[:, pl.ds(base, tile)] = acc + dot(hits[...], r3[pl.ds(2 * width + base, tile), :], NT)
        return 0

    lax.fori_loop(0, width // tile, block, 0)


def spread_out(e2, r3, spread, tile=256):
    rows = e2.shape[0] // 2
    width = r3.shape[0] // 3

    def block(t, _):
        base = pl.multiple_of(t * tile, tile)
        mid = r3[pl.ds(width + base, tile), :]
        high = r3[pl.ds(2 * width + base, tile), :]
        acc = dot(e2[rows:, :], mid, NT)
        acc = acc + dot(e2[:rows, :], high, NT)
        spread[:, pl.ds(base, tile)] = acc + dot(e2[rows:, :], high, NT)
        return 0

    lax.fori_loop(0, width // tile, block, 0)


def query_gradient(spread, pulled, scale_col, out, step=32):
    def block(b, _):
        at = pl.ds(pl.multiple_of(b * step, step), step)
        out[at, :] = spread[at, :] * scale_col[at, :1] - pulled[at, :]
        return 0

    lax.fori_loop(0, spread.shape[0] // step, block, 0)


def weigh(e_ref, scale_col, pos_col, w3, step=32):
    rows, docs = e_ref.shape
    w3[3 * rows :, :] = jnp.zeros((w3.shape[0] - 3 * rows, docs), BF16)
    ids = lax.broadcasted_iota(I32, (step, docs), 1)

    def block(b, _):
        at = pl.ds(pl.multiple_of(b * step, step), step)
        w = e_ref[at, :] * scale_col[at, :1]
        w = w - jnp.where(pos_col[at, :1] == ids, 1.0, 0.0)
        high, low = split(w)
        w3[at, :] = low
        w3[pl.ds(pl.multiple_of(rows + b * step, step), step), :] = high
        w3[pl.ds(pl.multiple_of(2 * rows + b * step, step), step), :] = high
        return 0

    lax.fori_loop(0, rows // step, block, 0)


def document_gradient(w3, q_t, out, tile=256):
    for t in range(out.shape[1] // tile):
        at = slice(t * tile, t * tile + tile)
        out[:, at] = dot(q_t[...], w3[:, at])


def collect(codes_t, d_ref, out, base, count, group=4):
    subs, docs = codes_t.shape
    sub_width = d_ref.shape[0] // subs
    word = lax.broadcasted_iota(I32, (HIGH_CODES, docs), 0)
    lane = lax.broadcasted_iota(I32, (sub_width, 128), 1)

    def one(b):
        g = b + base
        tables, values = [], []
        for s in range(group):
            m = group * g + s
            code = codes_t[pl.ds(m, 1), :]
            inner = code & (HIGH_CODES - 1)
            outer = jnp.broadcast_to(code >> 6, (sub_width, docs))
            tables.append(jnp.where(word == inner, 1.0, 0.0).astype(BF16))
            d = d_ref[pl.ds(pl.multiple_of(m * sub_width, sub_width), sub_width), :]
            high = d.astype(BF16).astype(F32)
            low = d - high
            masks = [outer == k for k in range(LOW_CODES)]
            rows = [jnp.where(mask, part, 0.0) for part in (high, low) for mask in masks]
            values.append(jnp.concatenate(rows, axis=0).astype(BF16))
        found = dot(jnp.concatenate(values, axis=0), jnp.concatenate(tables, axis=0), NT)
        rows = 2 * LOW_CODES * sub_width
        for s in range(group):
            at = 128 * (s // 2)
            piece = found[rows * s : rows * (s + 1), at : at + 128]
            piece = piece[: rows // 2] + piece[rows // 2 :]
            parts = [piece[sub_width * k : sub_width * (k + 1)] for k in range(LOW_CODES)]
            start = pl.multiple_of((group * g + s) * sub_width, sub_width)
            for k in range(2):
                first, second = parts[2 * k], parts[2 * k + 1]
                if s % 2:
                    first = pltpu.roll(first, 64, 1)
                else:
                    second = pltpu.roll(second, 64, 1)
                out[pl.ds(start, sub_width), 128 * k : 128 * k + 128] = jnp.where(
                    lane < 64, first, second
                )

    for b in range(count):
        one(b)


def transpose_run(part, base, count, out, step=128):
    def block(b, _):
        at = pl.ds(pl.multiple_of(base + b * step, step), step)
        out[:, at] = part[at, :].T
        return 0

    lax.fori_loop(0, count // step, block, 0)


class Place:
    def __init__(self):
        query, corpus = lax.axis_index("query"), lax.axis_index("corpus")
        self.y = lax.rem(query, 4)
        self.x = 2 * lax.div(query, 4) + lax.rem(lax.div(corpus, 2), 2)
        self.z = lax.div(corpus, 4)
        self.core = lax.rem(corpus, 2)

    def at(self, x=None, y=None, z=None, core=None):
        x = self.x if x is None else x
        y = self.y if y is None else y
        z = self.z if z is None else z
        core = self.core if core is None else core
        return (4 * lax.div(x, 2) + y, 4 * z + 2 * lax.rem(x, 2) + core)

    def next_y(self, d):
        return lax.rem(self.y + d, 4)

    def next_x(self, d):
        return lax.rem(self.x + d, 4)

    def next_z(self, d):
        return lax.rem(self.z + d, 8)


class Wire:
    def __init__(self, sent, arrived):
        self.sent, self.arrived, self.copies = sent, arrived, []
        self.settled, self.mark = 0, 0

    def send(self, src, dst, device):
        i = len(self.copies)
        copy = pltpu.make_async_remote_copy(
            src_ref=src,
            dst_ref=dst,
            send_sem=self.sent.at[i],
            recv_sem=self.arrived.at[i],
            device_id=device,
            device_id_type=pl.DeviceIdType.MESH,
        )
        copy.start()
        self.copies.append(copy)
        return copy

    def settle(self):
        for copy in self.copies[self.settled : self.mark]:
            copy.wait_send()
        self.settled, self.mark = self.mark, len(self.copies)

    def finish(self):
        for copy in self.copies[self.settled :]:
            copy.wait_send()


def rows_at(index, size):
    return pl.ds(pl.multiple_of(index * size, size), size)


def merge(stats):
    top = stats[0][0:1]
    for s in stats[1:]:
        top = jnp.maximum(top, s[0:1])
    total = sum(s[1:2] * jnp.exp(s[0:1] - top) for s in stats)
    own = sum(s[2:3] for s in stats)
    pad = jnp.zeros((8 - 3, top.shape[1]), F32)
    return jnp.concatenate([top, total, own, pad], axis=0)


def step(
    q_hbm, codes_hbm, pos_ref, book_hbm,
    grad_q, grad_b, loss_ref,
    q_ref, codes_t, book_ref, book_t, q3, r3, q_t, e_ref, stats_ref, cols,
    pos_col, scale_col, e2, hits, spread, pulled, w3, d_ref,
    near, far, part_q, half_q, sum_q, up, down, cross,
    words_b, part_b, half_b, sum_b, first_in, first_sum, second_in, second_sum, last_in,
    sent, arrived, loaded,
):
    loads = [
        pltpu.make_async_copy(book_hbm, book_ref, loaded.at[0]),
        pltpu.make_async_copy(codes_hbm, codes_t, loaded.at[1]),
        pltpu.make_async_copy(q_hbm, q_ref, loaded.at[2]),
    ]
    for load in loads:
        load.start()
    me = Place()
    wire = Wire(sent, arrived)
    x_pair = me.x + 1 - 2 * lax.rem(me.x, 2)
    other = 1 - me.core
    partners = [me.at(core=other), me.at(x=x_pair), me.at(x=x_pair, core=other)]
    far_partners = [me.at(z=me.next_z(d)) for d in range(1, 8)]
    y_partners = [me.at(y=me.next_y(d)) for d in range(1, 4)]
    x_partners = [me.at(x=me.next_x(d)) for d in range(1, 4)]
    greeted = [partners[0], partners[2]] + far_partners + y_partners + x_partners
    barrier = pltpu.get_barrier_semaphore()
    for device in greeted:
        pl.semaphore_signal(barrier, inc=1, device_id=device, device_id_type=pl.DeviceIdType.MESH)

    loads[0].wait()
    transpose_book(book_ref, book_t)
    loads[1].wait()
    rebuild(codes_t, book_t, r3)
    loads[2].wait()
    split_queries(q_ref, q3)
    score(q3, r3, e_ref)
    docs = codes_t.shape[1]
    here = pos_ref[...].reshape(1, -1) - lax.axis_index("corpus") * docs
    as_column(here, pos_col)
    statistics(e_ref, pos_col, cols, e2, hits)
    stats_ref[...] = cols[...].T[:8]
    pl.semaphore_wait(barrier, len(greeted))

    mine = 2 * lax.rem(me.x, 2) + me.core
    near[mine] = stats_ref[...]
    copies = [wire.send(stats_ref, near.at[mine], device) for device in partners]
    pull(hits, r3, pulled)
    for copy in copies:
        copy.wait_recv()
    far[me.z] = merge([near[k] for k in range(4)])
    copies = [wire.send(far.at[me.z], far.at[me.z], device) for device in far_partners]
    spread_out(e2, r3, spread)
    transpose_queries(q_ref, q_t)
    for copy in copies:
        copy.wait_recv()
    whole = merge([far[k] for k in range(8)])
    log_total = whole[0:1] + jnp.log(whole[1:2])
    loss_ref[...] = (log_total - whole[2:3]).reshape(-1)
    as_column(jnp.exp(stats_ref[0:1] - log_total), scale_col)

    query_gradient(spread, pulled, scale_col, part_q)
    half = part_q.shape[0] // 2
    chunk = half // 8
    q_core = wire.send(part_q.at[rows_at(other, half)], half_q, partners[0])
    weigh(e_ref, scale_col, pos_col, w3)
    document_gradient(w3, q_t, d_ref)
    q_core.wait_recv()
    sum_q[...] = part_q[rows_at(me.core, half)] + half_q[...]

    z_up, z_down = far_partners[0], far_partners[6]

    def ring_send(step):
        copies = []
        for buffers, ahead, steps, device in ((up, 4 - step, 4, z_up), (down, 8 - 3 + step, 3, z_down)):
            if step >= steps:
                continue
            at = rows_at(me.next_z(ahead), chunk)
            if step == 0:
                src = sum_q.at[at]
            else:
                src = buffers.at[step - 1]
                src[...] = src[...] + sum_q[at]
            copies.append(wire.send(src, buffers.at[step], device))
        return copies

    def arrive(copies):
        for copy in copies:
            copy.wait_recv()

    words, b_half = part_b.shape[0], part_b.shape[1] // 2
    lines = words // 8
    group_width = 4 * d_ref.shape[0] // codes_t.shape[0]

    def lines_at(k, first, size, second=None):
        start = k * (words // 2) + first * lines
        if second is not None:
            start = start + second * size
        return pl.ds(pl.multiple_of(start, size), size)

    order = (
        ((me.y, me.next_y, y_partners), (me.x, me.next_x, x_partners)),
        ((me.x, me.next_x, x_partners), (me.y, me.next_y, y_partners)),
    )
    passed, taken = [], [0, 0]

    def greet_passed():
        arrive(passed[taken[0] : taken[1]])
        taken[:] = taken[1], len(passed)

    def gather_words(core, part):
        offset, count = part
        base = core * b_half + offset
        collect(codes_t, d_ref, words_b, core * (b_half // group_width) + offset // group_width, count // group_width)
        transpose_run(words_b, base, count, part_b)

    def book_chain(part):
        offset, count = part
        inner = slice(offset, offset + count)
        theirs = pl.ds(pl.multiple_of(other * b_half + offset, 128), count)
        ours = pl.ds(pl.multiple_of(me.core * b_half + offset, 128), count)
        core = wire.send(part_b.at[:, theirs], half_b.at[:, inner], partners[0])
        yield
        core.wait_recv()
        sum_b[:, inner] = part_b[:, ours] + half_b[:, inner]
        firsts = []
        for k in range(2):
            _, following, devices = order[k][0]
            for d in range(1, 4):
                firsts.append(
                    wire.send(
                        sum_b.at[lines_at(k, following(d), lines), inner],
                        first_in.at[k, d - 1, :, inner],
                        devices[d - 1],
                    )
                )
        yield
        arrive(firsts)
        seconds = []
        for k in range(2):
            index, _, _ = order[k][0]
            acc = sum_b[lines_at(k, index, lines), inner]
            for d in range(3):
                acc = acc + first_in[k, d, :, inner]
            first_sum[k, :, inner] = acc
            _, following, devices = order[k][1]
            for d in range(1, 4):
                seconds.append(
                    wire.send(
                        first_sum.at[k, rows_at(following(d), lines // 4), inner],
                        second_in.at[k, d - 1, :, inner],
                        devices[d - 1],
                    )
                )
        yield
        arrive(seconds)
        for k in range(2):
            index, _, _ = order[k][1]
            acc = first_sum[k, rows_at(index, lines // 4), inner]
            for d in range(3):
                acc = acc + second_in[k, d, :, inner]
            last_in[me.z, k, :, inner] = acc
        mine = last_in.at[me.z, :, :, inner]
        lasts = [wire.send(mine, mine, device) for device in far_partners]
        yield
        arrive(lasts)
        acc = last_in[0, :, :, inner]
        for z in range(1, 8):
            acc = acc + last_in[z, :, :, inner]

        def share_b(at, device):
            return wire.send(grad_b.at[at, ours], grad_b.at[at, ours], device)

        seconds = []
        for k in range(2):
            at = lines_at(k, order[k][0][0], lines // 4, order[k][1][0])
            grad_b[at, ours] = acc[k]
            for device in order[k][1][2]:
                seconds.append(share_b(at, device))
        yield
        arrive(seconds)
        firsts = []
        for k in range(2):
            at = lines_at(k, order[k][0][0], lines)
            for device in order[k][0][2]:
                firsts.append(share_b(at, device))
        for k in range(2):
            passed.append(share_b(lines_at(k, order[k][0][0], lines), partners[0]))
        yield
        for d in (1, 3, 2):
            for k in range(2):
                arrive([firsts[3 * k + d - 1]])
                back = order[k][0][1](4 - d)
                passed.append(share_b(lines_at(k, back, lines), partners[0]))
        yield

    def q_rows(z):
        return pl.ds(pl.multiple_of(me.core * half + z * chunk, chunk), chunk)

    slices = 3
    size = chunk // slices

    def q_slice(z, k):
        return pl.ds(pl.multiple_of(me.core * half + z * chunk + k * size, size), size)

    def share(at, device):
        return wire.send(grad_q.at[at], grad_q.at[at], device)

    def pass_on(hop, k):
        copies = []
        for back_by, hops, device in ((8 - hop, 4, z_up), (hop, 3, z_down)):
            if hop < hops:
                copies.append(share(q_slice(me.next_z(back_by), k), device))
        return copies

    def query_chain():
        ring = ring_send(0)
        for step in range(1, 4):
            yield
            arrive(ring)
            ring = ring_send(step)
        yield
        arrive(ring)
        cross[0] = sum_q[rows_at(me.z, chunk)] + (up[3] + down[2])
        across = wire.send(cross.at[0], cross.at[1], partners[1])
        yield
        arrive([across])
        grad_q[q_rows(me.z)] = cross[0] + cross[1]
        ring = [pass_on(0, k) for k in range(slices)]
        passed.append(share(q_rows(me.z), partners[0]))
        for hop in range(1, 5):
            yield
            following = []
            for k in range(slices):
                arrive(ring[k])
                following.append(pass_on(hop, k) if hop < 4 else [])
                for ahead, hops in ((8 - hop, 4), (hop, 3)):
                    if hop - 1 < hops:
                        passed.append(share(q_slice(me.next_z(ahead), k), partners[0]))
            ring = following
        yield

    large, small = (0, 2 * b_half // 3), (2 * b_half // 3, b_half // 3)
    queries = query_chain()
    next(queries)
    gather_words(other, large)
    first = book_chain(large)
    next(first)
    next(queries)
    gather_words(me.core, large)
    next(first)
    next(queries)
    gather_words(other, small)
    second = book_chain(small)
    next(second)
    gather_words(me.core, small)
    next(second)
    next(queries)
    wire.settle()
    next(first)
    next(second)
    wire.settle()
    next(first)
    next(queries)
    next(second)
    next(queries)
    wire.settle()
    next(first)
    next(queries)
    wire.settle()
    greet_passed()
    next(second)
    next(first)
    next(queries)
    wire.settle()
    greet_passed()
    next(second)
    next(first)
    next(queries)
    wire.settle()
    greet_passed()
    next(second)
    next(queries)
    arrive(passed[taken[0] :])
    wire.finish()
    assert len(wire.copies) == COPIES, len(wire.copies)


def hand_over(*refs):
    inside, outside = refs[9], refs[10]
    steps = []
    for k in range(3):
        src, dst, held = refs[k], refs[3 + k], refs[6 + k]
        pieces = 4 if len(src.shape) > 1 else 1
        size = src.shape[0] // pieces
        for n in range(pieces):
            at = pl.ds(n * size, size)
            i = len(steps)
            steps.append(
                (
                    pltpu.make_async_copy(src.at[at], held.at[at], inside.at[i]),
                    pltpu.make_async_copy(held.at[at], dst.at[at], outside.at[i]),
                )
            )
    for load, _ in steps:
        load.start()
    for load, store in steps:
        load.wait()
        store.start()
    for _, store in steps:
        store.wait()


def local(queries, codes, positive, codebook):
    rows, width = queries.shape
    docs, subs = codes.shape
    words = codebook.shape[0]
    chunk = rows // 16
    lines = words // 8
    half = width // 2
    depth = 256 * pl.cdiv(3 * rows, 256)
    vmem = pl.BlockSpec(memory_space=pltpu.VMEM)
    hbm = pl.BlockSpec(memory_space=pltpu.HBM)
    grad_q, grad_b, loss = pl.pallas_call(
        step,
        in_specs=[hbm, hbm, vmem, hbm],
        out_specs=(vmem, vmem, vmem),
        out_shape=(
            jax.ShapeDtypeStruct((rows, width), F32),
            jax.ShapeDtypeStruct((words, width), F32),
            jax.ShapeDtypeStruct((rows,), F32),
        ),
        scratch_shapes=[
            pltpu.VMEM((rows, width), F32),
            pltpu.VMEM((subs, docs), I32),
            pltpu.VMEM((words, width), F32),
            pltpu.VMEM((width, words), F32),
            pltpu.VMEM((rows, 3 * width), BF16),
            pltpu.VMEM((3 * width, docs), BF16),
            pltpu.VMEM((width, depth), BF16),
            pltpu.VMEM((rows, docs), F32),
            pltpu.VMEM((8, rows), F32),
            pltpu.VMEM((rows, 128), F32),
            pltpu.VMEM((rows, 128), I32),
            pltpu.VMEM((rows, 128), F32),
            pltpu.VMEM((2 * rows, docs), BF16),
            pltpu.VMEM((rows, docs), BF16),
            pltpu.VMEM((rows, width), F32),
            pltpu.VMEM((rows, width), F32),
            pltpu.VMEM((depth, docs), BF16),
            pltpu.VMEM((width, docs), F32),
            pltpu.VMEM((4, 8, rows), F32),
            pltpu.VMEM((8, 8, rows), F32),
            pltpu.VMEM((rows, width), F32),
            pltpu.VMEM((rows // 2, width), F32),
            pltpu.VMEM((rows // 2, width), F32),
            pltpu.VMEM((4, chunk, width), F32),
            pltpu.VMEM((3, chunk, width), F32),
            pltpu.VMEM((2, chunk, width), F32),
            pltpu.VMEM((width, words), F32),
            pltpu.VMEM((words, width), F32),
            pltpu.VMEM((words, half), F32),
            pltpu.VMEM((words, half), F32),
            pltpu.VMEM((2, 3, lines, half), F32),
            pltpu.VMEM((2, lines, half), F32),
            pltpu.VMEM((2, 3, lines // 4, half), F32),
            pltpu.VMEM((2, lines // 4, half), F32),
            pltpu.VMEM((8, 2, lines // 4, half), F32),
            pltpu.SemaphoreType.DMA((COPIES,)),
            pltpu.SemaphoreType.DMA((COPIES,)),
            pltpu.SemaphoreType.DMA((3,)),
        ],
        compiler_params=pltpu.CompilerParams(
            collective_id=0, has_side_effects=True, vmem_limit_bytes=56 << 20
        ),
        name="step",
    )(queries, codes.T, positive, codebook)
    return pl.pallas_call(
        hand_over,
        in_specs=[hbm] * 3,
        out_specs=[hbm] * 3,
        out_shape=[jax.ShapeDtypeStruct(x.shape, F32) for x in (grad_q, grad_b, loss)],
        scratch_shapes=[
            *(pltpu.VMEM(x.shape, F32) for x in (grad_q, grad_b, loss)),
            pltpu.SemaphoreType.DMA((9,)),
            pltpu.SemaphoreType.DMA((9,)),
        ],
        name="hand_over",
    )(grad_q, grad_b, loss)


def solution(mesh):
    return jax.shard_map(
        local,
        mesh=mesh,
        in_specs=(P("query", None), P("corpus", None), P("query"), P()),
        out_specs=(P("query", None), P(), P("query")),
        check_vma=False,
    )
```

```python
import jax
import jax.numpy as jnp
from jax import lax
from jax.experimental import pallas as pl
from jax.experimental.pallas import tpu as pltpu
from jax.sharding import PartitionSpec as P

F32, BF16, I32 = jnp.float32, jnp.bfloat16, jnp.int32
NN = (((1,), (0,)), ((), ()))
NT = (((1,), (1,)), ((), ()))
HIGH_CODES = 64
LOW_CODES = 4
COPIES = 114


def dot(a, b, dims=NN):
    return lax.dot_general(a, b, dims, preferred_element_type=F32)


def split(x):
    high = x.astype(BF16)
    return high, (x - high.astype(F32)).astype(BF16)


def split3(x):
    high = x.astype(BF16)
    rest = x - high.astype(F32)
    mid = rest.astype(BF16)
    return high, mid, (rest - mid.astype(F32)).astype(BF16)


def split_queries(q_ref, q3, step=32):
    width = q_ref.shape[1]

    def block(b, _):
        at = pl.ds(pl.multiple_of(b * step, step), step)
        high, mid, low = split3(q_ref[at, :])
        q3[at, :width] = high
        q3[at, width : 2 * width] = mid
        q3[at, 2 * width :] = low
        return 0

    lax.fori_loop(0, q_ref.shape[0] // step, block, 0)


def transpose_queries(q_ref, q_t, step=128):
    rows = q_ref.shape[0]

    def block(b, _):
        at = pl.ds(pl.multiple_of(b * step, step), step)
        high, mid = split(q_ref[:, at].T)
        q_t[at, :rows] = high
        q_t[at, rows : 2 * rows] = mid
        q_t[at, 2 * rows : 3 * rows] = high
        q_t[at, 3 * rows :] = jnp.zeros((step, q_t.shape[1] - 3 * rows), BF16)
        return 0

    lax.fori_loop(0, q_ref.shape[1] // step, block, 0)


def transpose_book(book_ref, book_t, step=128):
    def block(b, _):
        at = pl.ds(pl.multiple_of(b * step, step), step)
        book_t[at, :] = book_ref[:, at].T
        return 0

    lax.fori_loop(0, book_ref.shape[1] // step, block, 0)


def rebuild(codes_t, book_t, r3, unroll=4):
    subs, docs = codes_t.shape
    width = book_t.shape[0]
    sub_width = width // subs

    def pair(p):
        parts = []
        for side in range(2):
            m = 2 * p + side
            base = pl.multiple_of(m * sub_width, sub_width)
            low = book_t[pl.ds(base, sub_width), :128]
            high = book_t[pl.ds(base, sub_width), 128:]
            code = codes_t[pl.ds(m, 1), :]
            tiles = []
            for t in range(docs // 128):
                picked = jnp.broadcast_to(code[:, 128 * t : 128 * t + 128], (sub_width, 128))
                lane = picked & 127
                a = jnp.take_along_axis(low, lane, axis=1, mode="promise_in_bounds")
                b = jnp.take_along_axis(high, lane, axis=1, mode="promise_in_bounds")
                tiles.append(jnp.where(picked < 128, a, b))
            parts.append(jnp.concatenate(tiles, axis=1))
        high, mid, low = split3(jnp.concatenate(parts, axis=0))
        at = pl.multiple_of(2 * p * sub_width, 2 * sub_width)
        r3[pl.ds(at, 2 * sub_width), :] = low
        r3[pl.ds(width + at, 2 * sub_width), :] = mid
        r3[pl.ds(2 * width + at, 2 * sub_width), :] = high

    def block(b, _):
        for u in range(unroll):
            pair(unroll * b + u)
        return 0

    lax.fori_loop(0, subs // 2 // unroll, block, 0)


def score(q3, r3, s_ref, tile=512):
    width = q3.shape[1] // 3

    def block(t, _):
        at = pl.ds(pl.multiple_of(t * tile, tile), tile)
        acc = dot(q3[...], r3[:, at])
        acc = acc + dot(q3[:, : 2 * width], r3[width:, at])
        s_ref[:, at] = acc + dot(q3[:, :width], r3[2 * width :, at])
        return 0

    lax.fori_loop(0, s_ref.shape[1] // tile, block, 0)


def statistics(s_ref, pos_col, cols, e2, hits, step=64):
    rows, docs = s_ref.shape
    lane = lax.broadcasted_iota(I32, (step, 128), 1)
    ids = lax.broadcasted_iota(I32, (step, docs), 1)

    def block(b, _):
        at = pl.ds(pl.multiple_of(b * step, step), step)
        s = s_ref[at, :]
        top = jnp.max(s, axis=1, keepdims=True)
        hit = pos_col[at, :1] == ids
        own = jnp.sum(jnp.where(hit, s, 0.0), axis=1, keepdims=True)
        hits[at, :] = jnp.where(hit, 1.0, 0.0).astype(BF16)
        e = jnp.exp(s - top)
        total = jnp.sum(e, axis=1, keepdims=True)
        s_ref[at, :] = e
        high, low = split(e)
        e2[at, :] = low
        e2[pl.ds(pl.multiple_of(rows + b * step, step), step), :] = high
        cols[at, :] = jnp.where(
            lane == 0, top, jnp.where(lane == 1, total, jnp.where(lane == 2, own, 0.0))
        )
        return 0

    lax.fori_loop(0, rows // step, block, 0)


def as_column(row, column):
    column[...] = jnp.broadcast_to(row, (128, row.shape[1])).T


def pull(hits, r3, pulled, tile=256):
    width = r3.shape[0] // 3

    def block(t, _):
        base = pl.multiple_of(t * tile, tile)
        acc = dot(hits[...], r3[pl.ds(width + base, tile), :], NT)
        pulled[:, pl.ds(base, tile)] = acc + dot(hits[...], r3[pl.ds(2 * width + base, tile), :], NT)
        return 0

    lax.fori_loop(0, width // tile, block, 0)


def spread_out(e2, r3, spread, tile=256):
    rows = e2.shape[0] // 2
    width = r3.shape[0] // 3

    def block(t, _):
        base = pl.multiple_of(t * tile, tile)
        mid = r3[pl.ds(width + base, tile), :]
        high = r3[pl.ds(2 * width + base, tile), :]
        acc = dot(e2[rows:, :], mid, NT)
        acc = acc + dot(e2[:rows, :], high, NT)
        spread[:, pl.ds(base, tile)] = acc + dot(e2[rows:, :], high, NT)
        return 0

    lax.fori_loop(0, width // tile, block, 0)


def query_gradient(spread, pulled, scale_col, out, step=32):
    def block(b, _):
        at = pl.ds(pl.multiple_of(b * step, step), step)
        out[at, :] = spread[at, :] * scale_col[at, :1] - pulled[at, :]
        return 0

    lax.fori_loop(0, spread.shape[0] // step, block, 0)


def weigh(e_ref, scale_col, pos_col, w3, step=32):
    rows, docs = e_ref.shape
    w3[3 * rows :, :] = jnp.zeros((w3.shape[0] - 3 * rows, docs), BF16)
    ids = lax.broadcasted_iota(I32, (step, docs), 1)

    def block(b, _):
        at = pl.ds(pl.multiple_of(b * step, step), step)
        w = e_ref[at, :] * scale_col[at, :1]
        w = w - jnp.where(pos_col[at, :1] == ids, 1.0, 0.0)
        high, low = split(w)
        w3[at, :] = low
        w3[pl.ds(pl.multiple_of(rows + b * step, step), step), :] = high
        w3[pl.ds(pl.multiple_of(2 * rows + b * step, step), step), :] = high
        return 0

    lax.fori_loop(0, rows // step, block, 0)


def document_gradient(w3, q_t, out, tile=256):
    for t in range(out.shape[1] // tile):
        at = slice(t * tile, t * tile + tile)
        out[:, at] = dot(q_t[...], w3[:, at])


def collect(codes_t, d_ref, out, base, count, group=4):
    subs, docs = codes_t.shape
    sub_width = d_ref.shape[0] // subs
    word = lax.broadcasted_iota(I32, (HIGH_CODES, docs), 0)
    lane = lax.broadcasted_iota(I32, (sub_width, 128), 1)

    def one(b):
        g = b + base
        tables, values = [], []
        for s in range(group):
            m = group * g + s
            code = codes_t[pl.ds(m, 1), :]
            inner = code & (HIGH_CODES - 1)
            outer = jnp.broadcast_to(code >> 6, (sub_width, docs))
            tables.append(jnp.where(word == inner, 1.0, 0.0).astype(BF16))
            d = d_ref[pl.ds(pl.multiple_of(m * sub_width, sub_width), sub_width), :]
            high = d.astype(BF16).astype(F32)
            low = d - high
            masks = [outer == k for k in range(LOW_CODES)]
            rows = [jnp.where(mask, part, 0.0) for part in (high, low) for mask in masks]
            values.append(jnp.concatenate(rows, axis=0).astype(BF16))
        found = dot(jnp.concatenate(values, axis=0), jnp.concatenate(tables, axis=0), NT)
        rows = 2 * LOW_CODES * sub_width
        for s in range(group):
            at = 128 * (s // 2)
            piece = found[rows * s : rows * (s + 1), at : at + 128]
            piece = piece[: rows // 2] + piece[rows // 2 :]
            parts = [piece[sub_width * k : sub_width * (k + 1)] for k in range(LOW_CODES)]
            start = pl.multiple_of((group * g + s) * sub_width, sub_width)
            for k in range(2):
                first, second = parts[2 * k], parts[2 * k + 1]
                if s % 2:
                    first = pltpu.roll(first, 64, 1)
                else:
                    second = pltpu.roll(second, 64, 1)
                out[pl.ds(start, sub_width), 128 * k : 128 * k + 128] = jnp.where(
                    lane < 64, first, second
                )

    for b in range(count):
        one(b)


def transpose_run(part, base, count, out, step=128):
    def block(b, _):
        at = pl.ds(pl.multiple_of(base + b * step, step), step)
        out[:, at] = part[at, :].T
        return 0

    lax.fori_loop(0, count // step, block, 0)


class Place:
    def __init__(self):
        query, corpus = lax.axis_index("query"), lax.axis_index("corpus")
        self.y = lax.rem(query, 4)
        self.x = 2 * lax.div(query, 4) + lax.rem(lax.div(corpus, 2), 2)
        self.z = lax.div(corpus, 4)
        self.core = lax.rem(corpus, 2)

    def at(self, x=None, y=None, z=None, core=None):
        x = self.x if x is None else x
        y = self.y if y is None else y
        z = self.z if z is None else z
        core = self.core if core is None else core
        return (4 * lax.div(x, 2) + y, 4 * z + 2 * lax.rem(x, 2) + core)

    def next_y(self, d):
        return lax.rem(self.y + d, 4)

    def next_x(self, d):
        return lax.rem(self.x + d, 4)

    def next_z(self, d):
        return lax.rem(self.z + d, 8)


class Wire:
    def __init__(self, sent, arrived):
        self.sent, self.arrived, self.copies = sent, arrived, []
        self.settled, self.mark = 0, 0

    def send(self, src, dst, device):
        i = len(self.copies)
        copy = pltpu.make_async_remote_copy(
            src_ref=src,
            dst_ref=dst,
            send_sem=self.sent.at[i],
            recv_sem=self.arrived.at[i],
            device_id=device,
            device_id_type=pl.DeviceIdType.MESH,
        )
        copy.start()
        self.copies.append(copy)
        return copy

    def settle(self):
        for copy in self.copies[self.settled : self.mark]:
            copy.wait_send()
        self.settled, self.mark = self.mark, len(self.copies)

    def finish(self):
        for copy in self.copies[self.settled :]:
            copy.wait_send()


def rows_at(index, size):
    return pl.ds(pl.multiple_of(index * size, size), size)


def merge(stats):
    top = stats[0][0:1]
    for s in stats[1:]:
        top = jnp.maximum(top, s[0:1])
    total = sum(s[1:2] * jnp.exp(s[0:1] - top) for s in stats)
    own = sum(s[2:3] for s in stats)
    pad = jnp.zeros((8 - 3, top.shape[1]), F32)
    return jnp.concatenate([top, total, own, pad], axis=0)


def step(
    q_hbm, codes_hbm, pos_ref, book_hbm,
    grad_q, grad_b, loss_ref,
    q_ref, codes_t, book_ref, book_t, q3, r3, q_t, e_ref, stats_ref, cols,
    pos_col, scale_col, e2, hits, spread, pulled, w3, d_ref,
    near, far, part_q, half_q, sum_q, ring_in, cross,
    words_b, part_b, half_b, sum_b, first_in, first_sum, second_in, second_sum, last_in,
    sent, arrived, loaded,
):
    loads = [
        pltpu.make_async_copy(book_hbm, book_ref, loaded.at[0]),
        pltpu.make_async_copy(codes_hbm, codes_t, loaded.at[1]),
        pltpu.make_async_copy(q_hbm, q_ref, loaded.at[2]),
    ]
    for load in loads:
        load.start()
    me = Place()
    wire = Wire(sent, arrived)
    x_pair = me.x + 1 - 2 * lax.rem(me.x, 2)
    other = 1 - me.core
    partners = [me.at(core=other), me.at(x=x_pair), me.at(x=x_pair, core=other)]
    far_partners = [me.at(z=me.next_z(d)) for d in range(1, 8)]
    y_partners = [me.at(y=me.next_y(d)) for d in range(1, 4)]
    x_partners = [me.at(x=me.next_x(d)) for d in range(1, 4)]
    greeted = [partners[0], partners[2]] + far_partners + y_partners + x_partners
    barrier = pltpu.get_barrier_semaphore()
    for device in greeted:
        pl.semaphore_signal(barrier, inc=1, device_id=device, device_id_type=pl.DeviceIdType.MESH)

    loads[0].wait()
    transpose_book(book_ref, book_t)
    loads[1].wait()
    rebuild(codes_t, book_t, r3)
    loads[2].wait()
    split_queries(q_ref, q3)
    score(q3, r3, e_ref)
    docs = codes_t.shape[1]
    here = pos_ref[...].reshape(1, -1) - lax.axis_index("corpus") * docs
    as_column(here, pos_col)
    statistics(e_ref, pos_col, cols, e2, hits)
    stats_ref[...] = cols[...].T[:8]
    pl.semaphore_wait(barrier, len(greeted))

    mine = 2 * lax.rem(me.x, 2) + me.core
    near[mine] = stats_ref[...]
    copies = [wire.send(stats_ref, near.at[mine], device) for device in partners]
    pull(hits, r3, pulled)
    for copy in copies:
        copy.wait_recv()
    far[me.z] = merge([near[k] for k in range(4)])
    copies = [wire.send(far.at[me.z], far.at[me.z], device) for device in far_partners]
    spread_out(e2, r3, spread)
    transpose_queries(q_ref, q_t)
    for copy in copies:
        copy.wait_recv()
    whole = merge([far[k] for k in range(8)])
    log_total = whole[0:1] + jnp.log(whole[1:2])
    loss_ref[...] = (log_total - whole[2:3]).reshape(-1)
    as_column(jnp.exp(stats_ref[0:1] - log_total), scale_col)

    query_gradient(spread, pulled, scale_col, part_q)
    half = part_q.shape[0] // 2
    chunk = half // 8
    q_core = wire.send(part_q.at[rows_at(other, half)], half_q, partners[0])
    weigh(e_ref, scale_col, pos_col, w3)
    document_gradient(w3, q_t, d_ref)
    q_core.wait_recv()
    sum_q[...] = part_q[rows_at(me.core, half)] + half_q[...]

    def arrive(copies):
        for copy in copies:
            copy.wait_recv()

    words, b_half = part_b.shape[0], part_b.shape[1] // 2
    lines = words // 8
    group_width = 4 * d_ref.shape[0] // codes_t.shape[0]

    def lines_at(k, first, size, second=None):
        start = k * (words // 2) + first * lines
        if second is not None:
            start = start + second * size
        return pl.ds(pl.multiple_of(start, size), size)

    order = (
        ((me.y, me.next_y, y_partners), (me.x, me.next_x, x_partners)),
        ((me.x, me.next_x, x_partners), (me.y, me.next_y, y_partners)),
    )
    passed, taken = [], [0, 0]

    def greet_passed():
        arrive(passed[taken[0] : taken[1]])
        taken[:] = taken[1], len(passed)

    def gather_words(core, part):
        offset, count = part
        base = core * b_half + offset
        collect(codes_t, d_ref, words_b, core * (b_half // group_width) + offset // group_width, count // group_width)
        transpose_run(words_b, base, count, part_b)

    def book_chain(part):
        offset, count = part
        inner = slice(offset, offset + count)
        theirs = pl.ds(pl.multiple_of(other * b_half + offset, 128), count)
        ours = pl.ds(pl.multiple_of(me.core * b_half + offset, 128), count)
        core = wire.send(part_b.at[:, theirs], half_b.at[:, inner], partners[0])
        yield
        core.wait_recv()
        sum_b[:, inner] = part_b[:, ours] + half_b[:, inner]
        firsts = []
        for k in range(2):
            _, following, devices = order[k][0]
            for d in range(1, 4):
                firsts.append(
                    wire.send(
                        sum_b.at[lines_at(k, following(d), lines), inner],
                        first_in.at[k, d - 1, :, inner],
                        devices[d - 1],
                    )
                )
        yield
        arrive(firsts)
        seconds = []
        for k in range(2):
            index, _, _ = order[k][0]
            acc = sum_b[lines_at(k, index, lines), inner]
            for d in range(3):
                acc = acc + first_in[k, d, :, inner]
            first_sum[k, :, inner] = acc
            _, following, devices = order[k][1]
            for d in range(1, 4):
                seconds.append(
                    wire.send(
                        first_sum.at[k, rows_at(following(d), lines // 4), inner],
                        second_in.at[k, d - 1, :, inner],
                        devices[d - 1],
                    )
                )
        yield
        arrive(seconds)
        for k in range(2):
            index, _, _ = order[k][1]
            acc = first_sum[k, rows_at(index, lines // 4), inner]
            for d in range(3):
                acc = acc + second_in[k, d, :, inner]
            last_in[me.z, k, :, inner] = acc
        mine = last_in.at[me.z, :, :, inner]
        lasts = [wire.send(mine, mine, device) for device in far_partners]
        yield
        arrive(lasts)
        acc = last_in[0, :, :, inner]
        for z in range(1, 8):
            acc = acc + last_in[z, :, :, inner]

        def share_b(at, device):
            return wire.send(grad_b.at[at, ours], grad_b.at[at, ours], device)

        seconds = []
        for k in range(2):
            at = lines_at(k, order[k][0][0], lines // 4, order[k][1][0])
            grad_b[at, ours] = acc[k]
            for device in order[k][1][2]:
                seconds.append(share_b(at, device))
        yield
        arrive(seconds)
        firsts = []
        for k in range(2):
            at = lines_at(k, order[k][0][0], lines)
            for device in order[k][0][2]:
                firsts.append(share_b(at, device))
        for k in range(2):
            passed.append(share_b(lines_at(k, order[k][0][0], lines), partners[0]))
        yield
        for d in (1, 3, 2):
            for k in range(2):
                arrive([firsts[3 * k + d - 1]])
                back = order[k][0][1](4 - d)
                passed.append(share_b(lines_at(k, back, lines), partners[0]))
        yield

    def q_rows(z):
        return pl.ds(pl.multiple_of(me.core * half + z * chunk, chunk), chunk)

    def share(at, device):
        return wire.send(grad_q.at[at], grad_q.at[at], device)

    def query_chain():
        terms = [
            wire.send(sum_q.at[rows_at(me.next_z(d), chunk)], ring_in.at[d - 1], far_partners[d - 1])
            for d in (4, 3, 5, 2, 6, 1, 7)
        ]
        yield
        arrive(terms)
        acc = sum_q[rows_at(me.z, chunk)]
        for d in range(7):
            acc = acc + ring_in[d]
        cross[0] = acc
        across = wire.send(cross.at[0], cross.at[1], partners[1])
        yield
        arrive([across])
        grad_q[q_rows(me.z)] = cross[0] + cross[1]
        passed.append(share(q_rows(me.z), partners[0]))
        shares = {d: share(q_rows(me.z), far_partners[d - 1]) for d in (4, 3, 5, 2, 6, 1, 7)}
        for part in ((1, 7, 2), (6, 3, 5, 4)):
            yield
            for d in part:
                arrive([shares[d]])
                passed.append(share(q_rows(me.next_z(8 - d)), partners[0]))
        yield

    large, small = (0, 2 * b_half // 3), (2 * b_half // 3, b_half // 3)
    queries = query_chain()
    next(queries)
    gather_words(other, large)
    first = book_chain(large)
    next(first)
    gather_words(me.core, large)
    next(first)
    gather_words(other, small)
    second = book_chain(small)
    next(second)
    gather_words(me.core, small)
    next(second)
    wire.settle()
    next(first)
    next(second)
    wire.settle()
    next(queries)
    next(first)
    next(second)
    wire.settle()
    next(queries)
    next(first)
    next(second)
    wire.settle()
    next(first)
    next(second)
    wire.settle()
    next(queries)
    greet_passed()
    next(first)
    next(second)
    wire.settle()
    next(queries)
    greet_passed()
    arrive(passed[taken[0] :])
    wire.finish()
    assert len(wire.copies) == COPIES, len(wire.copies)


def hand_over(*refs):
    inside, outside = refs[9], refs[10]
    steps = []
    for k in range(3):
        src, dst, held = refs[k], refs[3 + k], refs[6 + k]
        pieces = 4 if len(src.shape) > 1 else 1
        size = src.shape[0] // pieces
        for n in range(pieces):
            at = pl.ds(n * size, size)
            i = len(steps)
            steps.append(
                (
                    pltpu.make_async_copy(src.at[at], held.at[at], inside.at[i]),
                    pltpu.make_async_copy(held.at[at], dst.at[at], outside.at[i]),
                )
            )
    for load, _ in steps:
        load.start()
    for load, store in steps:
        load.wait()
        store.start()
    for _, store in steps:
        store.wait()


def local(queries, codes, positive, codebook):
    rows, width = queries.shape
    docs, subs = codes.shape
    words = codebook.shape[0]
    chunk = rows // 16
    lines = words // 8
    half = width // 2
    depth = 256 * pl.cdiv(3 * rows, 256)
    vmem = pl.BlockSpec(memory_space=pltpu.VMEM)
    hbm = pl.BlockSpec(memory_space=pltpu.HBM)
    grad_q, grad_b, loss = pl.pallas_call(
        step,
        in_specs=[hbm, hbm, vmem, hbm],
        out_specs=(vmem, vmem, vmem),
        out_shape=(
            jax.ShapeDtypeStruct((rows, width), F32),
            jax.ShapeDtypeStruct((words, width), F32),
            jax.ShapeDtypeStruct((rows,), F32),
        ),
        scratch_shapes=[
            pltpu.VMEM((rows, width), F32),
            pltpu.VMEM((subs, docs), I32),
            pltpu.VMEM((words, width), F32),
            pltpu.VMEM((width, words), F32),
            pltpu.VMEM((rows, 3 * width), BF16),
            pltpu.VMEM((3 * width, docs), BF16),
            pltpu.VMEM((width, depth), BF16),
            pltpu.VMEM((rows, docs), F32),
            pltpu.VMEM((8, rows), F32),
            pltpu.VMEM((rows, 128), F32),
            pltpu.VMEM((rows, 128), I32),
            pltpu.VMEM((rows, 128), F32),
            pltpu.VMEM((2 * rows, docs), BF16),
            pltpu.VMEM((rows, docs), BF16),
            pltpu.VMEM((rows, width), F32),
            pltpu.VMEM((rows, width), F32),
            pltpu.VMEM((depth, docs), BF16),
            pltpu.VMEM((width, docs), F32),
            pltpu.VMEM((4, 8, rows), F32),
            pltpu.VMEM((8, 8, rows), F32),
            pltpu.VMEM((rows, width), F32),
            pltpu.VMEM((rows // 2, width), F32),
            pltpu.VMEM((rows // 2, width), F32),
            pltpu.VMEM((7, chunk, width), F32),
            pltpu.VMEM((2, chunk, width), F32),
            pltpu.VMEM((width, words), F32),
            pltpu.VMEM((words, width), F32),
            pltpu.VMEM((words, half), F32),
            pltpu.VMEM((words, half), F32),
            pltpu.VMEM((2, 3, lines, half), F32),
            pltpu.VMEM((2, lines, half), F32),
            pltpu.VMEM((2, 3, lines // 4, half), F32),
            pltpu.VMEM((2, lines // 4, half), F32),
            pltpu.VMEM((8, 2, lines // 4, half), F32),
            pltpu.SemaphoreType.DMA((COPIES,)),
            pltpu.SemaphoreType.DMA((COPIES,)),
            pltpu.SemaphoreType.DMA((3,)),
        ],
        compiler_params=pltpu.CompilerParams(
            collective_id=0, has_side_effects=True, vmem_limit_bytes=56 << 20
        ),
        name="step",
    )(queries, codes.T, positive, codebook)
    return pl.pallas_call(
        hand_over,
        in_specs=[hbm] * 3,
        out_specs=[hbm] * 3,
        out_shape=[jax.ShapeDtypeStruct(x.shape, F32) for x in (grad_q, grad_b, loss)],
        scratch_shapes=[
            *(pltpu.VMEM(x.shape, F32) for x in (grad_q, grad_b, loss)),
            pltpu.SemaphoreType.DMA((9,)),
            pltpu.SemaphoreType.DMA((9,)),
        ],
        name="hand_over",
    )(grad_q, grad_b, loss)


def solution(mesh):
    return jax.shard_map(
        local,
        mesh=mesh,
        in_specs=(P("query", None), P("corpus", None), P("query"), P()),
        out_specs=(P("query", None), P(), P("query")),
        check_vma=False,
    )
```

```python
import jax
import jax.numpy as jnp
from jax import lax
from jax.experimental import pallas as pl
from jax.experimental.pallas import tpu as pltpu
from jax.sharding import PartitionSpec as P

F32, BF16, I32 = jnp.float32, jnp.bfloat16, jnp.int32
NN = (((1,), (0,)), ((), ()))
NT = (((1,), (1,)), ((), ()))
HIGH_CODES = 64
LOW_CODES = 4
COPIES = 130


def dot(a, b, dims=NN):
    return lax.dot_general(a, b, dims, preferred_element_type=F32)


def split(x):
    high = x.astype(BF16)
    return high, (x - high.astype(F32)).astype(BF16)


def split3(x):
    high = x.astype(BF16)
    rest = x - high.astype(F32)
    mid = rest.astype(BF16)
    return high, mid, (rest - mid.astype(F32)).astype(BF16)


def split_queries(q_ref, q3, step=32):
    width = q_ref.shape[1]

    def block(b, _):
        at = pl.ds(pl.multiple_of(b * step, step), step)
        high, mid, low = split3(q_ref[at, :])
        q3[at, :width] = high
        q3[at, width : 2 * width] = mid
        q3[at, 2 * width :] = low
        return 0

    lax.fori_loop(0, q_ref.shape[0] // step, block, 0)


def transpose_queries(q_ref, q_t, step=128):
    rows = q_ref.shape[0]

    def block(b, _):
        at = pl.ds(pl.multiple_of(b * step, step), step)
        high, mid = split(q_ref[:, at].T)
        q_t[at, :rows] = high
        q_t[at, rows : 2 * rows] = mid
        q_t[at, 2 * rows : 3 * rows] = high
        q_t[at, 3 * rows :] = jnp.zeros((step, q_t.shape[1] - 3 * rows), BF16)
        return 0

    lax.fori_loop(0, q_ref.shape[1] // step, block, 0)


def transpose_book(book_ref, book_t, step=128):
    def block(b, _):
        at = pl.ds(pl.multiple_of(b * step, step), step)
        book_t[at, :] = book_ref[:, at].T
        return 0

    lax.fori_loop(0, book_ref.shape[1] // step, block, 0)


def rebuild(codes_t, book_t, r3, unroll=4):
    subs, docs = codes_t.shape
    width = book_t.shape[0]
    sub_width = width // subs

    def pair(p):
        parts = []
        for side in range(2):
            m = 2 * p + side
            base = pl.multiple_of(m * sub_width, sub_width)
            low = book_t[pl.ds(base, sub_width), :128]
            high = book_t[pl.ds(base, sub_width), 128:]
            code = codes_t[pl.ds(m, 1), :]
            tiles = []
            for t in range(docs // 128):
                picked = jnp.broadcast_to(code[:, 128 * t : 128 * t + 128], (sub_width, 128))
                lane = picked & 127
                a = jnp.take_along_axis(low, lane, axis=1, mode="promise_in_bounds")
                b = jnp.take_along_axis(high, lane, axis=1, mode="promise_in_bounds")
                tiles.append(jnp.where(picked < 128, a, b))
            parts.append(jnp.concatenate(tiles, axis=1))
        high, mid, low = split3(jnp.concatenate(parts, axis=0))
        at = pl.multiple_of(2 * p * sub_width, 2 * sub_width)
        r3[pl.ds(at, 2 * sub_width), :] = low
        r3[pl.ds(width + at, 2 * sub_width), :] = mid
        r3[pl.ds(2 * width + at, 2 * sub_width), :] = high

    def block(b, _):
        for u in range(unroll):
            pair(unroll * b + u)
        return 0

    lax.fori_loop(0, subs // 2 // unroll, block, 0)


def score(q3, r3, s_ref, tile=512):
    width = q3.shape[1] // 3

    def block(t, _):
        at = pl.ds(pl.multiple_of(t * tile, tile), tile)
        acc = dot(q3[...], r3[:, at])
        acc = acc + dot(q3[:, : 2 * width], r3[width:, at])
        s_ref[:, at] = acc + dot(q3[:, :width], r3[2 * width :, at])
        return 0

    lax.fori_loop(0, s_ref.shape[1] // tile, block, 0)


def statistics(s_ref, pos_col, cols, e2, hits, step=64):
    rows, docs = s_ref.shape
    lane = lax.broadcasted_iota(I32, (step, 128), 1)
    ids = lax.broadcasted_iota(I32, (step, docs), 1)

    def block(b, _):
        at = pl.ds(pl.multiple_of(b * step, step), step)
        s = s_ref[at, :]
        top = jnp.max(s, axis=1, keepdims=True)
        hit = pos_col[at, :1] == ids
        own = jnp.sum(jnp.where(hit, s, 0.0), axis=1, keepdims=True)
        hits[at, :] = jnp.where(hit, 1.0, 0.0).astype(BF16)
        e = jnp.exp(s - top)
        total = jnp.sum(e, axis=1, keepdims=True)
        s_ref[at, :] = e
        high, low = split(e)
        e2[at, :] = low
        e2[pl.ds(pl.multiple_of(rows + b * step, step), step), :] = high
        cols[at, :] = jnp.where(
            lane == 0, top, jnp.where(lane == 1, total, jnp.where(lane == 2, own, 0.0))
        )
        return 0

    lax.fori_loop(0, rows // step, block, 0)


def as_column(row, column):
    column[...] = jnp.broadcast_to(row, (128, row.shape[1])).T


def pull(hits, r3, pulled, tile=256):
    width = r3.shape[0] // 3

    def block(t, _):
        base = pl.multiple_of(t * tile, tile)
        acc = dot(hits[...], r3[pl.ds(width + base, tile), :], NT)
        pulled[:, pl.ds(base, tile)] = acc + dot(hits[...], r3[pl.ds(2 * width + base, tile), :], NT)
        return 0

    lax.fori_loop(0, width // tile, block, 0)


def spread_out(e2, r3, spread, tile=256):
    rows = e2.shape[0] // 2
    width = r3.shape[0] // 3

    def block(t, _):
        base = pl.multiple_of(t * tile, tile)
        mid = r3[pl.ds(width + base, tile), :]
        high = r3[pl.ds(2 * width + base, tile), :]
        acc = dot(e2[rows:, :], mid, NT)
        acc = acc + dot(e2[:rows, :], high, NT)
        spread[:, pl.ds(base, tile)] = acc + dot(e2[rows:, :], high, NT)
        return 0

    lax.fori_loop(0, width // tile, block, 0)


def query_gradient(spread, pulled, scale_col, out, step=32):
    def block(b, _):
        at = pl.ds(pl.multiple_of(b * step, step), step)
        out[at, :] = spread[at, :] * scale_col[at, :1] - pulled[at, :]
        return 0

    lax.fori_loop(0, spread.shape[0] // step, block, 0)


def weigh(e_ref, scale_col, pos_col, w3, step=32):
    rows, docs = e_ref.shape
    w3[3 * rows :, :] = jnp.zeros((w3.shape[0] - 3 * rows, docs), BF16)
    ids = lax.broadcasted_iota(I32, (step, docs), 1)

    def block(b, _):
        at = pl.ds(pl.multiple_of(b * step, step), step)
        w = e_ref[at, :] * scale_col[at, :1]
        w = w - jnp.where(pos_col[at, :1] == ids, 1.0, 0.0)
        high, low = split(w)
        w3[at, :] = low
        w3[pl.ds(pl.multiple_of(rows + b * step, step), step), :] = high
        w3[pl.ds(pl.multiple_of(2 * rows + b * step, step), step), :] = high
        return 0

    lax.fori_loop(0, rows // step, block, 0)


def document_gradient(w3, q_t, out, tile=256):
    for t in range(out.shape[1] // tile):
        at = slice(t * tile, t * tile + tile)
        out[:, at] = dot(q_t[...], w3[:, at])


def collect(codes_t, d_ref, out, base, count, group=4):
    subs, docs = codes_t.shape
    sub_width = d_ref.shape[0] // subs
    word = lax.broadcasted_iota(I32, (HIGH_CODES, docs), 0)
    lane = lax.broadcasted_iota(I32, (sub_width, 128), 1)

    def one(b):
        g = b + base
        tables, values = [], []
        for s in range(group):
            m = group * g + s
            code = codes_t[pl.ds(m, 1), :]
            inner = code & (HIGH_CODES - 1)
            outer = jnp.broadcast_to(code >> 6, (sub_width, docs))
            tables.append(jnp.where(word == inner, 1.0, 0.0).astype(BF16))
            d = d_ref[pl.ds(pl.multiple_of(m * sub_width, sub_width), sub_width), :]
            high = d.astype(BF16).astype(F32)
            low = d - high
            masks = [outer == k for k in range(LOW_CODES)]
            rows = [jnp.where(mask, part, 0.0) for part in (high, low) for mask in masks]
            values.append(jnp.concatenate(rows, axis=0).astype(BF16))
        found = dot(jnp.concatenate(values, axis=0), jnp.concatenate(tables, axis=0), NT)
        rows = 2 * LOW_CODES * sub_width
        for s in range(group):
            at = 128 * (s // 2)
            piece = found[rows * s : rows * (s + 1), at : at + 128]
            piece = piece[: rows // 2] + piece[rows // 2 :]
            parts = [piece[sub_width * k : sub_width * (k + 1)] for k in range(LOW_CODES)]
            start = pl.multiple_of((group * g + s) * sub_width, sub_width)
            for k in range(2):
                first, second = parts[2 * k], parts[2 * k + 1]
                if s % 2:
                    first = pltpu.roll(first, 64, 1)
                else:
                    second = pltpu.roll(second, 64, 1)
                out[pl.ds(start, sub_width), 128 * k : 128 * k + 128] = jnp.where(
                    lane < 64, first, second
                )

    for b in range(count):
        one(b)


def transpose_run(part, base, count, out, step=128):
    def block(b, _):
        at = pl.ds(pl.multiple_of(base + b * step, step), step)
        out[:, at] = part[at, :].T
        return 0

    lax.fori_loop(0, count // step, block, 0)


class Place:
    def __init__(self):
        query, corpus = lax.axis_index("query"), lax.axis_index("corpus")
        self.y = lax.rem(query, 4)
        self.x = 2 * lax.div(query, 4) + lax.rem(lax.div(corpus, 2), 2)
        self.z = lax.div(corpus, 4)
        self.core = lax.rem(corpus, 2)

    def at(self, x=None, y=None, z=None, core=None):
        x = self.x if x is None else x
        y = self.y if y is None else y
        z = self.z if z is None else z
        core = self.core if core is None else core
        return (4 * lax.div(x, 2) + y, 4 * z + 2 * lax.rem(x, 2) + core)

    def next_y(self, d):
        return lax.rem(self.y + d, 4)

    def next_x(self, d):
        return lax.rem(self.x + d, 4)

    def next_z(self, d):
        return lax.rem(self.z + d, 8)


class Wire:
    def __init__(self, sent, arrived):
        self.sent, self.arrived, self.copies = sent, arrived, []
        self.settled, self.mark = 0, 0

    def send(self, src, dst, device):
        i = len(self.copies)
        copy = pltpu.make_async_remote_copy(
            src_ref=src,
            dst_ref=dst,
            send_sem=self.sent.at[i],
            recv_sem=self.arrived.at[i],
            device_id=device,
            device_id_type=pl.DeviceIdType.MESH,
        )
        copy.start()
        self.copies.append(copy)
        return copy

    def settle(self):
        for copy in self.copies[self.settled : self.mark]:
            copy.wait_send()
        self.settled, self.mark = self.mark, len(self.copies)

    def finish(self):
        for copy in self.copies[self.settled :]:
            copy.wait_send()


def rows_at(index, size):
    return pl.ds(pl.multiple_of(index * size, size), size)


def merge(stats):
    top = stats[0][0:1]
    for s in stats[1:]:
        top = jnp.maximum(top, s[0:1])
    total = sum(s[1:2] * jnp.exp(s[0:1] - top) for s in stats)
    own = sum(s[2:3] for s in stats)
    pad = jnp.zeros((8 - 3, top.shape[1]), F32)
    return jnp.concatenate([top, total, own, pad], axis=0)


def step(
    q_hbm, codes_hbm, pos_ref, book_hbm,
    grad_q, grad_b, loss_ref,
    q_ref, codes_t, book_ref, book_t, q3, r3, q_t, e_ref, stats_ref, cols,
    pos_col, scale_col, e2, hits, spread, pulled, w3, d_ref,
    near, far, part_q, half_q, sum_q, ring_in, cross,
    words_b, part_b, half_b, sum_b, first_in, first_sum, second_in, second_sum, last_in,
    sent, arrived, loaded,
):
    loads = [
        pltpu.make_async_copy(book_hbm, book_ref, loaded.at[0]),
        pltpu.make_async_copy(codes_hbm, codes_t, loaded.at[1]),
        pltpu.make_async_copy(q_hbm, q_ref, loaded.at[2]),
    ]
    for load in loads:
        load.start()
    me = Place()
    wire = Wire(sent, arrived)
    x_pair = me.x + 1 - 2 * lax.rem(me.x, 2)
    other = 1 - me.core
    partners = [me.at(core=other), me.at(x=x_pair), me.at(x=x_pair, core=other)]
    far_partners = [me.at(z=me.next_z(d)) for d in range(1, 8)]
    y_partners = [me.at(y=me.next_y(d)) for d in range(1, 4)]
    x_partners = [me.at(x=me.next_x(d)) for d in range(1, 4)]
    greeted = [partners[0], partners[2]] + far_partners + y_partners + x_partners
    barrier = pltpu.get_barrier_semaphore()
    for device in greeted:
        pl.semaphore_signal(barrier, inc=1, device_id=device, device_id_type=pl.DeviceIdType.MESH)

    loads[0].wait()
    transpose_book(book_ref, book_t)
    loads[1].wait()
    rebuild(codes_t, book_t, r3)
    loads[2].wait()
    split_queries(q_ref, q3)
    score(q3, r3, e_ref)
    docs = codes_t.shape[1]
    here = pos_ref[...].reshape(1, -1) - lax.axis_index("corpus") * docs
    as_column(here, pos_col)
    statistics(e_ref, pos_col, cols, e2, hits)
    stats_ref[...] = cols[...].T[:8]
    pl.semaphore_wait(barrier, len(greeted))

    mine = 2 * lax.rem(me.x, 2) + me.core
    near[mine] = stats_ref[...]
    copies = [wire.send(stats_ref, near.at[mine], device) for device in partners]
    pull(hits, r3, pulled)
    for copy in copies:
        copy.wait_recv()
    far[me.z] = merge([near[k] for k in range(4)])
    copies = [wire.send(far.at[me.z], far.at[me.z], device) for device in far_partners]
    spread_out(e2, r3, spread)
    transpose_queries(q_ref, q_t)
    for copy in copies:
        copy.wait_recv()
    whole = merge([far[k] for k in range(8)])
    log_total = whole[0:1] + jnp.log(whole[1:2])
    loss_ref[...] = (log_total - whole[2:3]).reshape(-1)
    as_column(jnp.exp(stats_ref[0:1] - log_total), scale_col)

    query_gradient(spread, pulled, scale_col, part_q)
    half = part_q.shape[0] // 2
    chunk = half // 8
    q_core = wire.send(part_q.at[rows_at(other, half)], half_q, partners[0])
    weigh(e_ref, scale_col, pos_col, w3)
    document_gradient(w3, q_t, d_ref)
    q_core.wait_recv()
    sum_q[...] = part_q[rows_at(me.core, half)] + half_q[...]

    def arrive(copies):
        for copy in copies:
            copy.wait_recv()

    words, b_half = part_b.shape[0], part_b.shape[1] // 2
    lines = words // 8
    group_width = 4 * d_ref.shape[0] // codes_t.shape[0]

    def lines_at(k, first, size, second=None):
        start = k * (words // 2) + first * lines
        if second is not None:
            start = start + second * size
        return pl.ds(pl.multiple_of(start, size), size)

    order = (
        ((me.y, me.next_y, y_partners), (me.x, me.next_x, x_partners)),
        ((me.x, me.next_x, x_partners), (me.y, me.next_y, y_partners)),
    )
    passed, taken = [], [0, 0]

    def greet_passed():
        arrive(passed[taken[0] : taken[1]])
        taken[:] = taken[1], len(passed)

    def gather_words(core, part):
        offset, count = part
        base = core * b_half + offset
        collect(codes_t, d_ref, words_b, core * (b_half // group_width) + offset // group_width, count // group_width)
        transpose_run(words_b, base, count, part_b)

    def book_chain(part):
        offset, count = part
        inner = slice(offset, offset + count)
        theirs = pl.ds(pl.multiple_of(other * b_half + offset, 128), count)
        ours = pl.ds(pl.multiple_of(me.core * b_half + offset, 128), count)
        core = wire.send(part_b.at[:, theirs], half_b.at[:, inner], partners[0])
        yield
        core.wait_recv()
        sum_b[:, inner] = part_b[:, ours] + half_b[:, inner]
        firsts = []
        for k in range(2):
            _, following, devices = order[k][0]
            for d in range(1, 4):
                firsts.append(
                    wire.send(
                        sum_b.at[lines_at(k, following(d), lines), inner],
                        first_in.at[k, d - 1, :, inner],
                        devices[d - 1],
                    )
                )
        yield
        arrive(firsts)
        seconds = []
        for k in range(2):
            index, _, _ = order[k][0]
            acc = sum_b[lines_at(k, index, lines), inner]
            for d in range(3):
                acc = acc + first_in[k, d, :, inner]
            first_sum[k, :, inner] = acc
            _, following, devices = order[k][1]
            for d in range(1, 4):
                seconds.append(
                    wire.send(
                        first_sum.at[k, rows_at(following(d), lines // 4), inner],
                        second_in.at[k, d - 1, :, inner],
                        devices[d - 1],
                    )
                )
        yield
        arrive(seconds)
        for k in range(2):
            index, _, _ = order[k][1]
            acc = first_sum[k, rows_at(index, lines // 4), inner]
            for d in range(3):
                acc = acc + second_in[k, d, :, inner]
            last_in[me.z, k, :, inner] = acc
        mine = last_in.at[me.z, :, :, inner]
        lasts = [wire.send(mine, mine, device) for device in far_partners]
        yield
        arrive(lasts)
        acc = last_in[0, :, :, inner]
        for z in range(1, 8):
            acc = acc + last_in[z, :, :, inner]

        def share_b(at, device):
            return wire.send(grad_b.at[at, ours], grad_b.at[at, ours], device)

        seconds = []
        for k in range(2):
            at = lines_at(k, order[k][0][0], lines // 4, order[k][1][0])
            grad_b[at, ours] = acc[k]
            for device in order[k][1][2]:
                seconds.append(share_b(at, device))
        yield
        arrive(seconds)
        firsts = []
        for k in range(2):
            at = lines_at(k, order[k][0][0], lines)
            for device in order[k][0][2]:
                firsts.append(share_b(at, device))
        for k in range(2):
            passed.append(share_b(lines_at(k, order[k][0][0], lines), partners[0]))
        yield
        for d in (1, 3, 2):
            for k in range(2):
                arrive([firsts[3 * k + d - 1]])
                back = order[k][0][1](4 - d)
                passed.append(share_b(lines_at(k, back, lines), partners[0]))
        yield

    def q_rows(z):
        return pl.ds(pl.multiple_of(me.core * half + z * chunk, chunk), chunk)

    def query_chain():
        terms = [
            wire.send(sum_q.at[rows_at(me.next_z(d), chunk)], ring_in.at[d - 1], far_partners[d - 1])
            for d in (4, 3, 5, 2, 6, 1, 7)
        ]
        side = lax.rem(me.x, 2)
        across_width = grad_q.shape[1] // 2
        ours, theirs = rows_at(side, across_width), rows_at(1 - side, across_width)

        def share(z, columns, device):
            at = q_rows(z)
            return wire.send(grad_q.at[at, columns], grad_q.at[at, columns], device)

        yield
        arrive(terms)
        acc = sum_q[rows_at(me.z, chunk)]
        for d in range(7):
            acc = acc + ring_in[d]
        cross[0] = acc
        across = wire.send(cross.at[0, :, theirs], cross.at[1, :, theirs], partners[1])
        yield
        arrive([across])
        grad_q[q_rows(me.z), ours] = cross[0, :, ours] + cross[1, :, ours]
        shares = {d: share(me.z, ours, far_partners[d - 1]) for d in (4, 3, 5, 2, 6, 1, 7)}
        beside = {0: share(me.z, ours, partners[1])}
        passed.append(share(me.z, ours, partners[0]))
        for part in ((1, 7, 2), (6, 3, 5, 4)):
            yield
            for d in part:
                arrive([shares[d]])
                beside[d] = share(me.next_z(8 - d), ours, partners[1])
                passed.append(share(me.next_z(8 - d), ours, partners[0]))
        yield
        for d in (0, 1, 7, 2, 6, 3, 5, 4):
            arrive([beside[d]])
            passed.append(share(me.next_z(8 - d), theirs, partners[0]))
        yield

    large, small = (0, 2 * b_half // 3), (2 * b_half // 3, b_half // 3)
    queries = query_chain()
    next(queries)
    gather_words(other, large)
    first = book_chain(large)
    next(first)
    gather_words(me.core, large)
    next(first)
    gather_words(other, small)
    second = book_chain(small)
    next(second)
    gather_words(me.core, small)
    next(second)
    wire.settle()
    next(first)
    next(second)
    wire.settle()
    next(queries)
    next(first)
    next(second)
    wire.settle()
    next(queries)
    next(first)
    next(second)
    wire.settle()
    next(queries)
    greet_passed()
    next(first)
    next(second)
    wire.settle()
    next(queries)
    greet_passed()
    next(first)
    next(second)
    wire.settle()
    next(queries)
    greet_passed()
    wire.settle()
    arrive(passed[taken[0] :])
    wire.finish()
    assert len(wire.copies) == COPIES, len(wire.copies)


def hand_over(*refs):
    inside, outside = refs[9], refs[10]
    steps = []
    for k in range(3):
        src, dst, held = refs[k], refs[3 + k], refs[6 + k]
        pieces = 4 if len(src.shape) > 1 else 1
        size = src.shape[0] // pieces
        for n in range(pieces):
            at = pl.ds(n * size, size)
            i = len(steps)
            steps.append(
                (
                    pltpu.make_async_copy(src.at[at], held.at[at], inside.at[i]),
                    pltpu.make_async_copy(held.at[at], dst.at[at], outside.at[i]),
                )
            )
    for load, _ in steps:
        load.start()
    for load, store in steps:
        load.wait()
        store.start()
    for _, store in steps:
        store.wait()


def local(queries, codes, positive, codebook):
    rows, width = queries.shape
    docs, subs = codes.shape
    words = codebook.shape[0]
    chunk = rows // 16
    lines = words // 8
    half = width // 2
    depth = 256 * pl.cdiv(3 * rows, 256)
    vmem = pl.BlockSpec(memory_space=pltpu.VMEM)
    hbm = pl.BlockSpec(memory_space=pltpu.HBM)
    grad_q, grad_b, loss = pl.pallas_call(
        step,
        in_specs=[hbm, hbm, vmem, hbm],
        out_specs=(vmem, vmem, vmem),
        out_shape=(
            jax.ShapeDtypeStruct((rows, width), F32),
            jax.ShapeDtypeStruct((words, width), F32),
            jax.ShapeDtypeStruct((rows,), F32),
        ),
        scratch_shapes=[
            pltpu.VMEM((rows, width), F32),
            pltpu.VMEM((subs, docs), I32),
            pltpu.VMEM((words, width), F32),
            pltpu.VMEM((width, words), F32),
            pltpu.VMEM((rows, 3 * width), BF16),
            pltpu.VMEM((3 * width, docs), BF16),
            pltpu.VMEM((width, depth), BF16),
            pltpu.VMEM((rows, docs), F32),
            pltpu.VMEM((8, rows), F32),
            pltpu.VMEM((rows, 128), F32),
            pltpu.VMEM((rows, 128), I32),
            pltpu.VMEM((rows, 128), F32),
            pltpu.VMEM((2 * rows, docs), BF16),
            pltpu.VMEM((rows, docs), BF16),
            pltpu.VMEM((rows, width), F32),
            pltpu.VMEM((rows, width), F32),
            pltpu.VMEM((depth, docs), BF16),
            pltpu.VMEM((width, docs), F32),
            pltpu.VMEM((4, 8, rows), F32),
            pltpu.VMEM((8, 8, rows), F32),
            pltpu.VMEM((rows, width), F32),
            pltpu.VMEM((rows // 2, width), F32),
            pltpu.VMEM((rows // 2, width), F32),
            pltpu.VMEM((7, chunk, width), F32),
            pltpu.VMEM((2, chunk, width), F32),
            pltpu.VMEM((width, words), F32),
            pltpu.VMEM((words, width), F32),
            pltpu.VMEM((words, half), F32),
            pltpu.VMEM((words, half), F32),
            pltpu.VMEM((2, 3, lines, half), F32),
            pltpu.VMEM((2, lines, half), F32),
            pltpu.VMEM((2, 3, lines // 4, half), F32),
            pltpu.VMEM((2, lines // 4, half), F32),
            pltpu.VMEM((8, 2, lines // 4, half), F32),
            pltpu.SemaphoreType.DMA((COPIES,)),
            pltpu.SemaphoreType.DMA((COPIES,)),
            pltpu.SemaphoreType.DMA((3,)),
        ],
        compiler_params=pltpu.CompilerParams(
            collective_id=0, has_side_effects=True, vmem_limit_bytes=56 << 20
        ),
        name="step",
    )(queries, codes.T, positive, codebook)
    return pl.pallas_call(
        hand_over,
        in_specs=[hbm] * 3,
        out_specs=[hbm] * 3,
        out_shape=[jax.ShapeDtypeStruct(x.shape, F32) for x in (grad_q, grad_b, loss)],
        scratch_shapes=[
            *(pltpu.VMEM(x.shape, F32) for x in (grad_q, grad_b, loss)),
            pltpu.SemaphoreType.DMA((9,)),
            pltpu.SemaphoreType.DMA((9,)),
        ],
        name="hand_over",
    )(grad_q, grad_b, loss)


def solution(mesh):
    return jax.shard_map(
        local,
        mesh=mesh,
        in_specs=(P("query", None), P("corpus", None), P("query"), P()),
        out_specs=(P("query", None), P(), P("query")),
        check_vma=False,
    )
```

```python
import jax
import jax.numpy as jnp
from jax import lax
from jax.experimental import pallas as pl
from jax.experimental.pallas import tpu as pltpu
from jax.sharding import PartitionSpec as P

F32, BF16, I32 = jnp.float32, jnp.bfloat16, jnp.int32
NN = (((1,), (0,)), ((), ()))
NT = (((1,), (1,)), ((), ()))
HIGH_CODES = 64
LOW_CODES = 4
COPIES = 118


def dot(a, b, dims=NN):
    return lax.dot_general(a, b, dims, preferred_element_type=F32)


def split(x):
    high = x.astype(BF16)
    return high, (x - high.astype(F32)).astype(BF16)


def split3(x):
    high = x.astype(BF16)
    rest = x - high.astype(F32)
    mid = rest.astype(BF16)
    return high, mid, (rest - mid.astype(F32)).astype(BF16)


def split_queries(q_ref, q3, step=32):
    width = q_ref.shape[1]

    def block(b, _):
        at = pl.ds(pl.multiple_of(b * step, step), step)
        high, mid, low = split3(q_ref[at, :])
        q3[at, :width] = high
        q3[at, width : 2 * width] = mid
        q3[at, 2 * width :] = low
        return 0

    lax.fori_loop(0, q_ref.shape[0] // step, block, 0)


def transpose_queries(q_ref, q_t, step=128):
    rows = q_ref.shape[0]

    def block(b, _):
        at = pl.ds(pl.multiple_of(b * step, step), step)
        high, mid = split(q_ref[:, at].T)
        q_t[at, :rows] = high
        q_t[at, rows : 2 * rows] = mid
        q_t[at, 2 * rows : 3 * rows] = high
        q_t[at, 3 * rows :] = jnp.zeros((step, q_t.shape[1] - 3 * rows), BF16)
        return 0

    lax.fori_loop(0, q_ref.shape[1] // step, block, 0)


def transpose_book(book_ref, book_t, step=128):
    def block(b, _):
        at = pl.ds(pl.multiple_of(b * step, step), step)
        book_t[at, :] = book_ref[:, at].T
        return 0

    lax.fori_loop(0, book_ref.shape[1] // step, block, 0)


def rebuild(codes_t, book_t, r3, unroll=4):
    subs, docs = codes_t.shape
    width = book_t.shape[0]
    sub_width = width // subs

    def pair(p):
        parts = []
        for side in range(2):
            m = 2 * p + side
            base = pl.multiple_of(m * sub_width, sub_width)
            low = book_t[pl.ds(base, sub_width), :128]
            high = book_t[pl.ds(base, sub_width), 128:]
            code = codes_t[pl.ds(m, 1), :]
            tiles = []
            for t in range(docs // 128):
                picked = jnp.broadcast_to(code[:, 128 * t : 128 * t + 128], (sub_width, 128))
                lane = picked & 127
                a = jnp.take_along_axis(low, lane, axis=1, mode="promise_in_bounds")
                b = jnp.take_along_axis(high, lane, axis=1, mode="promise_in_bounds")
                tiles.append(jnp.where(picked < 128, a, b))
            parts.append(jnp.concatenate(tiles, axis=1))
        high, mid, low = split3(jnp.concatenate(parts, axis=0))
        at = pl.multiple_of(2 * p * sub_width, 2 * sub_width)
        r3[pl.ds(at, 2 * sub_width), :] = low
        r3[pl.ds(width + at, 2 * sub_width), :] = mid
        r3[pl.ds(2 * width + at, 2 * sub_width), :] = high

    def block(b, _):
        for u in range(unroll):
            pair(unroll * b + u)
        return 0

    lax.fori_loop(0, subs // 2 // unroll, block, 0)


def score(q3, r3, s_ref, tile=512):
    width = q3.shape[1] // 3

    def block(t, _):
        at = pl.ds(pl.multiple_of(t * tile, tile), tile)
        acc = dot(q3[...], r3[:, at])
        acc = acc + dot(q3[:, : 2 * width], r3[width:, at])
        s_ref[:, at] = acc + dot(q3[:, :width], r3[2 * width :, at])
        return 0

    lax.fori_loop(0, s_ref.shape[1] // tile, block, 0)


def statistics(s_ref, pos_col, cols, e2, hits, step=64):
    rows, docs = s_ref.shape
    lane = lax.broadcasted_iota(I32, (step, 128), 1)
    ids = lax.broadcasted_iota(I32, (step, docs), 1)

    def block(b, _):
        at = pl.ds(pl.multiple_of(b * step, step), step)
        s = s_ref[at, :]
        top = jnp.max(s, axis=1, keepdims=True)
        hit = pos_col[at, :1] == ids
        own = jnp.sum(jnp.where(hit, s, 0.0), axis=1, keepdims=True)
        hits[at, :] = jnp.where(hit, 1.0, 0.0).astype(BF16)
        e = jnp.exp(s - top)
        total = jnp.sum(e, axis=1, keepdims=True)
        s_ref[at, :] = e
        high, low = split(e)
        e2[at, :] = low
        e2[pl.ds(pl.multiple_of(rows + b * step, step), step), :] = high
        cols[at, :] = jnp.where(
            lane == 0, top, jnp.where(lane == 1, total, jnp.where(lane == 2, own, 0.0))
        )
        return 0

    lax.fori_loop(0, rows // step, block, 0)


def as_column(row, column):
    column[...] = jnp.broadcast_to(row, (128, row.shape[1])).T


def pull(hits, r3, pulled, tile=256):
    width = r3.shape[0] // 3

    def block(t, _):
        base = pl.multiple_of(t * tile, tile)
        acc = dot(hits[...], r3[pl.ds(width + base, tile), :], NT)
        pulled[:, pl.ds(base, tile)] = acc + dot(hits[...], r3[pl.ds(2 * width + base, tile), :], NT)
        return 0

    lax.fori_loop(0, width // tile, block, 0)


def spread_out(e2, r3, spread, tile=256):
    rows = e2.shape[0] // 2
    width = r3.shape[0] // 3

    def block(t, _):
        base = pl.multiple_of(t * tile, tile)
        mid = r3[pl.ds(width + base, tile), :]
        high = r3[pl.ds(2 * width + base, tile), :]
        acc = dot(e2[rows:, :], mid, NT)
        acc = acc + dot(e2[:rows, :], high, NT)
        spread[:, pl.ds(base, tile)] = acc + dot(e2[rows:, :], high, NT)
        return 0

    lax.fori_loop(0, width // tile, block, 0)


def query_gradient(spread, pulled, scale_col, out, step=32):
    def block(b, _):
        at = pl.ds(pl.multiple_of(b * step, step), step)
        out[at, :] = spread[at, :] * scale_col[at, :1] - pulled[at, :]
        return 0

    lax.fori_loop(0, spread.shape[0] // step, block, 0)


def weigh(e_ref, scale_col, pos_col, w3, step=32):
    rows, docs = e_ref.shape
    w3[3 * rows :, :] = jnp.zeros((w3.shape[0] - 3 * rows, docs), BF16)
    ids = lax.broadcasted_iota(I32, (step, docs), 1)

    def block(b, _):
        at = pl.ds(pl.multiple_of(b * step, step), step)
        w = e_ref[at, :] * scale_col[at, :1]
        w = w - jnp.where(pos_col[at, :1] == ids, 1.0, 0.0)
        high, low = split(w)
        w3[at, :] = low
        w3[pl.ds(pl.multiple_of(rows + b * step, step), step), :] = high
        w3[pl.ds(pl.multiple_of(2 * rows + b * step, step), step), :] = high
        return 0

    lax.fori_loop(0, rows // step, block, 0)


def document_gradient(w3, q_t, out, tile=256):
    for t in range(out.shape[1] // tile):
        at = slice(t * tile, t * tile + tile)
        out[:, at] = dot(q_t[...], w3[:, at])


def collect(codes_t, d_ref, out, base, count, group=4):
    subs, docs = codes_t.shape
    sub_width = d_ref.shape[0] // subs
    word = lax.broadcasted_iota(I32, (HIGH_CODES, docs), 0)
    lane = lax.broadcasted_iota(I32, (sub_width, 128), 1)

    def one(b):
        g = b + base
        tables, values = [], []
        for s in range(group):
            m = group * g + s
            code = codes_t[pl.ds(m, 1), :]
            inner = code & (HIGH_CODES - 1)
            outer = jnp.broadcast_to(code >> 6, (sub_width, docs))
            tables.append(jnp.where(word == inner, 1.0, 0.0).astype(BF16))
            d = d_ref[pl.ds(pl.multiple_of(m * sub_width, sub_width), sub_width), :]
            high = d.astype(BF16).astype(F32)
            low = d - high
            masks = [outer == k for k in range(LOW_CODES)]
            rows = [jnp.where(mask, part, 0.0) for part in (high, low) for mask in masks]
            values.append(jnp.concatenate(rows, axis=0).astype(BF16))
        found = dot(jnp.concatenate(values, axis=0), jnp.concatenate(tables, axis=0), NT)
        rows = 2 * LOW_CODES * sub_width
        for s in range(group):
            at = 128 * (s // 2)
            piece = found[rows * s : rows * (s + 1), at : at + 128]
            piece = piece[: rows // 2] + piece[rows // 2 :]
            parts = [piece[sub_width * k : sub_width * (k + 1)] for k in range(LOW_CODES)]
            start = pl.multiple_of((group * g + s) * sub_width, sub_width)
            for k in range(2):
                first, second = parts[2 * k], parts[2 * k + 1]
                if s % 2:
                    first = pltpu.roll(first, 64, 1)
                else:
                    second = pltpu.roll(second, 64, 1)
                out[pl.ds(start, sub_width), 128 * k : 128 * k + 128] = jnp.where(
                    lane < 64, first, second
                )

    for b in range(count):
        one(b)


def transpose_run(part, base, count, out, step=128):
    def block(b, _):
        at = pl.ds(pl.multiple_of(base + b * step, step), step)
        out[:, at] = part[at, :].T
        return 0

    lax.fori_loop(0, count // step, block, 0)


class Place:
    def __init__(self):
        query, corpus = lax.axis_index("query"), lax.axis_index("corpus")
        self.y = lax.rem(query, 4)
        self.x = 2 * lax.div(query, 4) + lax.rem(lax.div(corpus, 2), 2)
        self.z = lax.div(corpus, 4)
        self.core = lax.rem(corpus, 2)

    def at(self, x=None, y=None, z=None, core=None):
        x = self.x if x is None else x
        y = self.y if y is None else y
        z = self.z if z is None else z
        core = self.core if core is None else core
        return (4 * lax.div(x, 2) + y, 4 * z + 2 * lax.rem(x, 2) + core)

    def next_y(self, d):
        return lax.rem(self.y + d, 4)

    def next_x(self, d):
        return lax.rem(self.x + d, 4)

    def next_z(self, d):
        return lax.rem(self.z + d, 8)


class Wire:
    def __init__(self, sent, arrived):
        self.sent, self.arrived, self.copies = sent, arrived, []
        self.settled, self.mark = 0, 0

    def send(self, src, dst, device):
        i = len(self.copies)
        copy = pltpu.make_async_remote_copy(
            src_ref=src,
            dst_ref=dst,
            send_sem=self.sent.at[i],
            recv_sem=self.arrived.at[i],
            device_id=device,
            device_id_type=pl.DeviceIdType.MESH,
        )
        copy.start()
        self.copies.append(copy)
        return copy

    def settle(self):
        for copy in self.copies[self.settled : self.mark]:
            copy.wait_send()
        self.settled, self.mark = self.mark, len(self.copies)

    def finish(self):
        for copy in self.copies[self.settled :]:
            copy.wait_send()


def rows_at(index, size):
    return pl.ds(pl.multiple_of(index * size, size), size)


def merge(stats):
    top = stats[0][0:1]
    for s in stats[1:]:
        top = jnp.maximum(top, s[0:1])
    total = sum(s[1:2] * jnp.exp(s[0:1] - top) for s in stats)
    own = sum(s[2:3] for s in stats)
    pad = jnp.zeros((8 - 3, top.shape[1]), F32)
    return jnp.concatenate([top, total, own, pad], axis=0)


def step(
    q_hbm, codes_hbm, pos_ref, book_hbm,
    grad_q, grad_b, loss_ref,
    q_ref, codes_t, book_ref, book_t, q3, r3, q_t, e_ref, stats_ref, cols,
    pos_col, scale_col, e2, hits, spread, pulled, w3, d_ref,
    near, far, part_q, half_q, sum_q, ring_in, relay, cross,
    words_b, part_b, half_b, sum_b, first_in, first_sum, second_in, second_sum, last_in,
    sent, arrived, loaded,
):
    loads = [
        pltpu.make_async_copy(book_hbm, book_ref, loaded.at[0]),
        pltpu.make_async_copy(codes_hbm, codes_t, loaded.at[1]),
        pltpu.make_async_copy(q_hbm, q_ref, loaded.at[2]),
    ]
    for load in loads:
        load.start()
    me = Place()
    wire = Wire(sent, arrived)
    x_pair = me.x + 1 - 2 * lax.rem(me.x, 2)
    other = 1 - me.core
    partners = [me.at(core=other), me.at(x=x_pair), me.at(x=x_pair, core=other)]
    far_partners = [me.at(z=me.next_z(d)) for d in range(1, 8)]
    y_partners = [me.at(y=me.next_y(d)) for d in range(1, 4)]
    x_partners = [me.at(x=me.next_x(d)) for d in range(1, 4)]
    greeted = [partners[0], partners[2]] + far_partners + y_partners + x_partners
    barrier = pltpu.get_barrier_semaphore()
    for device in greeted:
        pl.semaphore_signal(barrier, inc=1, device_id=device, device_id_type=pl.DeviceIdType.MESH)

    loads[0].wait()
    transpose_book(book_ref, book_t)
    loads[1].wait()
    rebuild(codes_t, book_t, r3)
    loads[2].wait()
    split_queries(q_ref, q3)
    score(q3, r3, e_ref)
    docs = codes_t.shape[1]
    here = pos_ref[...].reshape(1, -1) - lax.axis_index("corpus") * docs
    as_column(here, pos_col)
    statistics(e_ref, pos_col, cols, e2, hits)
    stats_ref[...] = cols[...].T[:8]
    pl.semaphore_wait(barrier, len(greeted))

    mine = 2 * lax.rem(me.x, 2) + me.core
    near[mine] = stats_ref[...]
    copies = [wire.send(stats_ref, near.at[mine], device) for device in partners]
    pull(hits, r3, pulled)
    for copy in copies:
        copy.wait_recv()
    far[me.z] = merge([near[k] for k in range(4)])
    copies = [wire.send(far.at[me.z], far.at[me.z], device) for device in far_partners]
    spread_out(e2, r3, spread)
    transpose_queries(q_ref, q_t)
    for copy in copies:
        copy.wait_recv()
    whole = merge([far[k] for k in range(8)])
    log_total = whole[0:1] + jnp.log(whole[1:2])
    loss_ref[...] = (log_total - whole[2:3]).reshape(-1)
    as_column(jnp.exp(stats_ref[0:1] - log_total), scale_col)

    query_gradient(spread, pulled, scale_col, part_q)
    half = part_q.shape[0] // 2
    chunk = half // 8
    q_core = wire.send(part_q.at[rows_at(other, half)], half_q, partners[0])
    weigh(e_ref, scale_col, pos_col, w3)
    document_gradient(w3, q_t, d_ref)
    q_core.wait_recv()
    sum_q[...] = part_q[rows_at(me.core, half)] + half_q[...]

    def arrive(copies):
        for copy in copies:
            copy.wait_recv()

    words, b_half = part_b.shape[0], part_b.shape[1] // 2
    lines = words // 8
    group_width = 4 * d_ref.shape[0] // codes_t.shape[0]

    def lines_at(k, first, size, second=None):
        start = k * (words // 2) + first * lines
        if second is not None:
            start = start + second * size
        return pl.ds(pl.multiple_of(start, size), size)

    order = (
        ((me.y, me.next_y, y_partners), (me.x, me.next_x, x_partners)),
        ((me.x, me.next_x, x_partners), (me.y, me.next_y, y_partners)),
    )
    passed, taken = [], [0, 0]

    def greet_passed():
        arrive(passed[taken[0] : taken[1]])
        taken[:] = taken[1], len(passed)

    def gather_words(core, part):
        offset, count = part
        base = core * b_half + offset
        collect(codes_t, d_ref, words_b, core * (b_half // group_width) + offset // group_width, count // group_width)
        transpose_run(words_b, base, count, part_b)

    def book_chain(part):
        offset, count = part
        inner = slice(offset, offset + count)
        theirs = pl.ds(pl.multiple_of(other * b_half + offset, 128), count)
        ours = pl.ds(pl.multiple_of(me.core * b_half + offset, 128), count)
        core = wire.send(part_b.at[:, theirs], half_b.at[:, inner], partners[0])
        yield
        core.wait_recv()
        sum_b[:, inner] = part_b[:, ours] + half_b[:, inner]
        firsts = []
        for k in range(2):
            _, following, devices = order[k][0]
            for d in range(1, 4):
                firsts.append(
                    wire.send(
                        sum_b.at[lines_at(k, following(d), lines), inner],
                        first_in.at[k, d - 1, :, inner],
                        devices[d - 1],
                    )
                )
        yield
        arrive(firsts)
        seconds = []
        for k in range(2):
            index, _, _ = order[k][0]
            acc = sum_b[lines_at(k, index, lines), inner]
            for d in range(3):
                acc = acc + first_in[k, d, :, inner]
            first_sum[k, :, inner] = acc
            _, following, devices = order[k][1]
            for d in range(1, 4):
                seconds.append(
                    wire.send(
                        first_sum.at[k, rows_at(following(d), lines // 4), inner],
                        second_in.at[k, d - 1, :, inner],
                        devices[d - 1],
                    )
                )
        yield
        arrive(seconds)
        for k in range(2):
            index, _, _ = order[k][1]
            acc = first_sum[k, rows_at(index, lines // 4), inner]
            for d in range(3):
                acc = acc + second_in[k, d, :, inner]
            last_in[me.z, k, :, inner] = acc
        mine = last_in.at[me.z, :, :, inner]
        lasts = [wire.send(mine, mine, device) for device in far_partners]
        yield
        arrive(lasts)
        acc = last_in[0, :, :, inner]
        for z in range(1, 8):
            acc = acc + last_in[z, :, :, inner]

        def share_b(at, device):
            return wire.send(grad_b.at[at, ours], grad_b.at[at, ours], device)

        seconds = []
        for k in range(2):
            at = lines_at(k, order[k][0][0], lines // 4, order[k][1][0])
            grad_b[at, ours] = acc[k]
            for device in order[k][1][2]:
                seconds.append(share_b(at, device))
        yield
        arrive(seconds)
        firsts = []
        for k in range(2):
            at = lines_at(k, order[k][0][0], lines)
            for device in order[k][0][2]:
                firsts.append(share_b(at, device))
        for k in range(2):
            passed.append(share_b(lines_at(k, order[k][0][0], lines), partners[0]))
        yield
        for d in (1, 3, 2):
            for k in range(2):
                arrive([firsts[3 * k + d - 1]])
                back = order[k][0][1](4 - d)
                passed.append(share_b(lines_at(k, back, lines), partners[0]))
        yield

    def q_rows(z):
        return pl.ds(pl.multiple_of(me.core * half + z * chunk, chunk), chunk)

    def share(at, device):
        return wire.send(grad_q.at[at], grad_q.at[at], device)

    middle = grad_q.shape[1] // 2

    def query_chain():
        terms = [
            wire.send(sum_q.at[rows_at(me.next_z(d), chunk)], ring_in.at[d - 1], far_partners[d - 1])
            for d in (3, 5, 2, 6, 1, 7)
        ]
        sides = ((far_partners[1], slice(0, middle)), (far_partners[5], slice(middle, 2 * middle)))
        legs = [
            wire.send(sum_q.at[rows_at(me.next_z(4), chunk), columns], relay.at[k], device)
            for k, (device, columns) in enumerate(sides)
        ]
        yield
        arrive(legs)
        for k, (device, columns) in enumerate(sides):
            terms.append(wire.send(relay.at[k], ring_in.at[3, :, columns], device))
        yield
        arrive(terms)
        acc = sum_q[rows_at(me.z, chunk)]
        for d in range(7):
            acc = acc + ring_in[d]
        cross[0] = acc
        across = wire.send(cross.at[0], cross.at[1], partners[1])
        yield
        arrive([across])
        grad_q[q_rows(me.z)] = cross[0] + cross[1]
        passed.append(share(q_rows(me.z), partners[0]))
        shares = {d: share(q_rows(me.z), far_partners[d - 1]) for d in (2, 6, 3, 5, 1, 7)}
        yield
        rest = []
        for d, (device, columns) in zip((2, 6), sides):
            at = q_rows(me.next_z(8 - d))
            arrive([shares[d]])
            rest.append(wire.send(grad_q.at[at, columns], grad_q.at[at, columns], device))
            passed.append(share(at, partners[0]))
        for part in ((1, 7), (3, 5, 4)):
            yield
            for d in part:
                arrive(rest if d == 4 else [shares[d]])
                passed.append(share(q_rows(me.next_z(8 - d)), partners[0]))
        yield

    large, small = (0, 2 * b_half // 3), (2 * b_half // 3, b_half // 3)
    queries = query_chain()
    next(queries)
    gather_words(other, large)
    first = book_chain(large)
    next(first)
    gather_words(me.core, large)
    next(first)
    next(queries)
    gather_words(other, small)
    second = book_chain(small)
    next(second)
    gather_words(me.core, small)
    next(second)
    wire.settle()
    next(first)
    next(second)
    wire.settle()
    next(queries)
    next(first)
    next(second)
    wire.settle()
    next(queries)
    next(first)
    next(second)
    wire.settle()
    next(queries)
    next(first)
    next(second)
    wire.settle()
    next(queries)
    greet_passed()
    next(first)
    next(second)
    wire.settle()
    next(queries)
    greet_passed()
    arrive(passed[taken[0] :])
    wire.finish()
    assert len(wire.copies) == COPIES, len(wire.copies)


def hand_over(*refs):
    inside, outside = refs[9], refs[10]
    steps = []
    for k in range(3):
        src, dst, held = refs[k], refs[3 + k], refs[6 + k]
        pieces = 4 if len(src.shape) > 1 else 1
        size = src.shape[0] // pieces
        for n in range(pieces):
            at = pl.ds(n * size, size)
            i = len(steps)
            steps.append(
                (
                    pltpu.make_async_copy(src.at[at], held.at[at], inside.at[i]),
                    pltpu.make_async_copy(held.at[at], dst.at[at], outside.at[i]),
                )
            )
    for load, _ in steps:
        load.start()
    for load, store in steps:
        load.wait()
        store.start()
    for _, store in steps:
        store.wait()


def local(queries, codes, positive, codebook):
    rows, width = queries.shape
    docs, subs = codes.shape
    words = codebook.shape[0]
    chunk = rows // 16
    lines = words // 8
    half = width // 2
    depth = 256 * pl.cdiv(3 * rows, 256)
    vmem = pl.BlockSpec(memory_space=pltpu.VMEM)
    hbm = pl.BlockSpec(memory_space=pltpu.HBM)
    grad_q, grad_b, loss = pl.pallas_call(
        step,
        in_specs=[hbm, hbm, vmem, hbm],
        out_specs=(vmem, vmem, vmem),
        out_shape=(
            jax.ShapeDtypeStruct((rows, width), F32),
            jax.ShapeDtypeStruct((words, width), F32),
            jax.ShapeDtypeStruct((rows,), F32),
        ),
        scratch_shapes=[
            pltpu.VMEM((rows, width), F32),
            pltpu.VMEM((subs, docs), I32),
            pltpu.VMEM((words, width), F32),
            pltpu.VMEM((width, words), F32),
            pltpu.VMEM((rows, 3 * width), BF16),
            pltpu.VMEM((3 * width, docs), BF16),
            pltpu.VMEM((width, depth), BF16),
            pltpu.VMEM((rows, docs), F32),
            pltpu.VMEM((8, rows), F32),
            pltpu.VMEM((rows, 128), F32),
            pltpu.VMEM((rows, 128), I32),
            pltpu.VMEM((rows, 128), F32),
            pltpu.VMEM((2 * rows, docs), BF16),
            pltpu.VMEM((rows, docs), BF16),
            pltpu.VMEM((rows, width), F32),
            pltpu.VMEM((rows, width), F32),
            pltpu.VMEM((depth, docs), BF16),
            pltpu.VMEM((width, docs), F32),
            pltpu.VMEM((4, 8, rows), F32),
            pltpu.VMEM((8, 8, rows), F32),
            pltpu.VMEM((rows, width), F32),
            pltpu.VMEM((rows // 2, width), F32),
            pltpu.VMEM((rows // 2, width), F32),
            pltpu.VMEM((7, chunk, width), F32),
            pltpu.VMEM((2, chunk, half), F32),
            pltpu.VMEM((2, chunk, width), F32),
            pltpu.VMEM((width, words), F32),
            pltpu.VMEM((words, width), F32),
            pltpu.VMEM((words, half), F32),
            pltpu.VMEM((words, half), F32),
            pltpu.VMEM((2, 3, lines, half), F32),
            pltpu.VMEM((2, lines, half), F32),
            pltpu.VMEM((2, 3, lines // 4, half), F32),
            pltpu.VMEM((2, lines // 4, half), F32),
            pltpu.VMEM((8, 2, lines // 4, half), F32),
            pltpu.SemaphoreType.DMA((COPIES,)),
            pltpu.SemaphoreType.DMA((COPIES,)),
            pltpu.SemaphoreType.DMA((3,)),
        ],
        compiler_params=pltpu.CompilerParams(
            collective_id=0, has_side_effects=True, vmem_limit_bytes=56 << 20
        ),
        name="step",
    )(queries, codes.T, positive, codebook)
    return pl.pallas_call(
        hand_over,
        in_specs=[hbm] * 3,
        out_specs=[hbm] * 3,
        out_shape=[jax.ShapeDtypeStruct(x.shape, F32) for x in (grad_q, grad_b, loss)],
        scratch_shapes=[
            *(pltpu.VMEM(x.shape, F32) for x in (grad_q, grad_b, loss)),
            pltpu.SemaphoreType.DMA((9,)),
            pltpu.SemaphoreType.DMA((9,)),
        ],
        name="hand_over",
    )(grad_q, grad_b, loss)


def solution(mesh):
    return jax.shard_map(
        local,
        mesh=mesh,
        in_specs=(P("query", None), P("corpus", None), P("query"), P()),
        out_specs=(P("query", None), P(), P("query")),
        check_vma=False,
    )
```
